256 devices in a mesh: grid: 16 (over z_hi, y), space: 16 (over z_lo, x, core).
Axes of the slice: x: 4, y: 4, z: 8 (z_hi: 4, z_lo: 2; z = z_hi * 2 + z_lo), core: 2. Of those that a mesh axis runs over, the one named last changes fastest.
Arguments:
- density: float32 [16, 512, 64, 128], P('grid', 'space'), may hold values from -6 to 6
- kappa: float32 [16, 512, 64, 128], P('grid', 'space'), may hold values from 0.02 to 0.16
- levels: int32 [16, 3], P('grid'), may hold values from 3 to 6, as said below
- coefs: int32 [16], P('grid'), may hold values from -2 to 1, as said below
Outputs:
- combined: float32 [16, 512, 64, 128], P('grid', 'space')
The draws below stay inside these ranges and needn't reach their ends.
Inputs may be any that keep to these rules, and one draw needn't show every extreme that they name: `levels`: each level vector is (3, 3, 3) plus nonnegative integers summing to 1, 2 or 3, no two grids alike; a level at or above log2 of an axis's cells keeps that whole axis. coefs[g] is +1 where the grid's levels sum to 12 or 10 and -2 where they sum to 11.
All inputs are finite; a program needn't handle non-finite values.
Results may differ from the reference program's by a relative error of at most 0.0003.
Values sent between devices are 32-bit elements; how exact they have to be, the bound alone decides.
No kernel may reach another device: no remote copies, remote signals or barrier semaphores. Data moves between devices by JAX's collectives and lax.ppermute only.
A program may use at most 64 MiB of HBM per device.

```python
import math
import jax
import jax.numpy as jnp
import numpy as np
from jax import lax

X = 512
Y = 64
Z = 128
ITERS = 8
GRIDS = 16


def ordered_offsets(key):
    extremes = [(3, 0, 0), (0, 3, 0), (0, 0, 3)]
    middle = []
    others = []
    for first in range(4):
        for second in range(4):
            for third in range(4):
                total_k = first + second + third
                vector = (first, second, third)
                if vector in extremes:
                    continue
                if total_k == 2:
                    middle.append(vector)
                elif total_k == 1 or total_k == 3:
                    others.append(vector)
    middle_table = jnp.asarray(np.array(middle, dtype=np.int32))
    other_table = jnp.asarray(np.array(others, dtype=np.int32))
    extreme_table = jnp.asarray(np.array(extremes, dtype=np.int32))
    key_middle = jax.random.fold_in(key, 11)
    key_rest = jax.random.fold_in(key, 12)
    middle_order = jax.random.permutation(key_middle, middle_table.shape[0])
    shuffled_middle = jnp.take(middle_table, middle_order, axis=0)
    rest = jnp.concatenate([shuffled_middle[1:], other_table], axis=0)
    rest_order = jax.random.permutation(key_rest, rest.shape[0])
    rest = jnp.take(rest, rest_order, axis=0)
    return jnp.concatenate([extreme_table, shuffled_middle[0:1], rest], axis=0)


def draw_levels(key, part):
    offsets = ordered_offsets(key)
    return (offsets[:GRIDS] + 3).astype(jnp.int32)


def draw_coefs(key, part):
    offsets = ordered_offsets(key)[:GRIDS]
    summed = jnp.sum(offsets, axis=1)
    return jnp.where(summed == 2, -2, 1).astype(jnp.int32)


def block_levels(stream_key, shape, pieces, least, high):
    factor_of, own = 1.0, jax.random.fold_in(stream_key, 6)
    for position, parts in pieces:
        heights = jnp.exp(jax.random.uniform(jax.random.fold_in(own, position), (parts,), jnp.float32, least / len(pieces), high / len(pieces)))
        factor_of = factor_of * jnp.repeat(heights, shape[position] // parts).reshape([-1 if axis == position else 1 for axis in range(len(shape))])
    return factor_of


def bell_draw(key, extent, spread, bound, cuts=(), kind=jnp.bfloat16):
    values = spread * jax.random.normal(key, extent, jnp.float32)
    if cuts:
        values = values * block_levels(key, extent, cuts, -0.22, 0.18)
    return jnp.clip(values, -bound, bound).astype(kind)


def setup_inputs(seed: int = 0) -> dict:
    splits = jax.random.split(jax.random.key(seed), 5)
    return {
        "density": bell_draw(splits[0], (GRIDS, X, Y, Z), 1.0, 6.0, ((0, 16), (1, 16)), jnp.float32),
        "kappa": jnp.clip(jnp.exp(math.log(0.16) - 2.0794415 * jax.random.uniform(splits[1], (GRIDS, X, Y, Z), jnp.float32) ** block_levels(splits[1], (GRIDS, X, Y, Z), ((0, 16), (1, 16)), -0.2, 0.2)), 0.02, 0.16),
        "levels": draw_levels(jax.random.fold_in(splits[4], 71), 0),
        "coefs": draw_coefs(jax.random.fold_in(splits[4], 71), 0),
    }


def build_tables(count):
    depth = count.bit_length() - 1
    hier = np.eye(count)
    dehier = np.eye(count)
    level_table = np.zeros(count, dtype=np.int64)
    for index in range(1, count):
        trailing = 0
        while (index >> trailing) & 1 == 0:
            trailing += 1
        spacing = 1 << trailing
        level_table[index] = depth - trailing
        hier[index, (index - spacing) % count] -= 0.5
        hier[index, (index + spacing) % count] -= 0.5
    for trailing in range(depth - 1, -1, -1):
        spacing = 1 << trailing
        for index in range(spacing, count, 2 * spacing):
            dehier[index] = dehier[index] + 0.5 * (dehier[(index - spacing) % count] + dehier[(index + spacing) % count])
    return jnp.asarray(hier, jnp.float32), jnp.asarray(dehier, jnp.float32), jnp.asarray(level_table.astype(np.int32))


def transform_all(field, mat_x, mat_y, mat_z):
    hi = lax.Precision.HIGHEST
    field = jnp.einsum("wx,gxyz->gwyz", mat_x, field, precision=hi)
    field = jnp.einsum("vy,gxyz->gxvz", mat_y, field, precision=hi)
    return jnp.einsum("gxyz,wz->gxyw", field, mat_z, precision=hi)


def reference(density, kappa, levels, coefs):
    hier_x, dehier_x, level_x = build_tables(X)
    hier_y, dehier_y, level_y = build_tables(Y)
    hier_z, dehier_z, level_z = build_tables(Z)
    faces = []
    for axis in (1, 2, 3):
        faces.append(0.5 * (kappa + jnp.roll(kappa, -1, axis)))
        faces.append(0.5 * (kappa + jnp.roll(kappa, 1, axis)))
    field = density
    for sweep_index in range(ITERS):
        flux = faces[0] * (jnp.roll(field, -1, 1) - field) + faces[1] * (jnp.roll(field, 1, 1) - field)
        flux = flux + faces[2] * (jnp.roll(field, -1, 2) - field) + faces[3] * (jnp.roll(field, 1, 2) - field)
        flux = flux + faces[4] * (jnp.roll(field, -1, 3) - field) + faces[5] * (jnp.roll(field, 1, 3) - field)
        field = field + flux
    surplus = transform_all(field, hier_x, hier_y, hier_z)
    mask_x = (level_x[None, :] <= levels[:, 0:1]).astype(jnp.float32)
    mask_y = (level_y[None, :] <= levels[:, 1:2]).astype(jnp.float32)
    mask_z = (level_z[None, :] <= levels[:, 2:3]).astype(jnp.float32)
    mask = mask_x[:, :, None, None] * mask_y[:, None, :, None] * mask_z[:, None, None, :]
    weight = coefs.astype(jnp.float32)[:, None, None, None]
    total = jnp.sum(weight * mask * surplus, axis=0)
    return transform_all(mask * total[None], dehier_x, dehier_y, dehier_z)
```

```python
import functools

import jax
import jax.numpy as jnp
import numpy as np
from jax import lax
from jax.experimental import pallas as pl
from jax.experimental.pallas import tpu as pltpu
from jax.sharding import PartitionSpec as P

ITERS = 8
LOW = 3
SPAN = 3
ROWS = 32
GAP = 8
NODES = ROWS // GAP + 1
LEFT = ITERS
RIGHT = ITERS + 1
TALL = LEFT + ROWS + RIGHT
NY = 64
NZ = 128
TOP = 1 << (LOW + SPAN)


def level_order(count):
    step = count >> (LOW + SPAN)
    order = list(range(0, count, count >> LOW))
    for level in range(LOW + 1, LOW + SPAN + 1):
        gap = count >> level
        order += list(range(gap, count, 2 * gap))
    assert len(order) == TOP and all(i % step == 0 for i in order)
    return order


def tables(count):
    order = level_order(count)
    hier = np.eye(count)
    hats = np.eye(count)
    for index in range(1, count):
        gap = index & -index
        hier[index, (index - gap) % count] -= 0.5
        hier[index, (index + gap) % count] -= 0.5
    gap = count // 2
    while gap:
        for index in range(gap, count, 2 * gap):
            hats[index] += 0.5 * (hats[(index - gap) % count] + hats[(index + gap) % count])
        gap //= 2
    return hier[order], hats[:, order]


@functools.lru_cache(None)
def constants():
    hy, dy = tables(NY)
    hz, dz = tables(NZ)
    spread = [v + 8 * s for v in range(8) for s in range(8)]
    hy = hy[:, spread]
    hz_t = np.zeros((NZ, 128))
    hz_t[:, :TOP] = hz.T
    dz_t = np.zeros((128, NZ))
    dz_t[:TOP] = dz.T
    hy3 = np.concatenate([hy] * 3, axis=1)
    dy3 = np.concatenate([dy] * 3, axis=1)
    return tuple(np.asarray(m, np.float32) for m in (hy3, hz_t, dy3, dz_t))


def staircase():
    widths = {0: SPAN, 1: SPAN - 1, 2: SPAN - 2, 3: SPAN - 3, 4: SPAN - 3}
    blocks = []
    place = 0
    for plane, left in widths.items():
        for extra in range(left + 1):
            groups = range(1 << (extra - 1), 1 << extra) if extra else range(1)
            for group in groups:
                width = 1 << (LOW + left - extra)
                blocks.append((plane, group, width, place // 128, place % 128))
                assert place % 128 + width <= 128
                place += width
    return blocks, -(-place // 128)


BLOCKS, TILES = staircase()
SHARED = 1 + max(b[3] for b in BLOCKS if b[0] < 2)


def split3(x):
    hi = x.astype(jnp.bfloat16)
    rest = x - hi.astype(jnp.float32)
    mid = rest.astype(jnp.bfloat16)
    lo = (rest - mid.astype(jnp.float32)).astype(jnp.bfloat16)
    return hi, mid, lo


def rows_dot(weights3, plane):
    stacked = jnp.concatenate(split3(plane), axis=0)
    return jnp.dot(weights3, stacked, preferred_element_type=jnp.float32)


def lanes_dot(planes, weights):
    total = None
    for piece in split3(planes):
        part = jnp.dot(piece, weights, preferred_element_type=jnp.float32)
        total = part if total is None else total + part
    return total


def next_y(row):
    return jnp.concatenate([row[1:], pltpu.roll(row[0:1], 7, 1)], axis=0)


def prev_y(row):
    return jnp.concatenate([pltpu.roll(row[7:8], 1, 1), row[:7]], axis=0)


def next_z(row):
    return pltpu.roll(row, NZ - 1, 2)


def prev_z(row):
    return pltpu.roll(row, 1, 2)


def fetch(ref, index):
    return jnp.stack([ref[index, pl.ds(v, 8, 8), :] for v in range(8)], axis=0)


def advance(f_ref, cx_ref, cy_ref, cz_ref, start, count):
    def one(i, here, flux):
        after = f_ref[i + 1]
        flux_x = cx_ref[i] * (after - here)
        flux_y = cy_ref[i] * (next_y(here) - here)
        flux_z = cz_ref[i] * (next_z(here) - here)
        f_ref[i] = (here + (flux_x - flux)) + ((flux_y - prev_y(flux_y)) + (flux_z - prev_z(flux_z)))
        return after, flux_x

    before = f_ref[start - 1]
    here = f_ref[start]
    flux = cx_ref[start - 1] * (here - before)
    unroll = 4

    def body(t, carry):
        here, flux = carry
        for k in range(unroll):
            here, flux = one(start + t * unroll + k, here, flux)
        return here, flux

    whole = count // unroll
    if whole:
        here, flux = lax.fori_loop(0, whole, body, (here, flux))
    for k in range(whole * unroll, count):
        here, flux = one(start + k, here, flux)


def diffuse_kernel(lev, coef, odd, den, kap, left, right, hy3, hz, out, f_ref, cx_ref, cy_ref, cz_ref):
    def load_rows(f_src, f_base, k_src, k_base, count, base, carry):
        def body(t, before):
            k = fetch(k_src, k_base + t)
            f_ref[base + t] = fetch(f_src, f_base + t)
            cx_ref[jnp.maximum(base + t - 1, 0)] = 0.5 * (before + k)
            cy_ref[base + t] = 0.5 * (k + next_y(k))
            cz_ref[base + t] = 0.5 * (k + next_z(k))
            return k
        return lax.fori_loop(0, count, body, carry)

    k = jnp.zeros((8, 8, 128), jnp.float32)
    k = load_rows(left, 0, left, LEFT, LEFT, 0, k)
    k = load_rows(den, 0, kap, 0, ROWS, LEFT, k)
    k = load_rows(right, 0, right, RIGHT, RIGHT, LEFT + ROWS, k)

    for step in range(1, ITERS + 1):
        reach = ITERS - step
        if 2 * reach + 1 >= GAP:
            advance(f_ref, cx_ref, cy_ref, cz_ref, LEFT - reach, ROWS + 2 * reach + 1)
        else:
            def node(n, _, reach=reach):
                advance(f_ref, cx_ref, cy_ref, cz_ref, LEFT + n * GAP - reach, 2 * reach + 1)
                return 0
            lax.fori_loop(0, NODES, node, 0)

    planes = []
    for n in range(NODES):
        plane = f_ref[LEFT + n * GAP].reshape(NY, NZ)
        planes.append(rows_dot(hy3[...], plane))
    nodal = lanes_dot(jnp.concatenate(planes, axis=0), hz[...]).reshape(NODES, 8, 8, 128)

    level_x, level_y, level_z = lev[0, 0], lev[0, 1], lev[0, 2]
    weight = coef[0].astype(jnp.float32)
    swapped = odd[0] == 1
    lane = lax.broadcasted_iota(jnp.int32, (8, 128), 1)
    groups_y = lax.shift_left(1, level_y - LOW)
    width_z = lax.shift_left(1, level_z)

    def planes_of(group):
        u = [nodal[n, group] for n in range(NODES)]
        outer = jnp.where(swapped, u[4], u[0])
        inner = jnp.where(swapped, u[0], u[4])
        return (
            outer,
            0.5 * (inner - outer),
            u[2] - 0.5 * (u[0] + u[4]),
            u[1] - 0.5 * (u[0] + u[2]),
            u[3] - 0.5 * (u[2] + u[4]),
        )

    need = (LOW, LOW + 1, LOW + 2, LOW + 3, LOW + 3)
    cache = {}
    tiles = [jnp.zeros((8, 128), jnp.float32)] * TILES
    for plane, group, width, tile, first in BLOCKS:
        if group not in cache:
            cache[group] = planes_of(group)
        keep = (lane < jnp.minimum(width_z, width)) & (group < groups_y) & (level_x >= need[plane])
        value = jnp.where(keep, weight * cache[group][plane], 0.0)
        tiles[tile] = tiles[tile] + (pltpu.roll(value, first, 1) if first else value)
    for member in range(out.shape[0]):
        for tile in range(TILES):
            out[member, 8 * tile : 8 * tile + 8] = tiles[tile]


def spread_kernel(lev, odd, mine, other, dy3, dz, out):
    level_x, level_y, level_z = lev[0, 0], lev[0, 1], lev[0, 2]
    swapped = odd[0] == 1
    lane = lax.broadcasted_iota(jnp.int32, (8, 128), 1)
    groups_y = lax.shift_left(1, level_y - LOW)
    width_z = lax.shift_left(1, level_z)
    need = (LOW, LOW + 1, LOW + 2, LOW + 3, LOW + 3)
    own = [mine[8 * t : 8 * t + 8] for t in range(TILES)]
    theirs = [other[8 * t : 8 * t + 8] for t in range(SHARED)]
    zero = jnp.zeros((8, 128), jnp.float32)
    planes = [[zero] * 8 for _ in range(5)]
    outer_other = [zero] * 8
    for plane, group, width, tile, first in BLOCKS:
        keep = (lane < jnp.minimum(width_z, width)) & (group < groups_y) & (level_x >= need[plane])

        def pick(source):
            value = pltpu.roll(source, 128 - first, 1) if first else source
            return jnp.where(keep, value, 0.0)

        if plane == 0:
            planes[0][group] = pick(own[tile])
            outer_other[group] = pick(theirs[tile])
        elif plane == 1:
            planes[1][group] = pick(own[tile] + theirs[tile])
        else:
            planes[plane][group] = pick(own[tile])
    wide = []
    outer = jnp.concatenate(planes[0], axis=0)
    middle = 0.5 * (outer + jnp.concatenate(outer_other, axis=0)) + jnp.concatenate(planes[1], axis=0)
    n0 = jnp.where(swapped, middle, outer)
    n4 = jnp.where(swapped, outer, middle)
    n2 = 0.5 * (n0 + n4) + jnp.concatenate(planes[2], axis=0)
    n1 = 0.5 * (n0 + n2) + jnp.concatenate(planes[3], axis=0)
    n3 = 0.5 * (n2 + n4) + jnp.concatenate(planes[4], axis=0)
    for n in (n0, n1, n2, n3, n4):
        wide.append(rows_dot(dy3[...], n))
    full = lanes_dot(jnp.concatenate(wide, axis=0), dz[...]).reshape(NODES, NY, NZ)
    for q in range(NODES - 1):
        slope = (full[q + 1] - full[q]) * (1.0 / GAP)
        for k in range(GAP):
            out[q * GAP + k] = full[q] + float(k) * slope


VMEM = pl.BlockSpec(memory_space=pltpu.VMEM)
SMEM = pl.BlockSpec(memory_space=pltpu.SMEM)


def diffuse(members, levels, coefs, odd, den, kap, left, right, interpret=False):
    hy3, hz, _, _ = constants()
    work = pltpu.VMEM((TALL, 8, 8, 128), jnp.float32)
    return pl.pallas_call(
        diffuse_kernel,
        out_shape=jax.ShapeDtypeStruct((members, 8 * TILES, 128), jnp.float32),
        in_specs=[SMEM] * 3 + [VMEM] * 6,
        out_specs=VMEM,
        scratch_shapes=[work] * 4,
        interpret=interpret,
        name="diffuse",
    )(levels, coefs, odd, den, kap, left, right, jnp.asarray(hy3, jnp.bfloat16), jnp.asarray(hz, jnp.bfloat16))


def spread(levels, odd, mine, other, interpret=False):
    _, _, dy3, dz = constants()
    return pl.pallas_call(
        spread_kernel,
        out_shape=jax.ShapeDtypeStruct((ROWS, NY, NZ), jnp.float32),
        in_specs=[SMEM] * 2 + [VMEM] * 4,
        out_specs=VMEM,
        interpret=interpret,
        name="spread",
    )(levels, odd, mine, other, jnp.asarray(dy3, jnp.bfloat16), jnp.asarray(dz, jnp.bfloat16))


def local(density, kappa, levels, coefs):
    den, kap = density[0], kappa[0]
    space, grid = lax.axis_size("space"), lax.axis_size("grid")
    assert den.shape == (ROWS, NY, NZ) and space * ROWS == 512
    up = [(i, (i + 1) % space) for i in range(space)]
    down = [(j, i) for i, j in up]
    pair = [(i, i ^ 1) for i in range(space)]
    left = lax.ppermute(jnp.concatenate([den[ROWS - LEFT :], kap[ROWS - LEFT :]], axis=0), "space", up)
    right = lax.ppermute(jnp.concatenate([den[:RIGHT], kap[:RIGHT]], axis=0), "space", down)
    odd = (lax.axis_index("space") % 2).astype(jnp.int32)[None]
    sent = diffuse(grid, levels, coefs, odd, den, kap, left, right)
    got = lax.all_to_all(sent, "grid", split_axis=0, concat_axis=0, tiled=True)
    total = jnp.sum(got, axis=0)
    other = lax.ppermute(total[: 8 * SHARED], "space", pair)
    return spread(levels, odd, total, other)[None]


def solution(mesh):
    in_specs = (
        P("grid", "space", None, None),
        P("grid", "space", None, None),
        P("grid", None),
        P("grid"),
    )
    out_specs = P("grid", "space", None, None)
    return jax.shard_map(local, mesh=mesh, in_specs=in_specs, out_specs=out_specs, check_vma=False)
```

```python
import functools

import jax
import jax.numpy as jnp
import numpy as np
from jax import lax
from jax.experimental import pallas as pl
from jax.experimental.pallas import tpu as pltpu
from jax.sharding import PartitionSpec as P

ITERS = 8
LOW = 3
SPAN = 3
ROWS = 32
GAP = 8
NODES = ROWS // GAP + 1
LEFT = ITERS
RIGHT = ITERS + 1
TALL = LEFT + ROWS + RIGHT
LOAD_UNROLL = 4
ROOM = 24 * 1024 * 1024
NY = 64
NZ = 128
TOP = 1 << (LOW + SPAN)


def level_order(count):
    step = count >> (LOW + SPAN)
    order = list(range(0, count, count >> LOW))
    for level in range(LOW + 1, LOW + SPAN + 1):
        gap = count >> level
        order += list(range(gap, count, 2 * gap))
    assert len(order) == TOP and all(i % step == 0 for i in order)
    return order


def tables(count):
    order = level_order(count)
    hier = np.eye(count)
    hats = np.eye(count)
    for index in range(1, count):
        gap = index & -index
        hier[index, (index - gap) % count] -= 0.5
        hier[index, (index + gap) % count] -= 0.5
    gap = count // 2
    while gap:
        for index in range(gap, count, 2 * gap):
            hats[index] += 0.5 * (hats[(index - gap) % count] + hats[(index + gap) % count])
        gap //= 2
    return hier[order], hats[:, order]


@functools.lru_cache(None)
def constants():
    hy, dy = tables(NY)
    hz, dz = tables(NZ)
    spread = [v + 8 * s for v in range(8) for s in range(8)]
    hy = hy[:, spread]
    hz_t = np.zeros((NZ, 128))
    hz_t[:, :TOP] = hz.T
    dz_t = np.zeros((128, NZ))
    dz_t[:TOP] = dz.T
    hy3 = np.concatenate([hy] * 3, axis=1)
    dy3 = np.concatenate([dy] * 3, axis=1)
    return tuple(np.asarray(m, np.float32) for m in (hy3, hz_t, dy3, dz_t))


def staircase():
    widths = {0: SPAN, 1: SPAN - 1, 2: SPAN - 2, 3: SPAN - 3, 4: SPAN - 3}
    blocks = []
    place = 0
    for plane, left in widths.items():
        for extra in range(left + 1):
            groups = range(1 << (extra - 1), 1 << extra) if extra else range(1)
            for group in groups:
                width = 1 << (LOW + left - extra)
                blocks.append((plane, group, width, place // 128, place % 128))
                assert place % 128 + width <= 128
                place += width
    return blocks, -(-place // 128)


BLOCKS, TILES = staircase()
SHARED = 1 + max(b[3] for b in BLOCKS if b[0] < 2)


def split3(x):
    hi = x.astype(jnp.bfloat16)
    rest = x - hi.astype(jnp.float32)
    mid = rest.astype(jnp.bfloat16)
    lo = (rest - mid.astype(jnp.float32)).astype(jnp.bfloat16)
    return hi, mid, lo


def rows_dot(weights3, plane):
    stacked = jnp.concatenate(split3(plane), axis=0)
    return jnp.dot(weights3, stacked, preferred_element_type=jnp.float32)


def lanes_dot(planes, weights):
    total = None
    for piece in split3(planes):
        part = jnp.dot(piece, weights, preferred_element_type=jnp.float32)
        total = part if total is None else total + part
    return total


def next_y(row):
    return jnp.concatenate([row[1:], pltpu.roll(row[0:1], 7, 1)], axis=0)


def prev_y(row):
    return jnp.concatenate([pltpu.roll(row[7:8], 1, 1), row[:7]], axis=0)


def next_z(row):
    return pltpu.roll(row, NZ - 1, 2)


def prev_z(row):
    return pltpu.roll(row, 1, 2)


def fetch(ref, index):
    row = ref.at[index]
    return jnp.stack([row[pl.ds(v, 8, 8), :] for v in range(8)], axis=0)


def step_rows(rows, take, put, coef, keep=None):
    before, here = take(rows[0] - 1), take(rows[0])
    flux = coef(0, rows[0] - 1) * (here - before)
    for i in rows:
        after = take(i + 1)
        flux_x = coef(0, i) * (after - here)
        flux_y = coef(1, i) * (next_y(here) - here)
        flux_z = coef(2, i) * (next_z(here) - here)
        if keep is not None:
            keep(i, here)
        put(i, (here + (flux_x - flux)) + ((flux_y - prev_y(flux_y)) + (flux_z - prev_z(flux_z))))
        here, flux = after, flux_x


def inner_rows(step):
    reach = ITERS - step
    if 2 * reach + 1 >= GAP:
        return [range(step, ROWS - step)]
    spans = [range(n - reach, min(n + reach + 1, ROWS - step)) for n in range(GAP, ROWS, GAP)]
    return [r for r in spans if len(r)]


def inner_kernel(den, kap, hy3, hz, f_ref, c_ref, old_l, old_r, ends, nodal):
    def load(t, _):
        k = fetch(kap, t)
        after = fetch(kap, jnp.minimum(t + 1, ROWS - 1))
        f_ref[t] = fetch(den, t)
        c_ref[0, t] = 0.5 * (k + after)
        c_ref[1, t] = 0.5 * (k + next_y(k))
        c_ref[2, t] = 0.5 * (k + next_z(k))
        return 0

    lax.fori_loop(0, ROWS, load, 0, unroll=LOAD_UNROLL)
    ends[0] = fetch(kap, 0)
    ends[1] = fetch(kap, ROWS - 1)

    for step in range(1, ITERS + 1):
        for rows in inner_rows(step):
            def keep(i, value, step=step):
                if i == step and step <= 4:
                    old_l[step - 1] = value
                if i == ROWS - 1 - step:
                    old_r[step - 1] = value

            def put(i, value):
                f_ref[i] = value

            step_rows(rows, lambda i: f_ref[i], put, lambda a, i: c_ref[a, i], keep)
    old_r[ITERS - 1] = f_ref[ROWS - 1 - ITERS]
    hierarchize([f_ref[GAP], f_ref[2 * GAP]], hy3, hz, nodal)


def hierarchize(rows, hy3, hz, out):
    planes = [rows_dot(hy3[...], row.reshape(NY, NZ)) for row in rows]
    out[...] = lanes_dot(jnp.concatenate(planes, axis=0), hz[...]).reshape(out.shape)


def edge_kernel(lev, coef, odd, f_in, c_in, old_l, old_r, ends, nodal_in, left, right, hy3, hz, out, f_new, c_new, nodal):
    fresh = set()

    def take(i):
        return f_new[i + LEFT] if i in fresh or not 0 <= i < ROWS else f_in[i]

    def put(i, value):
        fresh.add(i)
        f_new[i + LEFT] = value

    def coef_at(a, i):
        return c_in[a, i] if 0 <= i < ROWS - 1 or (a and i == ROWS - 1) else c_new[a, i + LEFT]

    def prepare(source, first, count, edge_row, edge_k):
        before = None
        for t in range(count):
            i = first + t
            k = fetch(source, count + t)
            f_new[i + LEFT] = fetch(source, t)
            c_new[1, i + LEFT] = 0.5 * (k + next_y(k))
            c_new[2, i + LEFT] = 0.5 * (k + next_z(k))
            if before is not None:
                c_new[0, i - 1 + LEFT] = 0.5 * (before + k)
            if i == edge_row + 1:
                c_new[0, edge_row + LEFT] = 0.5 * (edge_k + k)
            if i == edge_row:
                c_new[0, edge_row + LEFT] = 0.5 * (edge_k + k)
            before = k

    prepare(left, -LEFT, LEFT, -1, ends[0])
    prepare(right, ROWS, RIGHT, ROWS - 1, ends[1])

    for step in range(1, ITERS + 1):
        reach = ITERS - step
        if step <= 4:
            lefts, rights = [range(-reach, step)], [range(ROWS - step, ROWS + reach + 1)]
        else:
            lefts = [range(-reach, reach + 1)]
            rights = [range(ROWS - step, ROWS - step + 1), range(ROWS - reach, ROWS + reach + 1)]

        def take_l(i, step=step):
            return old_l[step - 1] if i == step and step <= 4 else take(i)

        def take_r(i, step=step):
            return old_r[step - 1] if i == ROWS - 1 - step else take(i)

        for rows in lefts:
            step_rows(rows, take_l, lambda i, v: put(i, v), coef_at)
        for k, rows in enumerate(rights):
            if k:
                step_rows(rows, take, lambda i, v: put(i, v), coef_at)
            else:
                step_rows(rows, take_r, lambda i, v: put(i, v), coef_at)

    hierarchize([take(0), take(3 * GAP), take(4 * GAP)], hy3, hz, nodal)
    finish(lev, coef, odd, [nodal.at[0], nodal_in.at[0], nodal_in.at[1], nodal.at[1], nodal.at[2]], out)


def finish(lev, coef, odd, nodal, out):
    level_x, level_y, level_z = lev[0, 0], lev[0, 1], lev[0, 2]
    weight = coef[0].astype(jnp.float32)
    swapped = odd[0] == 1
    lane = lax.broadcasted_iota(jnp.int32, (8, 128), 1)
    groups_y = lax.shift_left(1, level_y - LOW)
    width_z = lax.shift_left(1, level_z)

    def planes_of(group):
        u = [nodal[n][group] for n in range(NODES)]
        outer = jnp.where(swapped, u[4], u[0])
        inner = jnp.where(swapped, u[0], u[4])
        return (
            outer,
            0.5 * (inner - outer),
            u[2] - 0.5 * (u[0] + u[4]),
            u[1] - 0.5 * (u[0] + u[2]),
            u[3] - 0.5 * (u[2] + u[4]),
        )

    need = (LOW, LOW + 1, LOW + 2, LOW + 3, LOW + 3)
    cache = {}
    tiles = [jnp.zeros((8, 128), jnp.float32)] * TILES
    for plane, group, width, tile, first in BLOCKS:
        if group not in cache:
            cache[group] = planes_of(group)
        keep = (lane < jnp.minimum(width_z, width)) & (group < groups_y) & (level_x >= need[plane])
        value = jnp.where(keep, weight * cache[group][plane], 0.0)
        tiles[tile] = tiles[tile] + (pltpu.roll(value, first, 1) if first else value)
    for member in range(out.shape[0]):
        for tile in range(TILES):
            out[member, 8 * tile : 8 * tile + 8] = tiles[tile]


def spread_kernel(lev, odd, mine, other, dy3, dz, out):
    level_x, level_y, level_z = lev[0, 0], lev[0, 1], lev[0, 2]
    swapped = odd[0] == 1
    lane = lax.broadcasted_iota(jnp.int32, (8, 128), 1)
    groups_y = lax.shift_left(1, level_y - LOW)
    width_z = lax.shift_left(1, level_z)
    need = (LOW, LOW + 1, LOW + 2, LOW + 3, LOW + 3)
    own = [mine[8 * t : 8 * t + 8] for t in range(TILES)]
    theirs = [other[8 * t : 8 * t + 8] for t in range(SHARED)]
    zero = jnp.zeros((8, 128), jnp.float32)
    planes = [[zero] * 8 for _ in range(5)]
    outer_other = [zero] * 8
    for plane, group, width, tile, first in BLOCKS:
        keep = (lane < jnp.minimum(width_z, width)) & (group < groups_y) & (level_x >= need[plane])

        def pick(source):
            value = pltpu.roll(source, 128 - first, 1) if first else source
            return jnp.where(keep, value, 0.0)

        if plane == 0:
            planes[0][group] = pick(own[tile])
            outer_other[group] = pick(theirs[tile])
        elif plane == 1:
            planes[1][group] = pick(own[tile] + theirs[tile])
        else:
            planes[plane][group] = pick(own[tile])
    wide = []
    outer = jnp.concatenate(planes[0], axis=0)
    middle = 0.5 * (outer + jnp.concatenate(outer_other, axis=0)) + jnp.concatenate(planes[1], axis=0)
    n0 = jnp.where(swapped, middle, outer)
    n4 = jnp.where(swapped, outer, middle)
    n2 = 0.5 * (n0 + n4) + jnp.concatenate(planes[2], axis=0)
    n1 = 0.5 * (n0 + n2) + jnp.concatenate(planes[3], axis=0)
    n3 = 0.5 * (n2 + n4) + jnp.concatenate(planes[4], axis=0)
    for n in (n0, n1, n2, n3, n4):
        wide.append(rows_dot(dy3[...], n))
    full = lanes_dot(jnp.concatenate(wide, axis=0), dz[...]).reshape(NODES, NY, NZ)
    for q in range(NODES - 1):
        slope = (full[q + 1] - full[q]) * (1.0 / GAP)
        for k in range(GAP):
            out[q * GAP + k] = full[q] + float(k) * slope


VMEM = pl.BlockSpec(memory_space=pltpu.VMEM)
SMEM = pl.BlockSpec(memory_space=pltpu.SMEM)
FAR = pl.BlockSpec(memory_space=pltpu.HBM)


def send_kernel(den, kap, up, down, sem):
    copies = [
        pltpu.make_async_copy(den.at[pl.ds(ROWS - LEFT, LEFT)], up.at[pl.ds(0, LEFT)], sem.at[0]),
        pltpu.make_async_copy(kap.at[pl.ds(ROWS - LEFT, LEFT)], up.at[pl.ds(LEFT, LEFT)], sem.at[1]),
        pltpu.make_async_copy(den.at[pl.ds(0, RIGHT)], down.at[pl.ds(0, RIGHT)], sem.at[2]),
        pltpu.make_async_copy(kap.at[pl.ds(0, RIGHT)], down.at[pl.ds(RIGHT, RIGHT)], sem.at[3]),
    ]
    for copy in copies:
        copy.start()
    for copy in copies:
        copy.wait()


def params(room=ROOM):
    return pltpu.CompilerParams(vmem_limit_bytes=room)


def rows_shape(*lead):
    return jax.ShapeDtypeStruct((*lead, 8, 8, 128), jnp.float32)


def send(den, kap, interpret=False):
    return pl.pallas_call(
        send_kernel,
        out_shape=(
            jax.ShapeDtypeStruct((2 * LEFT, NY, NZ), jnp.float32),
            jax.ShapeDtypeStruct((2 * RIGHT, NY, NZ), jnp.float32),
        ),
        in_specs=[FAR] * 2,
        out_specs=(VMEM, VMEM),
        scratch_shapes=[pltpu.SemaphoreType.DMA((4,))],
        compiler_params=params(8 * 1024 * 1024),
        interpret=interpret,
        name="send",
    )(den, kap)


def inner(den, kap, interpret=False):
    hy3, hz, _, _ = constants()
    return pl.pallas_call(
        inner_kernel,
        out_shape=(rows_shape(ROWS), rows_shape(3, ROWS), rows_shape(4), rows_shape(ITERS), rows_shape(2), rows_shape(2)),
        in_specs=[VMEM] * 4,
        out_specs=(VMEM,) * 6,
        compiler_params=params(),
        cost_estimate=pl.CostEstimate(flops=20_000_000, bytes_accessed=8_000_000, transcendentals=0),
        interpret=interpret,
        name="inner",
    )(den, kap, jnp.asarray(hy3, jnp.bfloat16), jnp.asarray(hz, jnp.bfloat16))


def edge(members, levels, coefs, odd, state, left, right, interpret=False):
    hy3, hz, _, _ = constants()
    return pl.pallas_call(
        edge_kernel,
        out_shape=jax.ShapeDtypeStruct((members, 8 * TILES, 128), jnp.float32),
        in_specs=[SMEM] * 3 + [VMEM] * 10,
        out_specs=VMEM,
        scratch_shapes=[
            pltpu.VMEM((TALL, 8, 8, 128), jnp.float32),
            pltpu.VMEM((3, TALL, 8, 8, 128), jnp.float32),
            pltpu.VMEM((3, 8, 8, 128), jnp.float32),
        ],
        compiler_params=params(),
        interpret=interpret,
        name="edge",
    )(levels, coefs, odd, *state, left, right, jnp.asarray(hy3, jnp.bfloat16), jnp.asarray(hz, jnp.bfloat16))


def diffuse(members, levels, coefs, odd, den, kap, left, right, interpret=False):
    return edge(members, levels, coefs, odd, inner(den, kap, interpret), left, right, interpret)


def spread(levels, odd, mine, other, interpret=False):
    _, _, dy3, dz = constants()
    return pl.pallas_call(
        spread_kernel,
        out_shape=jax.ShapeDtypeStruct((ROWS, NY, NZ), jnp.float32),
        in_specs=[SMEM] * 2 + [VMEM] * 4,
        out_specs=VMEM,
        compiler_params=params(),
        interpret=interpret,
        name="spread",
    )(levels, odd, mine, other, jnp.asarray(dy3, jnp.bfloat16), jnp.asarray(dz, jnp.bfloat16))


def local(density, kappa, levels, coefs):
    den, kap = density[0], kappa[0]
    space, grid = lax.axis_size("space"), lax.axis_size("grid")
    assert den.shape == (ROWS, NY, NZ) and space * ROWS == 512
    up = [(i, (i + 1) % space) for i in range(space)]
    down = [(j, i) for i, j in up]
    pair = [(i, i ^ 1) for i in range(space)]
    going_up, going_down = send(den, kap)
    left = lax.ppermute(going_up, "space", up)
    right = lax.ppermute(going_down, "space", down)
    odd = (lax.axis_index("space") % 2).astype(jnp.int32)[None]
    sent = diffuse(grid, levels, coefs, odd, den, kap, left, right)
    got = lax.all_to_all(sent, "grid", split_axis=0, concat_axis=0, tiled=True)
    total = jnp.sum(got, axis=0)
    other = lax.ppermute(total[: 8 * SHARED], "space", pair)
    return spread(levels, odd, total, other)[None]


def solution(mesh):
    in_specs = (
        P("grid", "space", None, None),
        P("grid", "space", None, None),
        P("grid", None),
        P("grid"),
    )
    out_specs = P("grid", "space", None, None)
    return jax.shard_map(local, mesh=mesh, in_specs=in_specs, out_specs=out_specs, check_vma=False)
```

```python
import functools

import jax
import jax.numpy as jnp
import numpy as np
from jax import lax
from jax.experimental import pallas as pl
from jax.experimental.pallas import tpu as pltpu
from jax.sharding import PartitionSpec as P

ITERS = 8
LOW = 3
SPAN = 3
ROWS = 32
GAP = 8
NODES = ROWS // GAP + 1
LEFT = ITERS
RIGHT = ITERS + 1
TALL = LEFT + ROWS + RIGHT
LOAD_UNROLL = 4
CHUNK = 8
ROOM = 24 * 1024 * 1024
NY = 64
NZ = 128
TOP = 1 << (LOW + SPAN)


def level_order(count):
    step = count >> (LOW + SPAN)
    order = list(range(0, count, count >> LOW))
    for level in range(LOW + 1, LOW + SPAN + 1):
        gap = count >> level
        order += list(range(gap, count, 2 * gap))
    assert len(order) == TOP and all(i % step == 0 for i in order)
    return order


def tables(count):
    order = level_order(count)
    hier = np.eye(count)
    hats = np.eye(count)
    for index in range(1, count):
        gap = index & -index
        hier[index, (index - gap) % count] -= 0.5
        hier[index, (index + gap) % count] -= 0.5
    gap = count // 2
    while gap:
        for index in range(gap, count, 2 * gap):
            hats[index] += 0.5 * (hats[(index - gap) % count] + hats[(index + gap) % count])
        gap //= 2
    return hier[order], hats[:, order]


@functools.lru_cache(None)
def constants():
    hy, dy = tables(NY)
    hz, dz = tables(NZ)
    spread = [v + 8 * s for v in range(8) for s in range(8)]
    hy = hy[:, spread]
    hz_t = np.zeros((NZ, 128))
    hz_t[:, :TOP] = hz.T
    dz_t = np.zeros((128, NZ))
    dz_t[:TOP] = dz.T
    hy3 = np.concatenate([hy] * 3, axis=1)
    dy3 = np.concatenate([dy] * 3, axis=1)
    return tuple(np.asarray(m, np.float32) for m in (hy3, hz_t, dy3, dz_t))


def staircase():
    widths = {0: SPAN, 1: SPAN - 1, 2: SPAN - 2, 3: SPAN - 3, 4: SPAN - 3}
    blocks = []
    place = 0
    for plane, left in widths.items():
        for extra in range(left + 1):
            groups = range(1 << (extra - 1), 1 << extra) if extra else range(1)
            for group in groups:
                width = 1 << (LOW + left - extra)
                blocks.append((plane, group, width, place // 128, place % 128))
                assert place % 128 + width <= 128
                place += width
    return blocks, -(-place // 128)


BLOCKS, TILES = staircase()
SHARED = 1 + max(b[3] for b in BLOCKS if b[0] < 2)


def split3(x):
    hi = x.astype(jnp.bfloat16)
    rest = x - hi.astype(jnp.float32)
    mid = rest.astype(jnp.bfloat16)
    lo = (rest - mid.astype(jnp.float32)).astype(jnp.bfloat16)
    return hi, mid, lo


def rows_dot(weights3, plane):
    stacked = jnp.concatenate(split3(plane), axis=0)
    return jnp.dot(weights3, stacked, preferred_element_type=jnp.float32)


def lanes_dot(planes, weights):
    total = None
    for piece in split3(planes):
        part = jnp.dot(piece, weights, preferred_element_type=jnp.float32)
        total = part if total is None else total + part
    return total


def next_z(row):
    return pltpu.roll(row, NZ - 1, 2)


def prev_z(row):
    return pltpu.roll(row, 1, 2)


def fetch(ref, index):
    row = ref.at[index]
    return jnp.stack([row[pl.ds(v, 8, 8), :] for v in range(8)], axis=0)


def row_coefs(k):
    ahead = jnp.concatenate([k[1:], pltpu.roll(k[0:1], 7, 1)], axis=0)
    behind = pltpu.roll(k[7:8], 1, 1)
    cz, czm = 0.5 * (k + next_z(k)), 0.5 * (k + prev_z(k))
    return 0.5 * (k + ahead), cz, czm, (1.0 - cz) - czm, 0.5 * (k[0] + behind[0])


def step_rows(rows, take, put, coef, first_y, keep=None):
    before, here = take(rows[0] - 1), take(rows[0])
    flux = coef(0, rows[0] - 1) * (here - before)
    for i in rows:
        after = take(i + 1)
        ahead, behind = pltpu.roll(here[0:1], 7, 1), pltpu.roll(here[7:8], 1, 1)
        flux_y = coef(1, i) * (jnp.concatenate([here[1:], ahead], axis=0) - here)
        flux_b = first_y(i) * (here[0] - behind[0])
        along_z = (coef(2, i) * next_z(here) + coef(3, i) * prev_z(here)) + coef(4, i) * here
        flux_x = coef(0, i) * (after - here)
        if keep is not None:
            keep(i, here)
        along_y = flux_y - jnp.concatenate([flux_b[None], flux_y[:7]], axis=0)
        put(i, along_z + ((flux_x - flux) + along_y))
        here, flux = after, flux_x


def inner_rows(step):
    reach = ITERS - step
    if 2 * reach + 1 >= GAP:
        return [range(step, ROWS - step)]
    spans = [range(n - reach, min(n + reach + 1, ROWS - step)) for n in range(GAP, ROWS, GAP)]
    return [r for r in spans if len(r)]


def inner_kernel(den, kap, f_ref, c_ref, cl_ref, old_l, old_r, ends, den_v, kap_v, sem):
    parts = ROWS // CHUNK

    def copies(part):
        at = pl.ds(part * CHUNK, CHUNK)
        return (
            pltpu.make_async_copy(kap.at[at], kap_v.at[at], sem.at[0, part]),
            pltpu.make_async_copy(den.at[at], den_v.at[at], sem.at[1, part]),
        )

    for part in range(parts):
        for copy in copies(part):
            copy.start()
    before = jnp.zeros((8, 8, 128), jnp.float32)
    for part in range(parts):
        for copy in copies(part):
            copy.wait()

        def load(t, before):
            for u in range(LOAD_UNROLL):
                i = part * CHUNK + t * LOAD_UNROLL + u
                k = fetch(kap_v, i)
                f_ref[i] = fetch(den_v, i)
                c_ref[0, jnp.maximum(i - 1, 0)] = 0.5 * (before + k)
                c_ref[1, i], c_ref[2, i], c_ref[3, i], c_ref[4, i], cl_ref[i] = row_coefs(k)
                before = k
            return before

        before = lax.fori_loop(0, CHUNK // LOAD_UNROLL, load, before)
    ends[0] = fetch(kap_v, 0)
    ends[1] = before

    for step in range(1, ITERS + 1):
        for rows in inner_rows(step):
            def keep(i, value, step=step):
                if i == step and step <= 4:
                    old_l[step - 1] = value
                if i == ROWS - 1 - step:
                    old_r[step - 1] = value

            def put(i, value):
                f_ref[i] = value

            step_rows(rows, lambda i: f_ref[i], put, lambda a, i: c_ref[a, i], lambda i: cl_ref[i], keep)
    old_r[ITERS - 1] = f_ref[ROWS - 1 - ITERS]


def hierarchize(rows, hy3, hz, out):
    planes = [rows_dot(hy3[...], row.reshape(NY, NZ)) for row in rows]
    out[...] = lanes_dot(jnp.concatenate(planes, axis=0), hz[...]).reshape(out.shape)


def edge_kernel(lev, coef, odd, f_in, c_in, cl_in, old_l, old_r, ends, left, right, hy3, hz, out, f_new, c_new, cl_new, nodal):
    fresh = set()

    def take(i):
        return f_new[i + LEFT] if i in fresh or not 0 <= i < ROWS else f_in[i]

    def put(i, value):
        fresh.add(i)
        f_new[i + LEFT] = value

    def coef_at(a, i):
        return c_in[a, i] if 0 <= i < ROWS - 1 or (a and i == ROWS - 1) else c_new[a, i + LEFT]

    def first_y(i):
        return cl_in[i] if 0 <= i < ROWS else cl_new[i + LEFT]

    def prepare(source, first, count, edge_row, edge_k):
        before = None
        for t in range(count):
            i = first + t
            k = fetch(source, count + t)
            f_new[i + LEFT] = fetch(source, t)
            at = i + LEFT
            c_new[1, at], c_new[2, at], c_new[3, at], c_new[4, at], cl_new[at] = row_coefs(k)
            if before is not None:
                c_new[0, i - 1 + LEFT] = 0.5 * (before + k)
            if i == edge_row + 1:
                c_new[0, edge_row + LEFT] = 0.5 * (edge_k + k)
            if i == edge_row:
                c_new[0, edge_row + LEFT] = 0.5 * (edge_k + k)
            before = k

    prepare(left, -LEFT, LEFT, -1, ends[0])
    prepare(right, ROWS, RIGHT, ROWS - 1, ends[1])

    for step in range(1, ITERS + 1):
        reach = ITERS - step
        if step <= 4:
            lefts, rights = [range(-reach, step)], [range(ROWS - step, ROWS + reach + 1)]
        else:
            lefts = [range(-reach, reach + 1)]
            rights = [range(ROWS - step, ROWS - step + 1), range(ROWS - reach, ROWS + reach + 1)]

        def take_l(i, step=step):
            return old_l[step - 1] if i == step and step <= 4 else take(i)

        def take_r(i, step=step):
            return old_r[step - 1] if i == ROWS - 1 - step else take(i)

        for k in range(max(len(lefts), len(rights))):
            if k < len(lefts):
                step_rows(lefts[k], take_l, put, coef_at, first_y)
            if k < len(rights):
                step_rows(rights[k], take if k else take_r, put, coef_at, first_y)

    hierarchize([take(n * GAP) for n in range(NODES)], hy3, hz, nodal)
    finish(lev, coef, odd, nodal, out)


def finish(lev, coef, odd, nodal, out):
    level_x, level_y, level_z = lev[0, 0], lev[0, 1], lev[0, 2]
    weight = coef[0].astype(jnp.float32)
    swapped = odd[0] == 1
    lane = lax.broadcasted_iota(jnp.int32, (8, 128), 1)
    groups_y = lax.shift_left(1, level_y - LOW)
    width_z = lax.shift_left(1, level_z)

    def planes_of(group):
        u = [nodal[n, group] for n in range(NODES)]
        outer = jnp.where(swapped, u[4], u[0])
        inner = jnp.where(swapped, u[0], u[4])
        return (
            outer,
            0.5 * (inner - outer),
            u[2] - 0.5 * (u[0] + u[4]),
            u[1] - 0.5 * (u[0] + u[2]),
            u[3] - 0.5 * (u[2] + u[4]),
        )

    need = (LOW, LOW + 1, LOW + 2, LOW + 3, LOW + 3)
    cache = {}
    tiles = [jnp.zeros((8, 128), jnp.float32)] * TILES
    for plane, group, width, tile, first in BLOCKS:
        if group not in cache:
            cache[group] = planes_of(group)
        keep = (lane < jnp.minimum(width_z, width)) & (group < groups_y) & (level_x >= need[plane])
        value = jnp.where(keep, weight * cache[group][plane], 0.0)
        tiles[tile] = tiles[tile] + (pltpu.roll(value, first, 1) if first else value)
    for member in range(out.shape[0]):
        for tile in range(TILES):
            out[member, 8 * tile : 8 * tile + 8] = tiles[tile]


def spread_kernel(lev, odd, mine, other, dy3, dz, out):
    level_x, level_y, level_z = lev[0, 0], lev[0, 1], lev[0, 2]
    swapped = odd[0] == 1
    lane = lax.broadcasted_iota(jnp.int32, (8, 128), 1)
    groups_y = lax.shift_left(1, level_y - LOW)
    width_z = lax.shift_left(1, level_z)
    need = (LOW, LOW + 1, LOW + 2, LOW + 3, LOW + 3)
    own = [mine[8 * t : 8 * t + 8] for t in range(TILES)]
    theirs = [other[8 * t : 8 * t + 8] for t in range(SHARED)]
    zero = jnp.zeros((8, 128), jnp.float32)
    planes = [[zero] * 8 for _ in range(5)]
    outer_other = [zero] * 8
    for plane, group, width, tile, first in BLOCKS:
        keep = (lane < jnp.minimum(width_z, width)) & (group < groups_y) & (level_x >= need[plane])

        def pick(source):
            value = pltpu.roll(source, 128 - first, 1) if first else source
            return jnp.where(keep, value, 0.0)

        if plane == 0:
            planes[0][group] = pick(own[tile])
            outer_other[group] = pick(theirs[tile])
        elif plane == 1:
            planes[1][group] = pick(own[tile] + theirs[tile])
        else:
            planes[plane][group] = pick(own[tile])
    wide = []
    outer = jnp.concatenate(planes[0], axis=0)
    middle = 0.5 * (outer + jnp.concatenate(outer_other, axis=0)) + jnp.concatenate(planes[1], axis=0)
    n0 = jnp.where(swapped, middle, outer)
    n4 = jnp.where(swapped, outer, middle)
    n2 = 0.5 * (n0 + n4) + jnp.concatenate(planes[2], axis=0)
    n1 = 0.5 * (n0 + n2) + jnp.concatenate(planes[3], axis=0)
    n3 = 0.5 * (n2 + n4) + jnp.concatenate(planes[4], axis=0)
    for n in (n0, n1, n2, n3, n4):
        wide.append(rows_dot(dy3[...], n))
    full = lanes_dot(jnp.concatenate(wide, axis=0), dz[...]).reshape(NODES, NY, NZ)
    for q in range(NODES - 1):
        slope = (full[q + 1] - full[q]) * (1.0 / GAP)
        for k in range(GAP):
            out[q * GAP + k] = full[q] + float(k) * slope


VMEM = pl.BlockSpec(memory_space=pltpu.VMEM)
SMEM = pl.BlockSpec(memory_space=pltpu.SMEM)
FAR = pl.BlockSpec(memory_space=pltpu.HBM)


def send_kernel(den, kap, up, down, sem):
    copies = [
        pltpu.make_async_copy(den.at[pl.ds(ROWS - LEFT, LEFT)], up.at[pl.ds(0, LEFT)], sem.at[0]),
        pltpu.make_async_copy(kap.at[pl.ds(ROWS - LEFT, LEFT)], up.at[pl.ds(LEFT, LEFT)], sem.at[1]),
        pltpu.make_async_copy(den.at[pl.ds(0, RIGHT)], down.at[pl.ds(0, RIGHT)], sem.at[2]),
        pltpu.make_async_copy(kap.at[pl.ds(0, RIGHT)], down.at[pl.ds(RIGHT, RIGHT)], sem.at[3]),
    ]
    for copy in copies:
        copy.start()
    for copy in copies:
        copy.wait()


def params(room=ROOM):
    return pltpu.CompilerParams(vmem_limit_bytes=room)


def rows_shape(*lead):
    return jax.ShapeDtypeStruct((*lead, 8, 8, 128), jnp.float32)


def far(x):
    return pltpu.with_memory_space_constraint(x, pltpu.HBM)


def send(den, kap, interpret=False):
    return pl.pallas_call(
        send_kernel,
        out_shape=(
            jax.ShapeDtypeStruct((2 * LEFT, NY, NZ), jnp.float32),
            jax.ShapeDtypeStruct((2 * RIGHT, NY, NZ), jnp.float32),
        ),
        in_specs=[FAR] * 2,
        out_specs=(VMEM, VMEM),
        scratch_shapes=[pltpu.SemaphoreType.DMA((4,))],
        compiler_params=params(8 * 1024 * 1024),
        interpret=interpret,
        name="send",
    )(far(den), far(kap))


def inner(den, kap, interpret=False):
    rows = rows_shape(ROWS)
    return pl.pallas_call(
        inner_kernel,
        out_shape=(
            rows,
            rows_shape(5, ROWS),
            jax.ShapeDtypeStruct((ROWS, 8, 128), jnp.float32),
            rows_shape(4),
            rows_shape(ITERS),
            rows_shape(2),
        ),
        in_specs=[FAR] * 2,
        out_specs=(VMEM,) * 6,
        scratch_shapes=[pltpu.VMEM((ROWS, NY, NZ), jnp.float32)] * 2 + [pltpu.SemaphoreType.DMA((2, ROWS // CHUNK))],
        compiler_params=params(),
        cost_estimate=pl.CostEstimate(flops=20_000_000, bytes_accessed=8_000_000, transcendentals=0),
        interpret=interpret,
        name="inner",
    )(far(den), far(kap))


def edge(members, levels, coefs, odd, state, left, right, interpret=False):
    hy3, hz, _, _ = constants()
    return pl.pallas_call(
        edge_kernel,
        out_shape=jax.ShapeDtypeStruct((members, 8 * TILES, 128), jnp.float32),
        in_specs=[SMEM] * 3 + [VMEM] * 10,
        out_specs=VMEM,
        scratch_shapes=[
            pltpu.VMEM((TALL, 8, 8, 128), jnp.float32),
            pltpu.VMEM((5, TALL, 8, 8, 128), jnp.float32),
            pltpu.VMEM((TALL, 8, 128), jnp.float32),
            pltpu.VMEM((NODES, 8, 8, 128), jnp.float32),
        ],
        compiler_params=params(),
        interpret=interpret,
        name="edge",
    )(levels, coefs, odd, *state, left, right, jnp.asarray(hy3, jnp.bfloat16), jnp.asarray(hz, jnp.bfloat16))


def diffuse(members, levels, coefs, odd, den, kap, left, right, interpret=False):
    return edge(members, levels, coefs, odd, inner(den, kap, interpret), left, right, interpret)


def spread(levels, odd, mine, other, interpret=False):
    _, _, dy3, dz = constants()
    return pl.pallas_call(
        spread_kernel,
        out_shape=jax.ShapeDtypeStruct((ROWS, NY, NZ), jnp.float32),
        in_specs=[SMEM] * 2 + [VMEM] * 4,
        out_specs=VMEM,
        compiler_params=params(),
        interpret=interpret,
        name="spread",
    )(levels, odd, mine, other, jnp.asarray(dy3, jnp.bfloat16), jnp.asarray(dz, jnp.bfloat16))


def local(density, kappa, levels, coefs):
    den, kap = density[0], kappa[0]
    space, grid = lax.axis_size("space"), lax.axis_size("grid")
    assert den.shape == (ROWS, NY, NZ) and space * ROWS == 512
    up = [(i, (i + 1) % space) for i in range(space)]
    down = [(j, i) for i, j in up]
    pair = [(i, i ^ 1) for i in range(space)]
    going_up, going_down = send(den, kap)
    left = lax.ppermute(going_up, "space", up)
    right = lax.ppermute(going_down, "space", down)
    odd = (lax.axis_index("space") % 2).astype(jnp.int32)[None]
    sent = diffuse(grid, levels, coefs, odd, den, kap, left, right)
    got = lax.all_to_all(sent, "grid", split_axis=0, concat_axis=0, tiled=True)
    total = jnp.sum(got, axis=0)
    other = lax.ppermute(total[: 8 * SHARED], "space", pair)
    return spread(levels, odd, total, other)[None]


def solution(mesh):
    in_specs = (
        P("grid", "space", None, None),
        P("grid", "space", None, None),
        P("grid", None),
        P("grid"),
    )
    out_specs = P("grid", "space", None, None)
    return jax.shard_map(local, mesh=mesh, in_specs=in_specs, out_specs=out_specs, check_vma=False)
```

```python
import functools

import jax
import jax.numpy as jnp
import numpy as np
from jax import lax
from jax.experimental import pallas as pl
from jax.experimental.pallas import tpu as pltpu
from jax.sharding import PartitionSpec as P

ITERS = 8
LOW = 3
SPAN = 3
ROWS = 32
GAP = 8
NODES = ROWS // GAP + 1
LEFT = ITERS
RIGHT = ITERS + 1
TALL = LEFT + ROWS + RIGHT
LOAD_UNROLL = 4
CHUNK = 8
ROOM = 24 * 1024 * 1024
NY = 64
NZ = 128
TOP = 1 << (LOW + SPAN)


def level_order(count):
    step = count >> (LOW + SPAN)
    order = list(range(0, count, count >> LOW))
    for level in range(LOW + 1, LOW + SPAN + 1):
        gap = count >> level
        order += list(range(gap, count, 2 * gap))
    assert len(order) == TOP and all(i % step == 0 for i in order)
    return order


def tables(count):
    order = level_order(count)
    hier = np.eye(count)
    hats = np.eye(count)
    for index in range(1, count):
        gap = index & -index
        hier[index, (index - gap) % count] -= 0.5
        hier[index, (index + gap) % count] -= 0.5
    gap = count // 2
    while gap:
        for index in range(gap, count, 2 * gap):
            hats[index] += 0.5 * (hats[(index - gap) % count] + hats[(index + gap) % count])
        gap //= 2
    return hier[order], hats[:, order]


@functools.lru_cache(None)
def constants():
    hy, dy = tables(NY)
    hz, dz = tables(NZ)
    spread = [v + 8 * s for v in range(8) for s in range(8)]
    hy = hy[:, spread]
    hz_t = np.zeros((NZ, 128))
    hz_t[:, :TOP] = hz.T
    dz_t = np.zeros((128, NZ))
    dz_t[:TOP] = dz.T
    hy3 = np.concatenate([hy] * 3, axis=1)
    dy3 = np.concatenate([dy] * 3, axis=1)
    return tuple(np.asarray(m, np.float32) for m in (hy3, hz_t, dy3, dz_t))


def staircase():
    widths = {0: SPAN, 1: SPAN - 1, 2: SPAN - 2, 3: SPAN - 3, 4: SPAN - 3}
    blocks = []
    place = 0
    for plane, left in widths.items():
        for extra in range(left + 1):
            groups = range(1 << (extra - 1), 1 << extra) if extra else range(1)
            for group in groups:
                width = 1 << (LOW + left - extra)
                blocks.append((plane, group, width, place // 128, place % 128))
                assert place % 128 + width <= 128
                place += width
    return blocks, -(-place // 128)


BLOCKS, TILES = staircase()
NEED = (LOW, LOW + 1, LOW + 2, LOW + 3, LOW + 3)
SHARED = 1 + max(b[3] for b in BLOCKS if b[0] < 2)


def split3(x):
    hi = x.astype(jnp.bfloat16)
    rest = x - hi.astype(jnp.float32)
    mid = rest.astype(jnp.bfloat16)
    lo = (rest - mid.astype(jnp.float32)).astype(jnp.bfloat16)
    return hi, mid, lo


def rows_dot(weights3, plane):
    stacked = jnp.concatenate(split3(plane), axis=0)
    return jnp.dot(weights3, stacked, preferred_element_type=jnp.float32)


def lanes_dot(planes, weights):
    total = None
    for piece in split3(planes):
        part = jnp.dot(piece, weights, preferred_element_type=jnp.float32)
        total = part if total is None else total + part
    return total


def next_z(row):
    return pltpu.roll(row, NZ - 1, 2)


def prev_z(row):
    return pltpu.roll(row, 1, 2)


def fetch(ref, index):
    row = ref.at[index]
    return jnp.stack([row[pl.ds(v, 8, 8), :] for v in range(8)], axis=0)


def row_coefs(k):
    ahead = jnp.concatenate([k[1:], pltpu.roll(k[0:1], 7, 1)], axis=0)
    behind = pltpu.roll(k[7:8], 1, 1)
    cz, czm = 0.5 * (k + next_z(k)), 0.5 * (k + prev_z(k))
    return 0.5 * (k + ahead), cz, czm, (1.0 - cz) - czm, 0.5 * (k[0] + behind[0])


def step_rows(rows, take, put, coef, first_y, keep=None):
    before, here = take(rows[0] - 1), take(rows[0])
    flux = coef(0, rows[0] - 1) * (here - before)
    for i in rows:
        after = take(i + 1)
        ahead, behind = pltpu.roll(here[0:1], 7, 1), pltpu.roll(here[7:8], 1, 1)
        flux_y = coef(1, i) * (jnp.concatenate([here[1:], ahead], axis=0) - here)
        flux_b = first_y(i) * (here[0] - behind[0])
        along_z = (coef(2, i) * next_z(here) + coef(3, i) * prev_z(here)) + coef(4, i) * here
        flux_x = coef(0, i) * (after - here)
        if keep is not None:
            keep(i, here)
        along_y = flux_y - jnp.concatenate([flux_b[None], flux_y[:7]], axis=0)
        put(i, along_z + ((flux_x - flux) + along_y))
        here, flux = after, flux_x


def inner_rows(step):
    reach = ITERS - step
    if 2 * reach + 1 >= GAP:
        return [range(step, ROWS - step)]
    spans = [range(n - reach, min(n + reach + 1, ROWS - step)) for n in range(GAP, ROWS, GAP)]
    return [r for r in spans if len(r)]


def write_marks(lev, coef, odd, marks):
    level_x, level_y, level_z = lev[0, 0], lev[0, 1], lev[0, 2]
    weight = coef[0].astype(jnp.float32)
    lane = lax.broadcasted_iota(jnp.int32, (8, 128), 1)
    groups_y = lax.shift_left(1, level_y - LOW)
    width_z = lax.shift_left(1, level_z)
    for b, (plane, group, width, _, _) in enumerate(BLOCKS):
        keep = (lane < jnp.minimum(width_z, width)) & (group < groups_y) & (level_x >= NEED[plane])
        kept = jnp.where(keep, 1.0, 0.0)
        marks[b] = kept
        marks[len(BLOCKS) + b] = weight * kept
    marks[2 * len(BLOCKS)] = jnp.full((8, 128), odd[0].astype(jnp.float32))


def inner_kernel(lev, coef, odd, den, kap, hy3, hz, f_ref, c_ref, cl_ref, old_l, old_r, ends, marks, hy3_v, hz_v, den_v, kap_v, sem, sem_w):
    parts = ROWS // CHUNK

    def copies(part):
        at = pl.ds(part * CHUNK, CHUNK)
        return (
            pltpu.make_async_copy(kap.at[at], kap_v.at[at], sem.at[0, part]),
            pltpu.make_async_copy(den.at[at], den_v.at[at], sem.at[1, part]),
        )

    for part in range(parts):
        for copy in copies(part):
            copy.start()
    weights = [pltpu.make_async_copy(hy3, hy3_v, sem_w.at[0]), pltpu.make_async_copy(hz, hz_v, sem_w.at[1])]
    for copy in weights:
        copy.start()
    write_marks(lev, coef, odd, marks)
    before = jnp.zeros((8, 8, 128), jnp.float32)
    for part in range(parts):
        for copy in copies(part):
            copy.wait()

        def load(t, before):
            for u in range(LOAD_UNROLL):
                i = part * CHUNK + t * LOAD_UNROLL + u
                k = fetch(kap_v, i)
                f_ref[i] = fetch(den_v, i)
                c_ref[0, jnp.maximum(i - 1, 0)] = 0.5 * (before + k)
                c_ref[1, i], c_ref[2, i], c_ref[3, i], c_ref[4, i], cl_ref[i] = row_coefs(k)
                before = k
            return before

        before = lax.fori_loop(0, CHUNK // LOAD_UNROLL, load, before)
    ends[0] = fetch(kap_v, 0)
    ends[1] = before

    for step in range(1, ITERS + 1):
        for rows in inner_rows(step):
            def keep(i, value, step=step):
                if i == step and step <= 4:
                    old_l[step - 1] = value
                if i == ROWS - 1 - step:
                    old_r[step - 1] = value

            def put(i, value):
                f_ref[i] = value

            step_rows(rows, lambda i: f_ref[i], put, lambda a, i: c_ref[a, i], lambda i: cl_ref[i], keep)
    old_r[ITERS - 1] = f_ref[ROWS - 1 - ITERS]
    for copy in weights:
        copy.wait()


def hierarchize(rows, hy3, hz, out):
    planes = [rows_dot(hy3[...], row.reshape(NY, NZ)) for row in rows]
    out[...] = lanes_dot(jnp.concatenate(planes, axis=0), hz[...]).reshape(out.shape)


def edge_kernel(f_in, c_in, cl_in, old_l, old_r, ends, marks, hy3, hz, left, right, out, f_new, c_new, cl_new, nodal):
    fresh = set()

    def take(i):
        return f_new[i + LEFT] if i in fresh or not 0 <= i < ROWS else f_in[i]

    def put(i, value):
        fresh.add(i)
        f_new[i + LEFT] = value

    def coef_at(a, i):
        return c_in[a, i] if 0 <= i < ROWS - 1 or (a and i == ROWS - 1) else c_new[a, i + LEFT]

    def first_y(i):
        return cl_in[i] if 0 <= i < ROWS else cl_new[i + LEFT]

    def prepare(source, first, count, edge_row, edge_k):
        before = None
        for t in range(count):
            i = first + t
            k = fetch(source, count + t)
            f_new[i + LEFT] = fetch(source, t)
            at = i + LEFT
            c_new[1, at], c_new[2, at], c_new[3, at], c_new[4, at], cl_new[at] = row_coefs(k)
            if before is not None:
                c_new[0, i - 1 + LEFT] = 0.5 * (before + k)
            if i == edge_row + 1:
                c_new[0, edge_row + LEFT] = 0.5 * (edge_k + k)
            if i == edge_row:
                c_new[0, edge_row + LEFT] = 0.5 * (edge_k + k)
            before = k

    prepare(left, -LEFT, LEFT, -1, ends[0])
    prepare(right, ROWS, RIGHT, ROWS - 1, ends[1])

    for step in range(1, ITERS + 1):
        reach = ITERS - step
        if step <= 4:
            lefts, rights = [range(-reach, step)], [range(ROWS - step, ROWS + reach + 1)]
        else:
            lefts = [range(-reach, reach + 1)]
            rights = [range(ROWS - step, ROWS - step + 1), range(ROWS - reach, ROWS + reach + 1)]

        def take_l(i, step=step):
            return old_l[step - 1] if i == step and step <= 4 else take(i)

        def take_r(i, step=step):
            return old_r[step - 1] if i == ROWS - 1 - step else take(i)

        for k in range(max(len(lefts), len(rights))):
            if k < len(lefts):
                step_rows(lefts[k], take_l, put, coef_at, first_y)
            if k < len(rights):
                step_rows(rights[k], take if k else take_r, put, coef_at, first_y)

    hierarchize([take(n * GAP) for n in range(NODES)], hy3, hz, nodal)
    finish(marks, nodal, out)


def finish(marks, nodal, out):
    swapped = marks[2 * len(BLOCKS)] > 0.5

    def planes_of(group):
        u = [nodal[n, group] for n in range(NODES)]
        outer = jnp.where(swapped, u[4], u[0])
        inner = jnp.where(swapped, u[0], u[4])
        return (
            outer,
            0.5 * (inner - outer),
            u[2] - 0.5 * (u[0] + u[4]),
            u[1] - 0.5 * (u[0] + u[2]),
            u[3] - 0.5 * (u[2] + u[4]),
        )

    cache = {}
    tiles = [jnp.zeros((8, 128), jnp.float32)] * TILES
    for b, (plane, group, width, tile, first) in enumerate(BLOCKS):
        if group not in cache:
            cache[group] = planes_of(group)
        value = marks[len(BLOCKS) + b] * cache[group][plane]
        tiles[tile] = tiles[tile] + (pltpu.roll(value, first, 1) if first else value)
    for member in range(out.shape[0]):
        for tile in range(TILES):
            out[member, 8 * tile : 8 * tile + 8] = tiles[tile]


def spread_kernel(marks, mine, other, dy3, dz, out, held, sem):
    swapped = marks[2 * len(BLOCKS), 0:1] > 0.5
    own = [mine[8 * t : 8 * t + 8] for t in range(TILES)]
    theirs = [other[8 * t : 8 * t + 8] for t in range(SHARED)]
    zero = jnp.zeros((8, 128), jnp.float32)
    planes = [[zero] * 8 for _ in range(5)]
    outer_other = [zero] * 8
    for b, (plane, group, width, tile, first) in enumerate(BLOCKS):

        def pick(source):
            value = pltpu.roll(source, 128 - first, 1) if first else source
            return marks[b] * value

        if plane == 0:
            planes[0][group] = pick(own[tile])
            outer_other[group] = pick(theirs[tile])
        elif plane == 1:
            planes[1][group] = pick(own[tile] + theirs[tile])
        else:
            planes[plane][group] = pick(own[tile])
    wide = []
    outer = jnp.concatenate(planes[0], axis=0)
    middle = 0.5 * (outer + jnp.concatenate(outer_other, axis=0)) + jnp.concatenate(planes[1], axis=0)
    n0 = jnp.where(swapped, middle, outer)
    n4 = jnp.where(swapped, outer, middle)
    n2 = 0.5 * (n0 + n4) + jnp.concatenate(planes[2], axis=0)
    n1 = 0.5 * (n0 + n2) + jnp.concatenate(planes[3], axis=0)
    n3 = 0.5 * (n2 + n4) + jnp.concatenate(planes[4], axis=0)
    for n in (n0, n1, n2, n3, n4):
        wide.append(rows_dot(dy3[...], n))
    full = lanes_dot(jnp.concatenate(wide, axis=0), dz[...]).reshape(NODES, NY, NZ)
    copies = []
    for q in range(NODES - 1):
        slope = (full[q + 1] - full[q]) * (1.0 / GAP)
        for k in range(GAP):
            held[q * GAP + k] = full[q] + float(k) * slope
        at = pl.ds(q * GAP, GAP)
        copies.append(pltpu.make_async_copy(held.at[at], out.at[at], sem.at[q]))
        copies[-1].start()
    for copy in copies:
        copy.wait()


VMEM = pl.BlockSpec(memory_space=pltpu.VMEM)
SMEM = pl.BlockSpec(memory_space=pltpu.SMEM)
FAR = pl.BlockSpec(memory_space=pltpu.HBM)


def send_kernel(den, kap, up, down, sem):
    copies = [
        pltpu.make_async_copy(den.at[pl.ds(ROWS - LEFT, LEFT)], up.at[pl.ds(0, LEFT)], sem.at[0]),
        pltpu.make_async_copy(kap.at[pl.ds(ROWS - LEFT, LEFT)], up.at[pl.ds(LEFT, LEFT)], sem.at[1]),
        pltpu.make_async_copy(den.at[pl.ds(0, RIGHT)], down.at[pl.ds(0, RIGHT)], sem.at[2]),
        pltpu.make_async_copy(kap.at[pl.ds(0, RIGHT)], down.at[pl.ds(RIGHT, RIGHT)], sem.at[3]),
    ]
    for copy in copies:
        copy.start()
    for copy in copies:
        copy.wait()


def params(room=ROOM):
    return pltpu.CompilerParams(vmem_limit_bytes=room)


def rows_shape(*lead):
    return jax.ShapeDtypeStruct((*lead, 8, 8, 128), jnp.float32)


def far(x):
    return pltpu.with_memory_space_constraint(x, pltpu.HBM)


def send(den, kap, interpret=False):
    return pl.pallas_call(
        send_kernel,
        out_shape=(
            jax.ShapeDtypeStruct((2 * LEFT, NY, NZ), jnp.float32),
            jax.ShapeDtypeStruct((2 * RIGHT, NY, NZ), jnp.float32),
        ),
        in_specs=[FAR] * 2,
        out_specs=(VMEM, VMEM),
        scratch_shapes=[pltpu.SemaphoreType.DMA((4,))],
        compiler_params=params(8 * 1024 * 1024),
        interpret=interpret,
        name="send",
    )(far(den), far(kap))


def inner(levels, coefs, odd, den, kap, interpret=False):
    rows = rows_shape(ROWS)
    hy3, hz, _, _ = constants()
    return pl.pallas_call(
        inner_kernel,
        out_shape=(
            rows,
            rows_shape(5, ROWS),
            jax.ShapeDtypeStruct((ROWS, 8, 128), jnp.float32),
            rows_shape(4),
            rows_shape(ITERS),
            rows_shape(2),
            jax.ShapeDtypeStruct((2 * len(BLOCKS) + 1, 8, 128), jnp.float32),
            jax.ShapeDtypeStruct(hy3.shape, jnp.bfloat16),
            jax.ShapeDtypeStruct(hz.shape, jnp.bfloat16),
        ),
        in_specs=[SMEM] * 3 + [FAR] * 4,
        out_specs=(VMEM,) * 9,
        scratch_shapes=[pltpu.VMEM((ROWS, NY, NZ), jnp.float32)] * 2
        + [pltpu.SemaphoreType.DMA((2, ROWS // CHUNK)), pltpu.SemaphoreType.DMA((2,))],
        compiler_params=params(),
        cost_estimate=pl.CostEstimate(flops=20_000_000, bytes_accessed=8_000_000, transcendentals=0),
        interpret=interpret,
        name="inner",
    )(levels, coefs, odd, far(den), far(kap), far(jnp.asarray(hy3, jnp.bfloat16)), far(jnp.asarray(hz, jnp.bfloat16)))


def edge(members, state, left, right, interpret=False):
    return pl.pallas_call(
        edge_kernel,
        out_shape=jax.ShapeDtypeStruct((members, 8 * TILES, 128), jnp.float32),
        in_specs=[VMEM] * 11,
        out_specs=VMEM,
        scratch_shapes=[
            pltpu.VMEM((TALL, 8, 8, 128), jnp.float32),
            pltpu.VMEM((5, TALL, 8, 8, 128), jnp.float32),
            pltpu.VMEM((TALL, 8, 128), jnp.float32),
            pltpu.VMEM((NODES, 8, 8, 128), jnp.float32),
        ],
        compiler_params=params(),
        interpret=interpret,
        name="edge",
    )(*state, left, right)


def spread(marks, mine, other, interpret=False):
    _, _, dy3, dz = constants()
    return pl.pallas_call(
        spread_kernel,
        out_shape=jax.ShapeDtypeStruct((ROWS, NY, NZ), jnp.float32),
        in_specs=[VMEM] * 5,
        out_specs=FAR,
        scratch_shapes=[pltpu.VMEM((ROWS, NY, NZ), jnp.float32), pltpu.SemaphoreType.DMA((NODES - 1,))],
        compiler_params=params(),
        interpret=interpret,
        name="spread",
    )(marks, mine, other, jnp.asarray(dy3, jnp.bfloat16), jnp.asarray(dz, jnp.bfloat16))


def local(density, kappa, levels, coefs):
    den, kap = density[0], kappa[0]
    space, grid = lax.axis_size("space"), lax.axis_size("grid")
    assert den.shape == (ROWS, NY, NZ) and space * ROWS == 512
    up = [(i, (i + 1) % space) for i in range(space)]
    down = [(j, i) for i, j in up]
    pair = [(i, i ^ 1) for i in range(space)]
    going_up, going_down = send(den, kap)
    left = lax.ppermute(going_up, "space", up)
    right = lax.ppermute(going_down, "space", down)
    odd = (lax.axis_index("space") % 2).astype(jnp.int32)[None]
    state = inner(levels, coefs, odd, den, kap)
    sent = edge(grid, state, left, right)
    got = lax.all_to_all(sent, "grid", split_axis=0, concat_axis=0, tiled=True)
    total = jnp.sum(got, axis=0)
    other = lax.ppermute(total[: 8 * SHARED], "space", pair)
    return spread(state[6], total, other)[None]


def solution(mesh):
    in_specs = (
        P("grid", "space", None, None),
        P("grid", "space", None, None),
        P("grid", None),
        P("grid"),
    )
    out_specs = P("grid", "space", None, None)
    return jax.shard_map(local, mesh=mesh, in_specs=in_specs, out_specs=out_specs, check_vma=False)
```

```python
import functools

import jax
import jax.numpy as jnp
import numpy as np
from jax import lax
from jax.experimental import pallas as pl
from jax.experimental.pallas import tpu as pltpu
from jax.sharding import PartitionSpec as P

ITERS = 8
LOW = 3
SPAN = 3
ROWS = 32
GAP = 8
NODES = ROWS // GAP + 1
LEFT = ITERS
RIGHT = ITERS + 1
TALL = LEFT + ROWS + RIGHT
LOAD_UNROLL = 4
CHUNK = 8
ROOM = 24 * 1024 * 1024
NY = 64
NZ = 128
TOP = 1 << (LOW + SPAN)


def level_order(count):
    step = count >> (LOW + SPAN)
    order = list(range(0, count, count >> LOW))
    for level in range(LOW + 1, LOW + SPAN + 1):
        gap = count >> level
        order += list(range(gap, count, 2 * gap))
    assert len(order) == TOP and all(i % step == 0 for i in order)
    return order


def tables(count):
    order = level_order(count)
    hier = np.eye(count)
    hats = np.eye(count)
    for index in range(1, count):
        gap = index & -index
        hier[index, (index - gap) % count] -= 0.5
        hier[index, (index + gap) % count] -= 0.5
    gap = count // 2
    while gap:
        for index in range(gap, count, 2 * gap):
            hats[index] += 0.5 * (hats[(index - gap) % count] + hats[(index + gap) % count])
        gap //= 2
    return hier[order], hats[:, order]


@functools.lru_cache(None)
def constants():
    hy, dy = tables(NY)
    hz, dz = tables(NZ)
    spread = [v + 8 * s for v in range(8) for s in range(8)]
    hy = hy[:, spread]
    hz_t = np.zeros((NZ, 128))
    hz_t[:, :TOP] = hz.T
    dz_t = np.zeros((128, NZ))
    dz_t[:TOP] = dz.T
    hy3 = np.concatenate([hy] * 3, axis=1)
    dy3 = np.concatenate([dy] * 3, axis=1)
    return tuple(np.asarray(m, np.float32) for m in (hy3, hz_t, dy3, dz_t))


def staircase():
    spare = {0: SPAN, 1: SPAN - 1, 2: SPAN - 2, 3: SPAN - 3, 4: SPAN - 3}
    summed, kept = [], []
    for plane, left in spare.items():
        for extra in range(left + 1):
            whole = 1 << (LOW + left - extra)
            half = whole // 2 if extra < left else 0
            groups = range(1 << (extra - 1), 1 << extra) if extra else range(1)
            for group in groups:
                if half:
                    summed.append((plane, group, 0, half))
                kept.append((plane, group, half, whole - half))
    blocks = []
    for base, pieces in ((0, summed), (1, kept)):
        place = 0
        for piece in pieces:
            assert place % 128 + piece[3] <= 128
            blocks.append((*piece, base + place // 128, place % 128))
            place += piece[3]
        assert base or place <= 128
    return blocks, 1 + max(b[4] for b in blocks)


BLOCKS, TILES = staircase()
NEED = (LOW, LOW + 1, LOW + 2, LOW + 3, LOW + 3)


def shifted(value, lanes):
    return pltpu.roll(value, lanes % 128, 1) if lanes % 128 else value


def split3(x):
    hi = x.astype(jnp.bfloat16)
    rest = x - hi.astype(jnp.float32)
    mid = rest.astype(jnp.bfloat16)
    lo = (rest - mid.astype(jnp.float32)).astype(jnp.bfloat16)
    return hi, mid, lo


def rows_dot(weights3, plane):
    stacked = jnp.concatenate(split3(plane), axis=0)
    return jnp.dot(weights3, stacked, preferred_element_type=jnp.float32)


def lanes_dot(planes, weights):
    total = None
    for piece in split3(planes):
        part = jnp.dot(piece, weights, preferred_element_type=jnp.float32)
        total = part if total is None else total + part
    return total


def next_z(row):
    return pltpu.roll(row, NZ - 1, 2)


def prev_z(row):
    return pltpu.roll(row, 1, 2)


def fetch(ref, index):
    row = ref.at[index]
    return jnp.stack([row[pl.ds(v, 8, 8), :] for v in range(8)], axis=0)


def row_coefs(k):
    ahead = jnp.concatenate([k[1:], pltpu.roll(k[0:1], 7, 1)], axis=0)
    behind = pltpu.roll(k[7:8], 1, 1)
    cz, czm = 0.5 * (k + next_z(k)), 0.5 * (k + prev_z(k))
    return 0.5 * (k + ahead), cz, czm, (1.0 - cz) - czm, 0.5 * (k[0] + behind[0])


def step_rows(rows, take, put, coef, first_y, keep=None):
    before, here = take(rows[0] - 1), take(rows[0])
    flux = coef(0, rows[0] - 1) * (here - before)
    for i in rows:
        after = take(i + 1)
        ahead, behind = pltpu.roll(here[0:1], 7, 1), pltpu.roll(here[7:8], 1, 1)
        flux_y = coef(1, i) * (jnp.concatenate([here[1:], ahead], axis=0) - here)
        flux_b = first_y(i) * (here[0] - behind[0])
        along_z = (coef(2, i) * next_z(here) + coef(3, i) * prev_z(here)) + coef(4, i) * here
        flux_x = coef(0, i) * (after - here)
        if keep is not None:
            keep(i, here)
        along_y = flux_y - jnp.concatenate([flux_b[None], flux_y[:7]], axis=0)
        put(i, along_z + ((flux_x - flux) + along_y))
        here, flux = after, flux_x


def inner_rows(step):
    reach = ITERS - step
    if 2 * reach + 1 >= GAP:
        return [range(step, ROWS - step)]
    spans = [range(n - reach, min(n + reach + 1, ROWS - step)) for n in range(GAP, ROWS, GAP)]
    return [r for r in spans if len(r)]


def write_marks(lev, coef, odd, marks):
    level_x, level_y, level_z = lev[0, 0], lev[0, 1], lev[0, 2]
    weight = coef[0].astype(jnp.float32)
    lane = lax.broadcasted_iota(jnp.int32, (8, 128), 1)
    groups_y = lax.shift_left(1, level_y - LOW)
    width_z = lax.shift_left(1, level_z)
    for b, (plane, group, source, width, _, _) in enumerate(BLOCKS):
        keep = (lane >= source) & (lane < jnp.minimum(width_z, source + width)) & (group < groups_y) & (level_x >= NEED[plane])
        kept = jnp.where(keep, 1.0, 0.0)
        marks[b] = kept
        marks[len(BLOCKS) + b] = weight * kept
    marks[2 * len(BLOCKS)] = jnp.full((8, 128), odd[0].astype(jnp.float32))


def inner_kernel(lev, coef, odd, den, kap, hy3, hz, f_ref, c_ref, cl_ref, old_l, old_r, ends, marks, hy3_v, hz_v, den_v, kap_v, sem, sem_w):
    parts = ROWS // CHUNK

    def copies(part):
        at = pl.ds(part * CHUNK, CHUNK)
        return (
            pltpu.make_async_copy(kap.at[at], kap_v.at[at], sem.at[0, part]),
            pltpu.make_async_copy(den.at[at], den_v.at[at], sem.at[1, part]),
        )

    for part in range(parts):
        for copy in copies(part):
            copy.start()
    weights = [pltpu.make_async_copy(hy3, hy3_v, sem_w.at[0]), pltpu.make_async_copy(hz, hz_v, sem_w.at[1])]
    for copy in weights:
        copy.start()
    write_marks(lev, coef, odd, marks)
    before = jnp.zeros((8, 8, 128), jnp.float32)
    for part in range(parts):
        for copy in copies(part):
            copy.wait()

        def load(t, before):
            for u in range(LOAD_UNROLL):
                i = part * CHUNK + t * LOAD_UNROLL + u
                k = fetch(kap_v, i)
                f_ref[i] = fetch(den_v, i)
                c_ref[0, jnp.maximum(i - 1, 0)] = 0.5 * (before + k)
                c_ref[1, i], c_ref[2, i], c_ref[3, i], c_ref[4, i], cl_ref[i] = row_coefs(k)
                before = k
            return before

        before = lax.fori_loop(0, CHUNK // LOAD_UNROLL, load, before)
    ends[0] = fetch(kap_v, 0)
    ends[1] = before

    for step in range(1, ITERS + 1):
        for rows in inner_rows(step):
            def keep(i, value, step=step):
                if i == step and step <= 4:
                    old_l[step - 1] = value
                if i == ROWS - 1 - step:
                    old_r[step - 1] = value

            def put(i, value):
                f_ref[i] = value

            step_rows(rows, lambda i: f_ref[i], put, lambda a, i: c_ref[a, i], lambda i: cl_ref[i], keep)
    old_r[ITERS - 1] = f_ref[ROWS - 1 - ITERS]
    for copy in weights:
        copy.wait()


def hierarchize(rows, hy3, hz, out):
    planes = [rows_dot(hy3[...], row.reshape(NY, NZ)) for row in rows]
    out[...] = lanes_dot(jnp.concatenate(planes, axis=0), hz[...]).reshape(out.shape)


def edge_kernel(f_in, c_in, cl_in, old_l, old_r, ends, marks, hy3, hz, left, right, out, stay, f_new, c_new, cl_new, nodal):
    fresh = set()

    def take(i):
        return f_new[i + LEFT] if i in fresh or not 0 <= i < ROWS else f_in[i]

    def put(i, value):
        fresh.add(i)
        f_new[i + LEFT] = value

    def coef_at(a, i):
        return c_in[a, i] if 0 <= i < ROWS - 1 or (a and i == ROWS - 1) else c_new[a, i + LEFT]

    def first_y(i):
        return cl_in[i] if 0 <= i < ROWS else cl_new[i + LEFT]

    def prepare(source, first, count, edge_row, edge_k):
        before = None
        for t in range(count):
            i = first + t
            k = fetch(source, count + t)
            f_new[i + LEFT] = fetch(source, t)
            at = i + LEFT
            c_new[1, at], c_new[2, at], c_new[3, at], c_new[4, at], cl_new[at] = row_coefs(k)
            if before is not None:
                c_new[0, i - 1 + LEFT] = 0.5 * (before + k)
            if i == edge_row + 1:
                c_new[0, edge_row + LEFT] = 0.5 * (edge_k + k)
            if i == edge_row:
                c_new[0, edge_row + LEFT] = 0.5 * (edge_k + k)
            before = k

    prepare(left, -LEFT, LEFT, -1, ends[0])
    prepare(right, ROWS, RIGHT, ROWS - 1, ends[1])

    for step in range(1, ITERS + 1):
        reach = ITERS - step
        if step <= 4:
            lefts, rights = [range(-reach, step)], [range(ROWS - step, ROWS + reach + 1)]
        else:
            lefts = [range(-reach, reach + 1)]
            rights = [range(ROWS - step, ROWS - step + 1), range(ROWS - reach, ROWS + reach + 1)]

        def take_l(i, step=step):
            return old_l[step - 1] if i == step and step <= 4 else take(i)

        def take_r(i, step=step):
            return old_r[step - 1] if i == ROWS - 1 - step else take(i)

        for k in range(max(len(lefts), len(rights))):
            if k < len(lefts):
                step_rows(lefts[k], take_l, put, coef_at, first_y)
            if k < len(rights):
                step_rows(rights[k], take if k else take_r, put, coef_at, first_y)

    hierarchize([take(n * GAP) for n in range(NODES)], hy3, hz, nodal)
    finish(marks, nodal, out, stay)


def finish(marks, nodal, out, stay):
    swapped = marks[2 * len(BLOCKS)] > 0.5

    def planes_of(group):
        u = [nodal[n, group] for n in range(NODES)]
        outer = jnp.where(swapped, u[4], u[0])
        inner = jnp.where(swapped, u[0], u[4])
        return (
            outer,
            0.5 * (inner - outer),
            u[2] - 0.5 * (u[0] + u[4]),
            u[1] - 0.5 * (u[0] + u[2]),
            u[3] - 0.5 * (u[2] + u[4]),
        )

    cache = {}
    tiles = [jnp.zeros((8, 128), jnp.float32)] * TILES
    for b, (plane, group, source, width, tile, first) in enumerate(BLOCKS):
        if group not in cache:
            cache[group] = planes_of(group)
        value = marks[len(BLOCKS) + b] * cache[group][plane]
        tiles[tile] = tiles[tile] + shifted(value, first - source)
    for member in range(out.shape[0]):
        out[member] = tiles[0]
    for tile in range(1, TILES):
        stay[tile - 1] = tiles[tile]


def spread_kernel(marks, mine, other, dy3, dz, out, held, sem):
    swapped = marks[2 * len(BLOCKS), 0:1] > 0.5
    zero = jnp.zeros((8, 128), jnp.float32)
    planes = [[zero] * 8 for _ in range(5)]
    outer_other = [zero] * 8
    for b, (plane, group, source, width, tile, first) in enumerate(BLOCKS):

        def pick(value):
            return marks[b] * shifted(value, source - first)

        if plane == 1:
            planes[1][group] += pick(mine[tile] + other[tile])
        else:
            planes[plane][group] += pick(mine[tile])
        if plane == 0:
            outer_other[group] += pick(other[tile])
    wide = []
    outer = jnp.concatenate(planes[0], axis=0)
    middle = 0.5 * (outer + jnp.concatenate(outer_other, axis=0)) + jnp.concatenate(planes[1], axis=0)
    n0 = jnp.where(swapped, middle, outer)
    n4 = jnp.where(swapped, outer, middle)
    n2 = 0.5 * (n0 + n4) + jnp.concatenate(planes[2], axis=0)
    n1 = 0.5 * (n0 + n2) + jnp.concatenate(planes[3], axis=0)
    n3 = 0.5 * (n2 + n4) + jnp.concatenate(planes[4], axis=0)
    for n in (n0, n1, n2, n3, n4):
        wide.append(rows_dot(dy3[...], n))
    full = lanes_dot(jnp.concatenate(wide, axis=0), dz[...]).reshape(NODES, NY, NZ)
    copies = []
    for q in range(NODES - 1):
        slope = (full[q + 1] - full[q]) * (1.0 / GAP)
        for k in range(GAP):
            held[q * GAP + k] = full[q] + float(k) * slope
        at = pl.ds(q * GAP, GAP)
        copies.append(pltpu.make_async_copy(held.at[at], out.at[at], sem.at[q]))
        copies[-1].start()
    for copy in copies:
        copy.wait()


VMEM = pl.BlockSpec(memory_space=pltpu.VMEM)
SMEM = pl.BlockSpec(memory_space=pltpu.SMEM)
FAR = pl.BlockSpec(memory_space=pltpu.HBM)


def send_kernel(den, kap, up, down, sem):
    copies = [
        pltpu.make_async_copy(den.at[pl.ds(ROWS - LEFT, LEFT)], up.at[pl.ds(0, LEFT)], sem.at[0]),
        pltpu.make_async_copy(kap.at[pl.ds(ROWS - LEFT, LEFT)], up.at[pl.ds(LEFT, LEFT)], sem.at[1]),
        pltpu.make_async_copy(den.at[pl.ds(0, RIGHT)], down.at[pl.ds(0, RIGHT)], sem.at[2]),
        pltpu.make_async_copy(kap.at[pl.ds(0, RIGHT)], down.at[pl.ds(RIGHT, RIGHT)], sem.at[3]),
    ]
    for copy in copies:
        copy.start()
    for copy in copies:
        copy.wait()


def params(room=ROOM):
    return pltpu.CompilerParams(vmem_limit_bytes=room)


def rows_shape(*lead):
    return jax.ShapeDtypeStruct((*lead, 8, 8, 128), jnp.float32)


def far(x):
    return pltpu.with_memory_space_constraint(x, pltpu.HBM)


def send(den, kap, interpret=False):
    return pl.pallas_call(
        send_kernel,
        out_shape=(
            jax.ShapeDtypeStruct((2 * LEFT, NY, NZ), jnp.float32),
            jax.ShapeDtypeStruct((2 * RIGHT, NY, NZ), jnp.float32),
        ),
        in_specs=[FAR] * 2,
        out_specs=(VMEM, VMEM),
        scratch_shapes=[pltpu.SemaphoreType.DMA((4,))],
        compiler_params=params(8 * 1024 * 1024),
        interpret=interpret,
        name="send",
    )(far(den), far(kap))


def inner(levels, coefs, odd, den, kap, interpret=False):
    rows = rows_shape(ROWS)
    hy3, hz, _, _ = constants()
    return pl.pallas_call(
        inner_kernel,
        out_shape=(
            rows,
            rows_shape(5, ROWS),
            jax.ShapeDtypeStruct((ROWS, 8, 128), jnp.float32),
            rows_shape(4),
            rows_shape(ITERS),
            rows_shape(2),
            jax.ShapeDtypeStruct((2 * len(BLOCKS) + 1, 8, 128), jnp.float32),
            jax.ShapeDtypeStruct(hy3.shape, jnp.bfloat16),
            jax.ShapeDtypeStruct(hz.shape, jnp.bfloat16),
        ),
        in_specs=[SMEM] * 3 + [FAR] * 4,
        out_specs=(VMEM,) * 9,
        scratch_shapes=[pltpu.VMEM((ROWS, NY, NZ), jnp.float32)] * 2
        + [pltpu.SemaphoreType.DMA((2, ROWS // CHUNK)), pltpu.SemaphoreType.DMA((2,))],
        compiler_params=params(),
        cost_estimate=pl.CostEstimate(flops=20_000_000, bytes_accessed=8_000_000, transcendentals=0),
        interpret=interpret,
        name="inner",
    )(levels, coefs, odd, far(den), far(kap), far(jnp.asarray(hy3, jnp.bfloat16)), far(jnp.asarray(hz, jnp.bfloat16)))


def edge(members, state, left, right, interpret=False):
    return pl.pallas_call(
        edge_kernel,
        out_shape=(
            jax.ShapeDtypeStruct((members, 8, 128), jnp.float32),
            jax.ShapeDtypeStruct((TILES - 1, 8, 128), jnp.float32),
        ),
        in_specs=[VMEM] * 11,
        out_specs=(VMEM, VMEM),
        scratch_shapes=[
            pltpu.VMEM((TALL, 8, 8, 128), jnp.float32),
            pltpu.VMEM((5, TALL, 8, 8, 128), jnp.float32),
            pltpu.VMEM((TALL, 8, 128), jnp.float32),
            pltpu.VMEM((NODES, 8, 8, 128), jnp.float32),
        ],
        compiler_params=params(),
        interpret=interpret,
        name="edge",
    )(*state, left, right)


def spread(marks, mine, other, interpret=False):
    _, _, dy3, dz = constants()
    return pl.pallas_call(
        spread_kernel,
        out_shape=jax.ShapeDtypeStruct((ROWS, NY, NZ), jnp.float32),
        in_specs=[VMEM] * 5,
        out_specs=FAR,
        scratch_shapes=[pltpu.VMEM((ROWS, NY, NZ), jnp.float32), pltpu.SemaphoreType.DMA((NODES - 1,))],
        compiler_params=params(),
        interpret=interpret,
        name="spread",
    )(marks, mine, other, jnp.asarray(dy3, jnp.bfloat16), jnp.asarray(dz, jnp.bfloat16))


def local(density, kappa, levels, coefs):
    den, kap = density[0], kappa[0]
    space, grid = lax.axis_size("space"), lax.axis_size("grid")
    assert den.shape == (ROWS, NY, NZ) and space * ROWS == 512
    up = [(i, (i + 1) % space) for i in range(space)]
    down = [(j, i) for i, j in up]
    pair = [(i, i ^ 1) for i in range(space)]
    going_up, going_down = send(den, kap)
    left = lax.ppermute(going_up, "space", up)
    right = lax.ppermute(going_down, "space", down)
    odd = (lax.axis_index("space") % 2).astype(jnp.int32)[None]
    state = inner(levels, coefs, odd, den, kap)
    sent, stay = edge(grid, state, left, right)
    got = lax.all_to_all(sent, "grid", split_axis=0, concat_axis=0, tiled=True)
    mine = jnp.concatenate([jnp.sum(got, axis=0, keepdims=True), stay], axis=0)
    other = lax.ppermute(mine, "space", pair)
    return spread(state[6], mine, other)[None]


def solution(mesh):
    in_specs = (
        P("grid", "space", None, None),
        P("grid", "space", None, None),
        P("grid", None),
        P("grid"),
    )
    out_specs = P("grid", "space", None, None)
    return jax.shard_map(local, mesh=mesh, in_specs=in_specs, out_specs=out_specs, check_vma=False)
```

```python
import functools

import jax
import jax.numpy as jnp
import numpy as np
from jax import lax
from jax.experimental import pallas as pl
from jax.experimental.pallas import tpu as pltpu
from jax.sharding import PartitionSpec as P


ITERS = 8
LOW = 3
SPAN = 3
ROWS = 32
GAP = 8
NODES = ROWS // GAP + 1
LEFT = ITERS
RIGHT = ITERS + 1
TALL = LEFT + ROWS + RIGHT
LOAD_UNROLL = 4
CHUNK = 8
ROOM = 24 * 1024 * 1024
NY = 64
NZ = 128
TOP = 1 << (LOW + SPAN)


def level_order(count):
    step = count >> (LOW + SPAN)
    order = list(range(0, count, count >> LOW))
    for level in range(LOW + 1, LOW + SPAN + 1):
        gap = count >> level
        order += list(range(gap, count, 2 * gap))
    assert len(order) == TOP and all(i % step == 0 for i in order)
    return order


def tables(count):
    order = level_order(count)
    hier = np.eye(count)
    hats = np.eye(count)
    for index in range(1, count):
        gap = index & -index
        hier[index, (index - gap) % count] -= 0.5
        hier[index, (index + gap) % count] -= 0.5
    gap = count // 2
    while gap:
        for index in range(gap, count, 2 * gap):
            hats[index] += 0.5 * (hats[(index - gap) % count] + hats[(index + gap) % count])
        gap //= 2
    return hier[order], hats[:, order]


@functools.lru_cache(None)
def constants():
    hy, dy = tables(NY)
    hz, dz = tables(NZ)
    spread = [v + 8 * s for v in range(8) for s in range(8)]
    hy = hy[:, spread]
    hz_t = np.zeros((NZ, 128))
    hz_t[:, :TOP] = hz.T
    dz_t = np.zeros((128, NZ))
    dz_t[:TOP] = dz.T
    hy3 = np.concatenate([hy] * 3, axis=1)
    dy3 = np.concatenate([dy] * 3, axis=1)
    return tuple(np.asarray(m, np.float32) for m in (hy3, hz_t, dy3, dz_t))


def staircase():
    spare = {0: SPAN, 1: SPAN - 1, 2: SPAN - 2, 3: SPAN - 3, 4: SPAN - 3}
    summed, kept = [], []
    for plane, left in spare.items():
        for extra in range(left + 1):
            whole = 1 << (LOW + left - extra)
            half = whole // 2 if extra < left else 0
            groups = range(1 << (extra - 1), 1 << extra) if extra else range(1)
            for group in groups:
                if half:
                    summed.append((plane, group, 0, half))
                kept.append((plane, group, half, whole - half))
    blocks = []
    for base, pieces in ((0, summed), (1, kept)):
        place = 0
        for piece in pieces:
            assert place % 128 + piece[3] <= 128
            blocks.append((*piece, base + place // 128, place % 128))
            place += piece[3]
        assert base or place <= 128
    return blocks, 1 + max(b[4] for b in blocks)


BLOCKS, TILES = staircase()
NEED = (LOW, LOW + 1, LOW + 2, LOW + 3, LOW + 3)


def shifted(value, lanes):
    return pltpu.roll(value, lanes % 128, 1) if lanes % 128 else value


def parity():
    return lax.rem(lax.axis_index("space"), 2)


def split3(x):
    hi = x.astype(jnp.bfloat16)
    rest = x - hi.astype(jnp.float32)
    mid = rest.astype(jnp.bfloat16)
    lo = (rest - mid.astype(jnp.float32)).astype(jnp.bfloat16)
    return hi, mid, lo


def rows_dot(weights3, plane):
    stacked = jnp.concatenate(split3(plane), axis=0)
    return jnp.dot(weights3, stacked, preferred_element_type=jnp.float32)


def lanes_dot(planes, weights):
    total = None
    for piece in split3(planes):
        part = jnp.dot(piece, weights, preferred_element_type=jnp.float32)
        total = part if total is None else total + part
    return total


def next_z(row):
    return pltpu.roll(row, NZ - 1, 2)


def prev_z(row):
    return pltpu.roll(row, 1, 2)


def fetch(ref, index):
    row = ref.at[index]
    return jnp.stack([row[pl.ds(v, 8, 8), :] for v in range(8)], axis=0)


def row_coefs(k):
    ahead = jnp.concatenate([k[1:], pltpu.roll(k[0:1], 7, 1)], axis=0)
    behind = pltpu.roll(k[7:8], 1, 1)
    cz, czm = 0.5 * (k + next_z(k)), 0.5 * (k + prev_z(k))
    return 0.5 * (k + ahead), cz, czm, (1.0 - cz) - czm, 0.5 * (k[0] + behind[0])


def step_rows(rows, take, put, coef, first_y, keep=None):
    before, here = take(rows[0] - 1), take(rows[0])
    flux = coef(0, rows[0] - 1) * (here - before)
    for i in rows:
        after = take(i + 1)
        ahead, behind = pltpu.roll(here[0:1], 7, 1), pltpu.roll(here[7:8], 1, 1)
        flux_y = coef(1, i) * (jnp.concatenate([here[1:], ahead], axis=0) - here)
        flux_b = first_y(i) * (here[0] - behind[0])
        along_z = (coef(2, i) * next_z(here) + coef(3, i) * prev_z(here)) + coef(4, i) * here
        flux_x = coef(0, i) * (after - here)
        if keep is not None:
            keep(i, here)
        along_y = flux_y - jnp.concatenate([flux_b[None], flux_y[:7]], axis=0)
        put(i, along_z + ((flux_x - flux) + along_y))
        here, flux = after, flux_x


def inner_rows(step):
    reach = ITERS - step
    if 2 * reach + 1 >= GAP:
        return [range(step, ROWS - step)]
    spans = [range(n - reach, min(n + reach + 1, ROWS - step)) for n in range(GAP, ROWS, GAP)]
    return [r for r in spans if len(r)]


def write_marks(lev, coef, marks):
    level_x, level_y, level_z = lev[0, 0], lev[0, 1], lev[0, 2]
    weight = coef[0].astype(jnp.float32)
    lane = lax.broadcasted_iota(jnp.int32, (8, 128), 1)
    groups_y = lax.shift_left(1, level_y - LOW)
    width_z = lax.shift_left(1, level_z)
    for b, (plane, group, source, width, _, _) in enumerate(BLOCKS):
        keep = (lane >= source) & (lane < jnp.minimum(width_z, source + width)) & (group < groups_y) & (level_x >= NEED[plane])
        kept = jnp.where(keep, 1.0, 0.0)
        marks[b] = kept
        marks[len(BLOCKS) + b] = weight * kept
    marks[2 * len(BLOCKS)] = jnp.full((8, 128), parity() * 1.0, jnp.float32)


def inner_kernel(lev_h, coef, den, kap, hy3, hz, f_ref, c_ref, cl_ref, old_l, old_r, ends, marks, hy3_v, hz_v, den_v, kap_v, lev, sem, sem_w):
    parts = ROWS // CHUNK

    def copies(part):
        at = pl.ds(part * CHUNK, CHUNK)
        return (
            pltpu.make_async_copy(kap.at[at], kap_v.at[at], sem.at[0, part]),
            pltpu.make_async_copy(den.at[at], den_v.at[at], sem.at[1, part]),
        )

    for part in range(parts):
        for copy in copies(part):
            copy.start()
    weights = [pltpu.make_async_copy(hy3, hy3_v, sem_w.at[0]), pltpu.make_async_copy(hz, hz_v, sem_w.at[1])]
    scalars = [pltpu.make_async_copy(lev_h, lev, sem_w.at[2])]
    for copy in weights + scalars:
        copy.start()
    before = jnp.zeros((8, 8, 128), jnp.float32)
    for part in range(parts):
        for copy in copies(part):
            copy.wait()

        def load(t, before):
            for u in range(LOAD_UNROLL):
                i = part * CHUNK + t * LOAD_UNROLL + u
                k = fetch(kap_v, i)
                f_ref[i] = fetch(den_v, i)
                c_ref[0, jnp.maximum(i - 1, 0)] = 0.5 * (before + k)
                c_ref[1, i], c_ref[2, i], c_ref[3, i], c_ref[4, i], cl_ref[i] = row_coefs(k)
                before = k
            return before

        before = lax.fori_loop(0, CHUNK // LOAD_UNROLL, load, before)
    ends[0] = fetch(kap_v, 0)
    ends[1] = before

    for step in range(1, ITERS + 1):
        for rows in inner_rows(step):
            def keep(i, value, step=step):
                if i == step and step <= 4:
                    old_l[step - 1] = value
                if i == ROWS - 1 - step:
                    old_r[step - 1] = value

            def put(i, value):
                f_ref[i] = value

            step_rows(rows, lambda i: f_ref[i], put, lambda a, i: c_ref[a, i], lambda i: cl_ref[i], keep)
    old_r[ITERS - 1] = f_ref[ROWS - 1 - ITERS]
    for copy in scalars:
        copy.wait()
    write_marks(lev, coef, marks)
    for copy in weights:
        copy.wait()


def hierarchize(rows, hy3, hz, out):
    planes = [rows_dot(hy3[...], row.reshape(NY, NZ)) for row in rows]
    out[...] = lanes_dot(jnp.concatenate(planes, axis=0), hz[...]).reshape(out.shape)


def one_end(is_left, state, halo, f_new, c_new, cl_new):
    f_in, c_in, cl_in, old_l, old_r, ends = state
    fresh = set()

    def take(i):
        return f_new[i + LEFT] if i in fresh or not 0 <= i < ROWS else f_in[i]

    def put(i, value):
        fresh.add(i)
        f_new[i + LEFT] = value

    def coef_at(a, i):
        return c_in[a, i] if 0 <= i < ROWS - 1 or (a and i == ROWS - 1) else c_new[a, i + LEFT]

    def first_y(i):
        return cl_in[i] if 0 <= i < ROWS else cl_new[i + LEFT]

    skip = RIGHT - LEFT if is_left else 0
    first, count = (-LEFT, LEFT) if is_left else (ROWS, RIGHT)
    before = None if is_left else ends[1]
    for t in range(count):
        at = first + t + LEFT
        k = fetch(halo, RIGHT + skip + t)
        f_new[at] = fetch(halo, skip + t)
        c_new[1, at], c_new[2, at], c_new[3, at], c_new[4, at], cl_new[at] = row_coefs(k)
        if before is not None:
            c_new[0, at - 1] = 0.5 * (before + k)
        before = k
    if is_left:
        c_new[0, LEFT - 1] = 0.5 * (before + ends[0])

    for step in range(1, ITERS + 1):
        reach = ITERS - step
        if is_left:
            spans = [range(-reach, step if step <= 4 else reach + 1)]
        elif step <= 4:
            spans = [range(ROWS - step, ROWS + reach + 1)]
        else:
            spans = [range(ROWS - step, ROWS - step + 1), range(ROWS - reach, ROWS + reach + 1)]

        def take_old(i, step=step):
            if is_left:
                return old_l[step - 1] if i == step and step <= 4 else take(i)
            return old_r[step - 1] if i == ROWS - 1 - step else take(i)

        for n, rows in enumerate(spans):
            step_rows(rows, take if n else take_old, put, coef_at, first_y)
    return take


def chip_kernel(*refs):
    state, halo, out, work = refs[:6], refs[6], refs[7], refs[8:]

    @pl.when(parity() == 0)
    def _():
        take = one_end(False, state, halo, *work)
        out[0] = take(3 * GAP)
        out[1] = take(4 * GAP)

    @pl.when(parity() == 1)
    def _():
        out[0] = one_end(True, state, halo, *work)(0)


def cross_kernel(*refs):
    state, (marks, hy3, hz, near, halo, out, stay), work, nodes, nodal = refs[:6], refs[6:13], refs[13:16], refs[16], refs[17]
    for n in (1, 2):
        nodes[n] = state[0][n * GAP]

    @pl.when(parity() == 0)
    def _():
        nodes[0] = one_end(True, state, halo, *work)(0)
        nodes[3] = near[0]
        nodes[4] = near[1]

    @pl.when(parity() == 1)
    def _():
        take = one_end(False, state, halo, *work)
        nodes[0] = near[0]
        nodes[3] = take(3 * GAP)
        nodes[4] = take(4 * GAP)

    hierarchize([nodes[n] for n in range(NODES)], hy3, hz, nodal)
    finish(marks, nodal, out, stay)


def finish(marks, nodal, out, stay):
    swapped = marks[2 * len(BLOCKS)] > 0.5

    def planes_of(group):
        u = [nodal[n, group] for n in range(NODES)]
        outer = jnp.where(swapped, u[4], u[0])
        inner = jnp.where(swapped, u[0], u[4])
        return (
            outer,
            0.5 * (inner - outer),
            u[2] - 0.5 * (u[0] + u[4]),
            u[1] - 0.5 * (u[0] + u[2]),
            u[3] - 0.5 * (u[2] + u[4]),
        )

    cache = {}
    tiles = [jnp.zeros((8, 128), jnp.float32)] * TILES
    for b, (plane, group, source, width, tile, first) in enumerate(BLOCKS):
        if group not in cache:
            cache[group] = planes_of(group)
        value = marks[len(BLOCKS) + b] * cache[group][plane]
        tiles[tile] = tiles[tile] + shifted(value, first - source)
    for member in range(out.shape[0]):
        out[member] = tiles[0]
    for tile in range(1, TILES):
        stay[tile - 1] = tiles[tile]


def spread_kernel(marks, mine, other, dy3, dz, out, held, sem):
    swapped = marks[2 * len(BLOCKS), 0:1] > 0.5
    zero = jnp.zeros((8, 128), jnp.float32)
    planes = [[zero] * 8 for _ in range(5)]
    outer_other = [zero] * 8
    for b, (plane, group, source, width, tile, first) in enumerate(BLOCKS):

        def pick(value):
            return marks[b] * shifted(value, source - first)

        if plane == 1:
            planes[1][group] += pick(mine[tile] + other[tile])
        else:
            planes[plane][group] += pick(mine[tile])
        if plane == 0:
            outer_other[group] += pick(other[tile])
    wide = []
    outer = jnp.concatenate(planes[0], axis=0)
    middle = 0.5 * (outer + jnp.concatenate(outer_other, axis=0)) + jnp.concatenate(planes[1], axis=0)
    n0 = jnp.where(swapped, middle, outer)
    n4 = jnp.where(swapped, outer, middle)
    n2 = 0.5 * (n0 + n4) + jnp.concatenate(planes[2], axis=0)
    n1 = 0.5 * (n0 + n2) + jnp.concatenate(planes[3], axis=0)
    n3 = 0.5 * (n2 + n4) + jnp.concatenate(planes[4], axis=0)
    for n in (n0, n1, n2, n3, n4):
        wide.append(rows_dot(dy3[...], n))
    full = lanes_dot(jnp.concatenate(wide, axis=0), dz[...]).reshape(NODES, NY, NZ)
    copies = []
    for q in range(NODES - 1):
        slope = (full[q + 1] - full[q]) * (1.0 / GAP)
        for k in range(GAP):
            held[q * GAP + k] = full[q] + float(k) * slope
        at = pl.ds(q * GAP, GAP)
        copies.append(pltpu.make_async_copy(held.at[at], out.at[at], sem.at[q]))
        copies[-1].start()
    for copy in copies:
        copy.wait()


VMEM = pl.BlockSpec(memory_space=pltpu.VMEM)
SMEM = pl.BlockSpec(memory_space=pltpu.SMEM)
FAR = pl.BlockSpec(memory_space=pltpu.HBM)


def send_kernel(den, kap, cross, chip, sem):
    low = (ROWS - RIGHT) * parity()
    copies = []
    for n, (out, start) in enumerate(((cross, low), (chip, ROWS - RIGHT - low))):
        for m, source in enumerate((den, kap)):
            copies.append(
                pltpu.make_async_copy(source.at[pl.ds(start, RIGHT)], out.at[pl.ds(m * RIGHT, RIGHT)], sem.at[n, m])
            )
    for copy in copies:
        copy.start()
    for copy in copies:
        copy.wait()


def params(room=ROOM):
    return pltpu.CompilerParams(vmem_limit_bytes=room)


def rows_shape(*lead):
    return jax.ShapeDtypeStruct((*lead, 8, 8, 128), jnp.float32)


def far(x):
    return pltpu.with_memory_space_constraint(x, pltpu.HBM)


def send(den, kap, interpret=False):
    return pl.pallas_call(
        send_kernel,
        out_shape=(
            jax.ShapeDtypeStruct((2 * RIGHT, NY, NZ), jnp.float32),
            jax.ShapeDtypeStruct((2 * RIGHT, NY, NZ), jnp.float32),
        ),
        in_specs=[FAR] * 2,
        out_specs=(VMEM, VMEM),
        scratch_shapes=[pltpu.SemaphoreType.DMA((2, 2))],
        compiler_params=params(8 * 1024 * 1024),
        interpret=interpret,
        name="send",
    )(far(den), far(kap))


def inner(levels, coefs, den, kap, interpret=False):
    rows = rows_shape(ROWS)
    hy3, hz, _, _ = constants()
    return pl.pallas_call(
        inner_kernel,
        out_shape=(
            rows,
            rows_shape(5, ROWS),
            jax.ShapeDtypeStruct((ROWS, 8, 128), jnp.float32),
            rows_shape(4),
            rows_shape(ITERS),
            rows_shape(2),
            jax.ShapeDtypeStruct((2 * len(BLOCKS) + 1, 8, 128), jnp.float32),
            jax.ShapeDtypeStruct(hy3.shape, jnp.bfloat16),
            jax.ShapeDtypeStruct(hz.shape, jnp.bfloat16),
        ),
        in_specs=[FAR, SMEM] + [FAR] * 4,
        out_specs=(VMEM,) * 9,
        scratch_shapes=[pltpu.VMEM((ROWS, NY, NZ), jnp.float32)] * 2
        + [
            pltpu.SMEM((1, 3), jnp.int32),
            pltpu.SemaphoreType.DMA((2, ROWS // CHUNK)),
            pltpu.SemaphoreType.DMA((3,)),
        ],
        compiler_params=params(),
        cost_estimate=pl.CostEstimate(flops=20_000_000, bytes_accessed=8_000_000, transcendentals=0),
        interpret=interpret,
        name="inner",
    )(far(levels), coefs, far(den), far(kap), far(jnp.asarray(hy3, jnp.bfloat16)), far(jnp.asarray(hz, jnp.bfloat16)))


def work():
    return [
        pltpu.VMEM((TALL, 8, 8, 128), jnp.float32),
        pltpu.VMEM((5, TALL, 8, 8, 128), jnp.float32),
        pltpu.VMEM((TALL, 8, 128), jnp.float32),
    ]


def chip_end(state, halo, interpret=False):
    return pl.pallas_call(
        chip_kernel,
        out_shape=rows_shape(2),
        in_specs=[VMEM] * 7,
        out_specs=VMEM,
        scratch_shapes=work(),
        compiler_params=params(),
        cost_estimate=pl.CostEstimate(flops=10_000_000, bytes_accessed=4_000_000, transcendentals=0),
        interpret=interpret,
        name="chip_end",
    )(*state[:6], halo)


def cross_end(members, state, near, halo, interpret=False):
    return pl.pallas_call(
        cross_kernel,
        out_shape=(
            jax.ShapeDtypeStruct((members, 8, 128), jnp.float32),
            jax.ShapeDtypeStruct((TILES - 1, 8, 128), jnp.float32),
        ),
        in_specs=[VMEM] * 11,
        out_specs=(VMEM, VMEM),
        scratch_shapes=work() + [pltpu.VMEM((NODES, 8, 8, 128), jnp.float32)] * 2,
        compiler_params=params(),
        interpret=interpret,
        name="cross_end",
    )(*state, near, halo)


def spread(marks, mine, other, interpret=False):
    _, _, dy3, dz = constants()
    return pl.pallas_call(
        spread_kernel,
        out_shape=jax.ShapeDtypeStruct((ROWS, NY, NZ), jnp.float32),
        in_specs=[VMEM] * 5,
        out_specs=FAR,
        scratch_shapes=[pltpu.VMEM((ROWS, NY, NZ), jnp.float32), pltpu.SemaphoreType.DMA((NODES - 1,))],
        compiler_params=params(),
        interpret=interpret,
        name="spread",
    )(marks, mine, other, jnp.asarray(dy3, jnp.bfloat16), jnp.asarray(dz, jnp.bfloat16))


def local(density, kappa, levels, coefs):
    den, kap = density[0], kappa[0]
    space, grid = lax.axis_size("space"), lax.axis_size("grid")
    assert den.shape == (ROWS, NY, NZ) and space * ROWS == 512
    pair = [(i, i ^ 1) for i in range(space)]
    other_chip = [(i, (i + 1 if i % 2 else i - 1) % space) for i in range(space)]
    to_cross, to_chip = send(den, kap)
    cross = lax.ppermute(to_cross, "space", other_chip)
    chip = lax.ppermute(to_chip, "space", pair)
    state = inner(levels, coefs, den, kap)
    near = chip_end(state, chip)
    sent, stay = cross_end(grid, state, near, cross)
    got = lax.all_to_all(sent, "grid", split_axis=0, concat_axis=0, tiled=True)
    mine = jnp.concatenate([jnp.sum(got, axis=0, keepdims=True), stay], axis=0)
    other = lax.ppermute(mine, "space", pair)
    return spread(state[6], mine, other)[None]


def solution(mesh):
    in_specs = (
        P("grid", "space", None, None),
        P("grid", "space", None, None),
        P("grid", None),
        P("grid"),
    )
    out_specs = P("grid", "space", None, None)
    return jax.shard_map(local, mesh=mesh, in_specs=in_specs, out_specs=out_specs, check_vma=False)
```

```python
import functools

import jax
import jax.numpy as jnp
import numpy as np
from jax import lax
from jax.experimental import pallas as pl
from jax.experimental.pallas import tpu as pltpu
from jax.sharding import PartitionSpec as P


ITERS = 8
LOW = 3
SPAN = 3
ROWS = 32
GAP = 8
NODES = ROWS // GAP + 1
LEFT = ITERS
RIGHT = ITERS + 1
TALL = LEFT + ROWS + RIGHT
CHUNK = 8
ROOM = 24 * 1024 * 1024
NY = 64
NZ = 128
TOP = 1 << (LOW + SPAN)


def level_order(count):
    step = count >> (LOW + SPAN)
    order = list(range(0, count, count >> LOW))
    for level in range(LOW + 1, LOW + SPAN + 1):
        gap = count >> level
        order += list(range(gap, count, 2 * gap))
    assert len(order) == TOP and all(i % step == 0 for i in order)
    return order


def tables(count):
    order = level_order(count)
    hier = np.eye(count)
    hats = np.eye(count)
    for index in range(1, count):
        gap = index & -index
        hier[index, (index - gap) % count] -= 0.5
        hier[index, (index + gap) % count] -= 0.5
    gap = count // 2
    while gap:
        for index in range(gap, count, 2 * gap):
            hats[index] += 0.5 * (hats[(index - gap) % count] + hats[(index + gap) % count])
        gap //= 2
    return hier[order], hats[:, order]


@functools.lru_cache(None)
def constants():
    hy, dy = tables(NY)
    hz, dz = tables(NZ)
    spread = [v + 8 * s for v in range(8) for s in range(8)]
    hy = hy[:, spread]
    hz_t = np.zeros((NZ, 128))
    hz_t[:, :TOP] = hz.T
    dz_t = np.zeros((128, NZ))
    dz_t[:TOP] = dz.T
    hy3 = np.concatenate([hy] * 3, axis=1)
    dy3 = np.concatenate([dy] * 3, axis=1)
    return tuple(np.asarray(m, np.float32) for m in (hy3, hz_t, dy3, dz_t))


def staircase():
    spare = {0: SPAN, 1: SPAN - 1, 2: SPAN - 2, 3: SPAN - 3, 4: SPAN - 3}
    summed, kept = [], []
    for plane, left in spare.items():
        for extra in range(left + 1):
            whole = 1 << (LOW + left - extra)
            half = whole // 2 if extra < left else 0
            groups = range(1 << (extra - 1), 1 << extra) if extra else range(1)
            for group in groups:
                if half:
                    summed.append((plane, group, 0, half))
                kept.append((plane, group, half, whole - half))
    blocks = []
    for base, pieces in ((0, summed), (1, kept)):
        place = 0
        for piece in pieces:
            assert place % 128 + piece[3] <= 128
            blocks.append((*piece, base + place // 128, place % 128))
            place += piece[3]
        assert base or place <= 128
    return blocks, 1 + max(b[4] for b in blocks)


BLOCKS, TILES = staircase()
NEED = (LOW, LOW + 1, LOW + 2, LOW + 3, LOW + 3)


def shifted(value, lanes):
    return pltpu.roll(value, lanes % 128, 1) if lanes % 128 else value


def parity():
    return lax.rem(lax.axis_index("space"), 2)


def split3(x):
    hi = x.astype(jnp.bfloat16)
    rest = x - hi.astype(jnp.float32)
    mid = rest.astype(jnp.bfloat16)
    lo = (rest - mid.astype(jnp.float32)).astype(jnp.bfloat16)
    return hi, mid, lo


def rows_dot(weights3, plane):
    stacked = jnp.concatenate(split3(plane), axis=0)
    return jnp.dot(weights3, stacked, preferred_element_type=jnp.float32)


def lanes_dot(planes, weights):
    total = None
    for piece in split3(planes):
        part = jnp.dot(piece, weights, preferred_element_type=jnp.float32)
        total = part if total is None else total + part
    return total


def next_z(row):
    return pltpu.roll(row, NZ - 1, 2)


def prev_z(row):
    return pltpu.roll(row, 1, 2)


def fetch(ref, index):
    row = ref.at[index]
    return jnp.stack([row[pl.ds(v, 8, 8), :] for v in range(8)], axis=0)


def row_coefs(k):
    ahead = jnp.concatenate([k[1:], pltpu.roll(k[0:1], 7, 1)], axis=0)
    behind = pltpu.roll(k[7:8], 1, 1)
    cz, czm = 0.5 * (k + next_z(k)), 0.5 * (k + prev_z(k))
    return 0.5 * (k + ahead), cz, czm, (1.0 - cz) - czm, 0.5 * (k[0] + behind[0])


def step_rows(rows, take, put, coef, first_y, keep=None):
    before, here = take(rows[0] - 1), take(rows[0])
    flux = coef(0, rows[0] - 1) * (here - before)
    for i in rows:
        after = take(i + 1)
        ahead, behind = pltpu.roll(here[0:1], 7, 1), pltpu.roll(here[7:8], 1, 1)
        flux_y = coef(1, i) * (jnp.concatenate([here[1:], ahead], axis=0) - here)
        flux_b = first_y(i) * (here[0] - behind[0])
        along_z = (coef(2, i) * next_z(here) + coef(3, i) * prev_z(here)) + coef(4, i) * here
        flux_x = coef(0, i) * (after - here)
        if keep is not None:
            keep(i, here)
        along_y = flux_y - jnp.concatenate([flux_b[None], flux_y[:7]], axis=0)
        put(i, along_z + ((flux_x - flux) + along_y))
        here, flux = after, flux_x


def inner_rows(step):
    reach = ITERS - step
    if 2 * reach + 1 >= GAP:
        return [range(step, ROWS - step)]
    spans = [range(n - reach, min(n + reach + 1, ROWS - step)) for n in range(GAP, ROWS, GAP)]
    return [r for r in spans if len(r)]


def write_marks(lev, marks):
    level_x, level_y, level_z = lev[0, 0], lev[0, 1], lev[0, 2]
    lane = lax.broadcasted_iota(jnp.int32, (8, 128), 1)
    groups_y = lax.shift_left(1, level_y - LOW)
    width_z = lax.shift_left(1, level_z)
    for b, (plane, group, source, width, _, _) in enumerate(BLOCKS):
        keep = (lane >= source) & (lane < jnp.minimum(width_z, source + width)) & (group < groups_y) & (level_x >= NEED[plane])
        marks[b] = jnp.where(keep, 1.0, 0.0)
    marks[len(BLOCKS)] = jnp.full((8, 128), parity() * 1.0, jnp.float32)


def inner_kernel(lev_h, den, kap, hy3, hz, f_ref, c_ref, cl_ref, old_l, old_r, ends, marks, hy3_v, hz_v, den_v, kap_v, lev, sem, sem_w):
    parts = ROWS // CHUNK

    def copies(part):
        at = pl.ds(part * CHUNK, CHUNK)
        return (
            pltpu.make_async_copy(kap.at[at], kap_v.at[at], sem.at[0, part]),
            pltpu.make_async_copy(den.at[at], den_v.at[at], sem.at[1, part]),
        )

    for part in range(parts):
        for copy in copies(part):
            copy.start()
    weights = [pltpu.make_async_copy(hy3, hy3_v, sem_w.at[0]), pltpu.make_async_copy(hz, hz_v, sem_w.at[1])]
    scalars = [pltpu.make_async_copy(lev_h, lev, sem_w.at[2])]
    for copy in scalars + weights:
        copy.start()
    for copy in scalars:
        copy.wait()
    write_marks(lev, marks)
    for part in range(parts):
        for copy in copies(part):
            copy.wait()

        @pl.when(parity() < 2)
        def _(part=part):
            before = fetch(kap_v, part * CHUNK - 1) if part else None
            for i in range(part * CHUNK, part * CHUNK + CHUNK):
                k = fetch(kap_v, i)
                f_ref[i] = fetch(den_v, i)
                if before is not None:
                    c_ref[0, i - 1] = 0.5 * (before + k)
                c_ref[1, i], c_ref[2, i], c_ref[3, i], c_ref[4, i], cl_ref[i] = row_coefs(k)
                before = k

    ends[0] = fetch(kap_v, 0)
    ends[1] = fetch(kap_v, ROWS - 1)

    for step in range(1, ITERS + 1):
        for rows in inner_rows(step):
            def keep(i, value, step=step):
                if i == step and step <= 4:
                    old_l[step - 1] = value
                if i == ROWS - 1 - step:
                    old_r[step - 1] = value

            def put(i, value):
                f_ref[i] = value

            step_rows(rows, lambda i: f_ref[i], put, lambda a, i: c_ref[a, i], lambda i: cl_ref[i], keep)
    old_r[ITERS - 1] = f_ref[ROWS - 1 - ITERS]
    for copy in weights:
        copy.wait()


def hierarchize(rows, hy3, hz, out):
    planes = [rows_dot(hy3[...], row.reshape(NY, NZ)) for row in rows]
    out[...] = lanes_dot(jnp.concatenate(planes, axis=0), hz[...]).reshape(out.shape)


def read_end(is_left, state, halo, f_new, c_new, cl_new):
    ends = state[5]
    skip = RIGHT - LEFT if is_left else 0
    first, count = (-LEFT, LEFT) if is_left else (ROWS, RIGHT)
    before = None if is_left else ends[1]
    for t in range(count):
        at = first + t + LEFT
        k = fetch(halo, RIGHT + skip + t)
        f_new[at] = fetch(halo, skip + t)
        c_new[1, at], c_new[2, at], c_new[3, at], c_new[4, at], cl_new[at] = row_coefs(k)
        if before is not None:
            c_new[0, at - 1] = 0.5 * (before + k)
        before = k
    if is_left:
        c_new[0, LEFT - 1] = 0.5 * (before + ends[0])


def one_end(is_left, state, halo, f_new, c_new, cl_new):
    read_end(is_left, state, halo, f_new, c_new, cl_new)
    f_in, c_in, cl_in, old_l, old_r, _ = state
    fresh = set()

    def take(i):
        return f_new[i + LEFT] if i in fresh or not 0 <= i < ROWS else f_in[i]

    def put(i, value):
        fresh.add(i)
        f_new[i + LEFT] = value

    def coef_at(a, i):
        return c_in[a, i] if 0 <= i < ROWS - 1 or (a and i == ROWS - 1) else c_new[a, i + LEFT]

    def first_y(i):
        return cl_in[i] if 0 <= i < ROWS else cl_new[i + LEFT]

    for step in range(1, ITERS + 1):
        reach = ITERS - step
        if is_left:
            spans = [range(-reach, step if step <= 4 else reach + 1)]
        elif step <= 4:
            spans = [range(ROWS - step, ROWS + reach + 1)]
        else:
            spans = [range(ROWS - step, ROWS - step + 1), range(ROWS - reach, ROWS + reach + 1)]

        def take_old(i, step=step):
            if is_left:
                return old_l[step - 1] if i == step and step <= 4 else take(i)
            return old_r[step - 1] if i == ROWS - 1 - step else take(i)

        for n, rows in enumerate(spans):
            step_rows(rows, take if n else take_old, put, coef_at, first_y)
    return take


def chip_kernel(*refs):
    state, halo, out, work = refs[:6], refs[6], refs[7], refs[8:]

    @pl.when(parity() == 0)
    def _():
        take = one_end(False, state, halo, *work)
        out[0] = take(3 * GAP)
        out[1] = take(4 * GAP)

    @pl.when(parity() == 1)
    def _():
        out[0] = one_end(True, state, halo, *work)(0)


def cross_kernel(*refs):
    state, (marks, hy3, hz, near, halo, coef, out, stay) = refs[:6], refs[6:14]
    work, nodes, nodal = refs[14:17], refs[17], refs[18]
    for n in (1, 2):
        nodes[n] = state[0][n * GAP]

    @pl.when(parity() == 0)
    def _():
        nodes[0] = one_end(True, state, halo, *work)(0)
        nodes[3] = near[0]
        nodes[4] = near[1]

    @pl.when(parity() == 1)
    def _():
        take = one_end(False, state, halo, *work)
        nodes[0] = near[0]
        nodes[3] = take(3 * GAP)
        nodes[4] = take(4 * GAP)

    hierarchize([nodes[n] for n in range(NODES)], hy3, hz, nodal)
    finish(coef, marks, nodal, out, stay)


def finish(coef, marks, nodal, out, stay):
    swapped = marks[len(BLOCKS)] > 0.5

    def planes_of(group):
        u = [nodal[n, group] for n in range(NODES)]
        outer = jnp.where(swapped, u[4], u[0])
        inner = jnp.where(swapped, u[0], u[4])
        return (
            outer,
            0.5 * (inner - outer),
            u[2] - 0.5 * (u[0] + u[4]),
            u[1] - 0.5 * (u[0] + u[2]),
            u[3] - 0.5 * (u[2] + u[4]),
        )

    cache = {}
    tiles = [jnp.zeros((8, 128), jnp.float32)] * TILES
    for b, (plane, group, source, width, tile, first) in enumerate(BLOCKS):
        if group not in cache:
            cache[group] = planes_of(group)
        value = marks[b] * cache[group][plane]
        tiles[tile] = tiles[tile] + shifted(value, first - source)
    weight = jnp.broadcast_to(coef[...].astype(jnp.float32), (8, 128))
    tiles = [weight * tile for tile in tiles]
    for member in range(out.shape[0]):
        out[member] = tiles[0]
    for tile in range(1, TILES):
        stay[tile - 1] = tiles[tile]


def spread_kernel(marks, mine, other, dy3, dz, out, held, sem):
    swapped = marks[len(BLOCKS), 0:1] > 0.5
    zero = jnp.zeros((8, 128), jnp.float32)
    planes = [[zero] * 8 for _ in range(5)]
    outer_other = [zero] * 8
    for b, (plane, group, source, width, tile, first) in enumerate(BLOCKS):

        def pick(value):
            return marks[b] * shifted(value, source - first)

        if plane == 1:
            planes[1][group] += pick(mine[tile] + other[tile])
        else:
            planes[plane][group] += pick(mine[tile])
        if plane == 0:
            outer_other[group] += pick(other[tile])
    wide = []
    outer = jnp.concatenate(planes[0], axis=0)
    middle = 0.5 * (outer + jnp.concatenate(outer_other, axis=0)) + jnp.concatenate(planes[1], axis=0)
    n0 = jnp.where(swapped, middle, outer)
    n4 = jnp.where(swapped, outer, middle)
    n2 = 0.5 * (n0 + n4) + jnp.concatenate(planes[2], axis=0)
    n1 = 0.5 * (n0 + n2) + jnp.concatenate(planes[3], axis=0)
    n3 = 0.5 * (n2 + n4) + jnp.concatenate(planes[4], axis=0)
    for n in (n0, n1, n2, n3, n4):
        wide.append(rows_dot(dy3[...], n))
    full = lanes_dot(jnp.concatenate(wide, axis=0), dz[...]).reshape(NODES, NY, NZ)
    copies = []
    for q in range(NODES - 1):
        slope = (full[q + 1] - full[q]) * (1.0 / GAP)
        for k in range(GAP):
            held[q * GAP + k] = full[q] + float(k) * slope
        at = pl.ds(q * GAP, GAP)
        copies.append(pltpu.make_async_copy(held.at[at], out.at[at], sem.at[q]))
        copies[-1].start()
    for copy in copies:
        copy.wait()


VMEM = pl.BlockSpec(memory_space=pltpu.VMEM)
SMEM = pl.BlockSpec(memory_space=pltpu.SMEM)
FAR = pl.BlockSpec(memory_space=pltpu.HBM)


def send_kernel(den, kap, cross, chip, sem):
    low = (ROWS - RIGHT) * parity()
    copies = []
    for n, (out, start) in enumerate(((cross, low), (chip, ROWS - RIGHT - low))):
        for m, source in enumerate((den, kap)):
            copies.append(
                pltpu.make_async_copy(source.at[pl.ds(start, RIGHT)], out.at[pl.ds(m * RIGHT, RIGHT)], sem.at[n, m])
            )
    for copy in copies:
        copy.start()
    for copy in copies:
        copy.wait()


def params(room=ROOM):
    return pltpu.CompilerParams(vmem_limit_bytes=room)


def rows_shape(*lead):
    return jax.ShapeDtypeStruct((*lead, 8, 8, 128), jnp.float32)


def far(x):
    return pltpu.with_memory_space_constraint(x, pltpu.HBM)


def send(den, kap, interpret=False):
    return pl.pallas_call(
        send_kernel,
        out_shape=(
            jax.ShapeDtypeStruct((2 * RIGHT, NY, NZ), jnp.float32),
            jax.ShapeDtypeStruct((2 * RIGHT, NY, NZ), jnp.float32),
        ),
        in_specs=[FAR] * 2,
        out_specs=(VMEM, VMEM),
        scratch_shapes=[pltpu.SemaphoreType.DMA((2, 2))],
        compiler_params=params(8 * 1024 * 1024),
        interpret=interpret,
        name="send",
    )(far(den), far(kap))


def inner(levels, den, kap, interpret=False):
    rows = rows_shape(ROWS)
    hy3, hz, _, _ = constants()
    return pl.pallas_call(
        inner_kernel,
        out_shape=(
            rows,
            rows_shape(5, ROWS),
            jax.ShapeDtypeStruct((ROWS, 8, 128), jnp.float32),
            rows_shape(4),
            rows_shape(ITERS),
            rows_shape(2),
            jax.ShapeDtypeStruct((len(BLOCKS) + 1, 8, 128), jnp.float32),
            jax.ShapeDtypeStruct(hy3.shape, jnp.bfloat16),
            jax.ShapeDtypeStruct(hz.shape, jnp.bfloat16),
        ),
        in_specs=[FAR] * 5,
        out_specs=(VMEM,) * 9,
        scratch_shapes=[pltpu.VMEM((ROWS, NY, NZ), jnp.float32)] * 2
        + [
            pltpu.SMEM((1, 3), jnp.int32),
            pltpu.SemaphoreType.DMA((2, ROWS // CHUNK)),
            pltpu.SemaphoreType.DMA((3,)),
        ],
        compiler_params=params(),
        cost_estimate=pl.CostEstimate(flops=20_000_000, bytes_accessed=8_000_000, transcendentals=0),
        interpret=interpret,
        name="inner",
    )(far(levels), far(den), far(kap), far(jnp.asarray(hy3, jnp.bfloat16)), far(jnp.asarray(hz, jnp.bfloat16)))


def work():
    return [
        pltpu.VMEM((TALL, 8, 8, 128), jnp.float32),
        pltpu.VMEM((5, TALL, 8, 8, 128), jnp.float32),
        pltpu.VMEM((TALL, 8, 128), jnp.float32),
    ]


def chip_end(state, halo, interpret=False):
    return pl.pallas_call(
        chip_kernel,
        out_shape=rows_shape(2),
        in_specs=[VMEM] * 7,
        out_specs=VMEM,
        scratch_shapes=work(),
        compiler_params=params(),
        cost_estimate=pl.CostEstimate(flops=10_000_000, bytes_accessed=4_000_000, transcendentals=0),
        interpret=interpret,
        name="chip_end",
    )(*state[:6], halo)


def cross_end(members, coefs, state, near, halo, interpret=False):
    return pl.pallas_call(
        cross_kernel,
        out_shape=(
            jax.ShapeDtypeStruct((members, 8, 128), jnp.float32),
            jax.ShapeDtypeStruct((TILES - 1, 8, 128), jnp.float32),
        ),
        in_specs=[VMEM] * 12,
        out_specs=(VMEM, VMEM),
        scratch_shapes=work() + [pltpu.VMEM((NODES, 8, 8, 128), jnp.float32)] * 2,
        compiler_params=params(),
        interpret=interpret,
        name="cross_end",
    )(*state, near, halo, coefs.reshape(1, 1))


def spread(marks, mine, other, interpret=False):
    _, _, dy3, dz = constants()
    return pl.pallas_call(
        spread_kernel,
        out_shape=jax.ShapeDtypeStruct((ROWS, NY, NZ), jnp.float32),
        in_specs=[VMEM] * 5,
        out_specs=FAR,
        scratch_shapes=[pltpu.VMEM((ROWS, NY, NZ), jnp.float32), pltpu.SemaphoreType.DMA((NODES - 1,))],
        compiler_params=params(),
        interpret=interpret,
        name="spread",
    )(marks, mine, other, jnp.asarray(dy3, jnp.bfloat16), jnp.asarray(dz, jnp.bfloat16))


def local(density, kappa, levels, coefs):
    den, kap = density[0], kappa[0]
    space, grid = lax.axis_size("space"), lax.axis_size("grid")
    assert den.shape == (ROWS, NY, NZ) and space * ROWS == 512
    pair = [(i, i ^ 1) for i in range(space)]
    other_chip = [(i, (i + 1 if i % 2 else i - 1) % space) for i in range(space)]
    to_cross, to_chip = send(den, kap)
    cross = lax.ppermute(to_cross, "space", other_chip)
    chip = lax.ppermute(to_chip, "space", pair)
    state = inner(levels, den, kap)
    near = chip_end(state, chip)
    sent, stay = cross_end(grid, coefs, state, near, cross)
    got = lax.all_to_all(sent, "grid", split_axis=0, concat_axis=0, tiled=True)
    mine = jnp.concatenate([jnp.sum(got, axis=0, keepdims=True), stay], axis=0)
    other = lax.ppermute(mine, "space", pair)
    return spread(state[6], mine, other)[None]


def solution(mesh):
    in_specs = (
        P("grid", "space", None, None),
        P("grid", "space", None, None),
        P("grid", None),
        P("grid"),
    )
    out_specs = P("grid", "space", None, None)
    return jax.shard_map(local, mesh=mesh, in_specs=in_specs, out_specs=out_specs, check_vma=False)
```

```python
import functools

import jax
import jax.numpy as jnp
import numpy as np
from jax import lax
from jax.experimental import pallas as pl
from jax.experimental.pallas import tpu as pltpu
from jax.sharding import PartitionSpec as P


ITERS = 8
LOW = 3
SPAN = 3
ROWS = 32
GAP = 8
NODES = ROWS // GAP + 1
LEFT = ITERS
RIGHT = ITERS
TALL = LEFT + ROWS + RIGHT + 1
SENT = 2 * ITERS + 1
CHUNK = 8
ROOM = 24 * 1024 * 1024
NY = 64
NZ = 128
TOP = 1 << (LOW + SPAN)


def level_order(count):
    step = count >> (LOW + SPAN)
    order = list(range(0, count, count >> LOW))
    for level in range(LOW + 1, LOW + SPAN + 1):
        gap = count >> level
        order += list(range(gap, count, 2 * gap))
    assert len(order) == TOP and all(i % step == 0 for i in order)
    return order


def tables(count):
    order = level_order(count)
    hier = np.eye(count)
    hats = np.eye(count)
    for index in range(1, count):
        gap = index & -index
        hier[index, (index - gap) % count] -= 0.5
        hier[index, (index + gap) % count] -= 0.5
    gap = count // 2
    while gap:
        for index in range(gap, count, 2 * gap):
            hats[index] += 0.5 * (hats[(index - gap) % count] + hats[(index + gap) % count])
        gap //= 2
    return hier[order], hats[:, order]


@functools.lru_cache(None)
def constants():
    hy, dy = tables(NY)
    hz, dz = tables(NZ)
    spread = [v + 8 * s for v in range(8) for s in range(8)]
    hy = hy[:, spread]
    hz_t = np.zeros((NZ, 128))
    hz_t[:, :TOP] = hz.T
    dz_t = np.zeros((128, NZ))
    dz_t[:TOP] = dz.T
    hy3 = np.concatenate([hy] * 3, axis=1)
    dy3 = np.concatenate([dy] * 3, axis=1)
    return tuple(np.asarray(m, np.float32) for m in (hy3, hz_t, dy3, dz_t))


def staircase():
    spare = {0: SPAN, 1: SPAN - 1, 2: SPAN - 2, 3: SPAN - 3, 4: SPAN - 3}
    summed, kept = [], []
    for plane, left in spare.items():
        for extra in range(left + 1):
            whole = 1 << (LOW + left - extra)
            half = whole // 2 if extra < left else 0
            groups = range(1 << (extra - 1), 1 << extra) if extra else range(1)
            for group in groups:
                if half:
                    summed.append((plane, group, 0, half))
                kept.append((plane, group, half, whole - half))
    blocks = []
    for base, pieces in ((0, summed), (1, kept)):
        place = 0
        for piece in pieces:
            assert place % 128 + piece[3] <= 128
            blocks.append((*piece, base + place // 128, place % 128))
            place += piece[3]
        assert base or place <= 128
    return blocks, 1 + max(b[4] for b in blocks)


BLOCKS, TILES = staircase()
NEED = (LOW, LOW + 1, LOW + 2, LOW + 3, LOW + 3)


def shifted(value, lanes):
    return pltpu.roll(value, lanes % 128, 1) if lanes % 128 else value


def parity():
    return lax.rem(lax.axis_index("space"), 2)


def split3(x):
    hi = x.astype(jnp.bfloat16)
    rest = x - hi.astype(jnp.float32)
    mid = rest.astype(jnp.bfloat16)
    lo = (rest - mid.astype(jnp.float32)).astype(jnp.bfloat16)
    return hi, mid, lo


def rows_dot(weights3, plane):
    stacked = jnp.concatenate(split3(plane), axis=0)
    return jnp.dot(weights3, stacked, preferred_element_type=jnp.float32)


def lanes_dot(planes, weights):
    total = None
    for piece in split3(planes):
        part = jnp.dot(piece, weights, preferred_element_type=jnp.float32)
        total = part if total is None else total + part
    return total


def next_z(row):
    return pltpu.roll(row, NZ - 1, 2)


def prev_z(row):
    return pltpu.roll(row, 1, 2)


def fetch(ref, index):
    row = ref.at[index]
    return jnp.stack([row[pl.ds(v, 8, 8), :] for v in range(8)], axis=0)


def row_coefs(k):
    ahead = jnp.concatenate([k[1:], pltpu.roll(k[0:1], 7, 1)], axis=0)
    behind = pltpu.roll(k[7:8], 1, 1)
    cz, czm = 0.5 * (k + next_z(k)), 0.5 * (k + prev_z(k))
    return 0.5 * (k + ahead), cz, czm, (1.0 - cz) - czm, 0.5 * (k[0] + behind[0])


def step_rows(rows, take, put, coef, first_y, keep=None):
    before, here = take(rows[0] - 1), take(rows[0])
    flux = coef(0, rows[0] - 1) * (here - before)
    for i in rows:
        after = take(i + 1)
        ahead, behind = pltpu.roll(here[0:1], 7, 1), pltpu.roll(here[7:8], 1, 1)
        flux_y = coef(1, i) * (jnp.concatenate([here[1:], ahead], axis=0) - here)
        flux_b = first_y(i) * (here[0] - behind[0])
        along_z = (coef(2, i) * next_z(here) + coef(3, i) * prev_z(here)) + coef(4, i) * here
        flux_x = coef(0, i) * (after - here)
        if keep is not None:
            keep(i, here)
        along_y = flux_y - jnp.concatenate([flux_b[None], flux_y[:7]], axis=0)
        put(i, along_z + ((flux_x - flux) + along_y))
        here, flux = after, flux_x


def inner_rows(step):
    reach = ITERS - step
    if 2 * reach + 1 >= GAP:
        return [range(step, ROWS - step)]
    spans = [range(n - reach, min(n + reach + 1, ROWS - step)) for n in range(GAP, ROWS, GAP)]
    return [r for r in spans if len(r)]


def write_marks(lev, marks):
    level_x, level_y, level_z = lev[0, 0], lev[0, 1], lev[0, 2]
    lane = lax.broadcasted_iota(jnp.int32, (8, 128), 1)
    groups_y = lax.shift_left(1, level_y - LOW)
    width_z = lax.shift_left(1, level_z)
    for b, (plane, group, source, width, _, _) in enumerate(BLOCKS):
        keep = (lane >= source) & (lane < jnp.minimum(width_z, source + width)) & (group < groups_y) & (level_x >= NEED[plane])
        marks[b] = jnp.where(keep, 1.0, 0.0)
    marks[len(BLOCKS)] = jnp.full((8, 128), parity() * 1.0, jnp.float32)


def inner_kernel(lev_h, den, kap, hy3, hz, f_ref, c_ref, cl_ref, old_l, old_r, ends, marks, hy3_v, hz_v, den_v, kap_v, lev, sem, sem_w):
    parts = ROWS // CHUNK

    def copies(part):
        at = pl.ds(part * CHUNK, CHUNK)
        return (
            pltpu.make_async_copy(kap.at[at], kap_v.at[at], sem.at[0, part]),
            pltpu.make_async_copy(den.at[at], den_v.at[at], sem.at[1, part]),
        )

    for part in range(parts):
        for copy in copies(part):
            copy.start()
    weights = [pltpu.make_async_copy(hy3, hy3_v, sem_w.at[0]), pltpu.make_async_copy(hz, hz_v, sem_w.at[1])]
    scalars = [pltpu.make_async_copy(lev_h, lev, sem_w.at[2])]
    for copy in scalars + weights:
        copy.start()
    for copy in scalars:
        copy.wait()
    write_marks(lev, marks)
    for part in range(parts):
        for copy in copies(part):
            copy.wait()

        @pl.when(parity() < 2)
        def _(part=part):
            before = fetch(kap_v, part * CHUNK - 1) if part else None
            for i in range(part * CHUNK, part * CHUNK + CHUNK):
                k = fetch(kap_v, i)
                f_ref[i] = fetch(den_v, i)
                if before is not None:
                    c_ref[0, i - 1] = 0.5 * (before + k)
                c_ref[1, i], c_ref[2, i], c_ref[3, i], c_ref[4, i], cl_ref[i] = row_coefs(k)
                before = k

    ends[0] = fetch(kap_v, 0)
    ends[1] = fetch(kap_v, ROWS - 1)

    for step in range(1, ITERS + 1):
        for rows in inner_rows(step):
            def keep(i, value, step=step):
                if i == step and step <= 4:
                    old_l[step - 1] = value
                if i == ROWS - 1 - step:
                    old_r[step - 1] = value

            def put(i, value):
                f_ref[i] = value

            step_rows(rows, lambda i: f_ref[i], put, lambda a, i: c_ref[a, i], lambda i: cl_ref[i], keep)
    old_r[ITERS - 1] = f_ref[ROWS - 1 - ITERS]
    for copy in weights:
        copy.wait()


def hierarchize(rows, hy3, hz, out):
    planes = [rows_dot(hy3[...], row.reshape(NY, NZ)) for row in rows]
    out[...] = lanes_dot(jnp.concatenate(planes, axis=0), hz[...]).reshape(out.shape)


def read_end(is_left, state, halo, f_new, c_new, cl_new):
    ends = state[5]
    first = -LEFT if is_left else ROWS
    before = None if is_left else ends[1]
    for t in range(ITERS):
        at = first + t + LEFT
        k = fetch(halo, ITERS + t)
        f_new[at] = fetch(halo, t)
        c_new[1, at], c_new[2, at], c_new[3, at], c_new[4, at], cl_new[at] = row_coefs(k)
        if before is not None:
            c_new[0, at - 1] = 0.5 * (before + k)
        before = k
    if is_left:
        c_new[0, LEFT - 1] = 0.5 * (before + ends[0])
    else:
        f_new[TALL - 1] = f_new[TALL - 2]
        c_new[0, TALL - 2] = jnp.zeros_like(before)


def one_end(is_left, state, halo, f_new, c_new, cl_new):
    read_end(is_left, state, halo, f_new, c_new, cl_new)
    f_in, c_in, cl_in, old_l, old_r, _ = state
    fresh = set()

    def take(i):
        return f_new[i + LEFT] if i in fresh or not 0 <= i < ROWS else f_in[i]

    def put(i, value):
        fresh.add(i)
        f_new[i + LEFT] = value

    def coef_at(a, i):
        return c_in[a, i] if 0 <= i < ROWS - 1 or (a and i == ROWS - 1) else c_new[a, i + LEFT]

    def first_y(i):
        return cl_in[i] if 0 <= i < ROWS else cl_new[i + LEFT]

    for step in range(1, ITERS + 1):
        reach = ITERS - step
        if is_left:
            spans = [range(-reach, step if step <= 4 else reach + 1)]
        elif step <= 4:
            spans = [range(ROWS - step, ROWS + reach + 1)]
        else:
            spans = [range(ROWS - step, ROWS - step + 1), range(ROWS - reach, ROWS + reach + 1)]

        def take_old(i, step=step):
            if is_left:
                return old_l[step - 1] if i == step and step <= 4 else take(i)
            return old_r[step - 1] if i == ROWS - 1 - step else take(i)

        for n, rows in enumerate(spans):
            step_rows(rows, take if n else take_old, put, coef_at, first_y)
    return take


def chip_kernel(*refs):
    state, halo, out, work = refs[:6], refs[6], refs[7], refs[8:]

    @pl.when(parity() == 0)
    def _():
        take = one_end(False, state, halo, *work)
        out[0] = take(3 * GAP)
        out[1] = take(4 * GAP) + fetch(halo, SENT - 1)

    @pl.when(parity() == 1)
    def _():
        out[0] = one_end(True, state, halo, *work)(0)


def cross_kernel(*refs):
    state, (marks, hy3, hz, near, halo, coef, out, stay) = refs[:6], refs[6:14]
    work, nodes, nodal = refs[14:17], refs[17], refs[18]
    for n in (1, 2):
        nodes[n] = state[0][n * GAP]

    @pl.when(parity() == 0)
    def _():
        nodes[0] = one_end(True, state, halo, *work)(0)
        nodes[3] = near[0]
        nodes[4] = near[1]

    @pl.when(parity() == 1)
    def _():
        take = one_end(False, state, halo, *work)
        nodes[0] = near[0]
        nodes[3] = take(3 * GAP)
        nodes[4] = take(4 * GAP) + fetch(halo, SENT - 1)

    hierarchize([nodes[n] for n in range(NODES)], hy3, hz, nodal)
    finish(coef, marks, nodal, out, stay)


def finish(coef, marks, nodal, out, stay):
    swapped = marks[len(BLOCKS)] > 0.5

    def planes_of(group):
        u = [nodal[n, group] for n in range(NODES)]
        outer = jnp.where(swapped, u[4], u[0])
        inner = jnp.where(swapped, u[0], u[4])
        return (
            outer,
            0.5 * (inner - outer),
            u[2] - 0.5 * (u[0] + u[4]),
            u[1] - 0.5 * (u[0] + u[2]),
            u[3] - 0.5 * (u[2] + u[4]),
        )

    cache = {}
    tiles = [jnp.zeros((8, 128), jnp.float32)] * TILES
    for b, (plane, group, source, width, tile, first) in enumerate(BLOCKS):
        if group not in cache:
            cache[group] = planes_of(group)
        value = marks[b] * cache[group][plane]
        tiles[tile] = tiles[tile] + shifted(value, first - source)
    weight = jnp.broadcast_to(coef[...].astype(jnp.float32), (8, 128))
    tiles = [weight * tile for tile in tiles]
    for member in range(out.shape[0]):
        out[member] = tiles[0]
    for tile in range(1, TILES):
        stay[tile - 1] = tiles[tile]


def spread_kernel(marks, mine, other, dy3, dz, out, held, sem):
    swapped = marks[len(BLOCKS), 0:1] > 0.5
    zero = jnp.zeros((8, 128), jnp.float32)
    planes = [[zero] * 8 for _ in range(5)]
    outer_other = [zero] * 8
    for b, (plane, group, source, width, tile, first) in enumerate(BLOCKS):

        def pick(value):
            return marks[b] * shifted(value, source - first)

        if plane == 1:
            planes[1][group] += pick(mine[tile] + other[tile])
        else:
            planes[plane][group] += pick(mine[tile])
        if plane == 0:
            outer_other[group] += pick(other[tile])
    wide = []
    outer = jnp.concatenate(planes[0], axis=0)
    middle = 0.5 * (outer + jnp.concatenate(outer_other, axis=0)) + jnp.concatenate(planes[1], axis=0)
    n0 = jnp.where(swapped, middle, outer)
    n4 = jnp.where(swapped, outer, middle)
    n2 = 0.5 * (n0 + n4) + jnp.concatenate(planes[2], axis=0)
    n1 = 0.5 * (n0 + n2) + jnp.concatenate(planes[3], axis=0)
    n3 = 0.5 * (n2 + n4) + jnp.concatenate(planes[4], axis=0)
    for n in (n0, n1, n2, n3, n4):
        wide.append(rows_dot(dy3[...], n))
    full = lanes_dot(jnp.concatenate(wide, axis=0), dz[...]).reshape(NODES, NY, NZ)
    copies = []
    for q in range(NODES - 1):
        slope = (full[q + 1] - full[q]) * (1.0 / GAP)
        for k in range(GAP):
            held[q * GAP + k] = full[q] + float(k) * slope
        at = pl.ds(q * GAP, GAP)
        copies.append(pltpu.make_async_copy(held.at[at], out.at[at], sem.at[q]))
        copies[-1].start()
    for copy in copies:
        copy.wait()


VMEM = pl.BlockSpec(memory_space=pltpu.VMEM)
SMEM = pl.BlockSpec(memory_space=pltpu.SMEM)
FAR = pl.BlockSpec(memory_space=pltpu.HBM)


def straight(halo, far):
    part = halo[ITERS - 1]
    part = far[0] - part
    for j in range(ITERS):
        after = halo[ITERS + j + 1] if j < ITERS - 1 else far[1]
        part = part * (0.5 * (halo[ITERS + j] + after))
    return part


def send_kernel(low_core, den, kap, out, far, sem):
    start = jnp.where(parity() == low_core, 0, ROWS - ITERS)
    copies = []
    for m, source in enumerate((den, kap)):
        copies.append(
            pltpu.make_async_copy(source.at[pl.ds(start, ITERS)], out.at[pl.ds(m * ITERS, ITERS)], sem.at[m])
        )
        copies.append(pltpu.make_async_copy(source.at[ITERS], far.at[m], sem.at[2 + m]))
    for copy in copies:
        copy.start()
    for copy in copies:
        copy.wait()
    out[SENT - 1] = straight(out, far)


def params(room=ROOM):
    return pltpu.CompilerParams(vmem_limit_bytes=room)


def rows_shape(*lead):
    return jax.ShapeDtypeStruct((*lead, 8, 8, 128), jnp.float32)


def far(x):
    return pltpu.with_memory_space_constraint(x, pltpu.HBM)


def send(low_core, den, kap, interpret=False):
    return pl.pallas_call(
        functools.partial(send_kernel, low_core),
        out_shape=jax.ShapeDtypeStruct((SENT, NY, NZ), jnp.float32),
        in_specs=[FAR] * 2,
        out_specs=VMEM,
        scratch_shapes=[pltpu.VMEM((2, NY, NZ), jnp.float32), pltpu.SemaphoreType.DMA((4,))],
        compiler_params=params(8 * 1024 * 1024),
        interpret=interpret,
        name="send",
    )(far(den), far(kap))


def inner(levels, den, kap, interpret=False):
    rows = rows_shape(ROWS)
    hy3, hz, _, _ = constants()
    return pl.pallas_call(
        inner_kernel,
        out_shape=(
            rows,
            rows_shape(5, ROWS),
            jax.ShapeDtypeStruct((ROWS, 8, 128), jnp.float32),
            rows_shape(4),
            rows_shape(ITERS),
            rows_shape(2),
            jax.ShapeDtypeStruct((len(BLOCKS) + 1, 8, 128), jnp.float32),
            jax.ShapeDtypeStruct(hy3.shape, jnp.bfloat16),
            jax.ShapeDtypeStruct(hz.shape, jnp.bfloat16),
        ),
        in_specs=[FAR] * 5,
        out_specs=(VMEM,) * 9,
        scratch_shapes=[pltpu.VMEM((ROWS, NY, NZ), jnp.float32)] * 2
        + [
            pltpu.SMEM((1, 3), jnp.int32),
            pltpu.SemaphoreType.DMA((2, ROWS // CHUNK)),
            pltpu.SemaphoreType.DMA((3,)),
        ],
        compiler_params=params(),
        cost_estimate=pl.CostEstimate(flops=20_000_000, bytes_accessed=8_000_000, transcendentals=0),
        interpret=interpret,
        name="inner",
    )(far(levels), far(den), far(kap), far(jnp.asarray(hy3, jnp.bfloat16)), far(jnp.asarray(hz, jnp.bfloat16)))


def work():
    return [
        pltpu.VMEM((TALL, 8, 8, 128), jnp.float32),
        pltpu.VMEM((5, TALL, 8, 8, 128), jnp.float32),
        pltpu.VMEM((TALL, 8, 128), jnp.float32),
    ]


def chip_end(state, halo, interpret=False):
    return pl.pallas_call(
        chip_kernel,
        out_shape=rows_shape(2),
        in_specs=[VMEM] * 7,
        out_specs=VMEM,
        scratch_shapes=work(),
        compiler_params=params(),
        cost_estimate=pl.CostEstimate(flops=10_000_000, bytes_accessed=4_000_000, transcendentals=0),
        interpret=interpret,
        name="chip_end",
    )(*state[:6], halo)


def cross_end(members, coefs, state, near, halo, interpret=False):
    return pl.pallas_call(
        cross_kernel,
        out_shape=(
            jax.ShapeDtypeStruct((members, 8, 128), jnp.float32),
            jax.ShapeDtypeStruct((TILES - 1, 8, 128), jnp.float32),
        ),
        in_specs=[VMEM] * 12,
        out_specs=(VMEM, VMEM),
        scratch_shapes=work() + [pltpu.VMEM((NODES, 8, 8, 128), jnp.float32)] * 2,
        compiler_params=params(),
        interpret=interpret,
        name="cross_end",
    )(*state, near, halo, coefs.reshape(1, 1))


def spread(marks, mine, other, interpret=False):
    _, _, dy3, dz = constants()
    return pl.pallas_call(
        spread_kernel,
        out_shape=jax.ShapeDtypeStruct((ROWS, NY, NZ), jnp.float32),
        in_specs=[VMEM] * 5,
        out_specs=FAR,
        scratch_shapes=[pltpu.VMEM((ROWS, NY, NZ), jnp.float32), pltpu.SemaphoreType.DMA((NODES - 1,))],
        compiler_params=params(),
        interpret=interpret,
        name="spread",
    )(marks, mine, other, jnp.asarray(dy3, jnp.bfloat16), jnp.asarray(dz, jnp.bfloat16))


def local(density, kappa, levels, coefs):
    den, kap = density[0], kappa[0]
    space, grid = lax.axis_size("space"), lax.axis_size("grid")
    assert den.shape == (ROWS, NY, NZ) and space * ROWS == 512
    pair = [(i, i ^ 1) for i in range(space)]
    other_chip = [(i, (i + 1 if i % 2 else i - 1) % space) for i in range(space)]
    cross = lax.ppermute(send(0, den, kap), "space", other_chip)
    chip = lax.ppermute(send(1, den, kap), "space", pair)
    state = inner(levels, den, kap)
    near = chip_end(state, chip)
    sent, stay = cross_end(grid, coefs, state, near, cross)
    got = lax.all_to_all(sent, "grid", split_axis=0, concat_axis=0, tiled=True)
    mine = jnp.concatenate([jnp.sum(got, axis=0, keepdims=True), stay], axis=0)
    other = lax.ppermute(mine, "space", pair)
    return spread(state[6], mine, other)[None]


def solution(mesh):
    in_specs = (
        P("grid", "space", None, None),
        P("grid", "space", None, None),
        P("grid", None),
        P("grid"),
    )
    out_specs = P("grid", "space", None, None)
    return jax.shard_map(local, mesh=mesh, in_specs=in_specs, out_specs=out_specs, check_vma=False)
```

```python
import functools

import jax
import jax.numpy as jnp
import numpy as np
from jax import lax
from jax.experimental import pallas as pl
from jax.experimental.pallas import tpu as pltpu
from jax.sharding import PartitionSpec as P


ITERS = 8
LOW = 3
SPAN = 3
ROWS = 32
GAP = 8
NODES = ROWS // GAP + 1
LEFT = ITERS
RIGHT = ITERS
TALL = LEFT + ROWS + RIGHT + 1
SENT = 2 * ITERS + 1
CHUNK = 8
ROOM = 24 * 1024 * 1024
NY = 64
NZ = 128
TOP = 1 << (LOW + SPAN)


def level_order(count):
    step = count >> (LOW + SPAN)
    order = list(range(0, count, count >> LOW))
    for level in range(LOW + 1, LOW + SPAN + 1):
        gap = count >> level
        order += list(range(gap, count, 2 * gap))
    assert len(order) == TOP and all(i % step == 0 for i in order)
    return order


def tables(count):
    order = level_order(count)
    hier = np.eye(count)
    hats = np.eye(count)
    for index in range(1, count):
        gap = index & -index
        hier[index, (index - gap) % count] -= 0.5
        hier[index, (index + gap) % count] -= 0.5
    gap = count // 2
    while gap:
        for index in range(gap, count, 2 * gap):
            hats[index] += 0.5 * (hats[(index - gap) % count] + hats[(index + gap) % count])
        gap //= 2
    return hier[order], hats[:, order]


@functools.lru_cache(None)
def constants():
    hy, dy = tables(NY)
    hz, dz = tables(NZ)
    spread = [v + 8 * s for v in range(8) for s in range(8)]
    hy = hy[:, spread]
    hz_t = np.zeros((NZ, 128))
    hz_t[:, :TOP] = hz.T
    dz_t = np.zeros((128, NZ))
    dz_t[:TOP] = dz.T
    hy3 = np.concatenate([hy] * 3, axis=1)
    dy3 = np.concatenate([dy] * 3, axis=1)
    return tuple(np.asarray(m, np.float32) for m in (hy3, hz_t, dy3, dz_t))


def staircase():
    spare = {0: SPAN, 1: SPAN - 1, 2: SPAN - 2, 3: SPAN - 3, 4: SPAN - 3}
    summed, kept = [], []
    for plane, left in spare.items():
        for extra in range(left + 1):
            whole = 1 << (LOW + left - extra)
            half = whole // 2 if extra < left else 0
            groups = range(1 << (extra - 1), 1 << extra) if extra else range(1)
            for group in groups:
                if half:
                    summed.append((plane, group, 0, half))
                kept.append((plane, group, half, whole - half))
    blocks = []
    for base, pieces in ((0, summed), (1, kept)):
        place = 0
        for piece in pieces:
            assert place % 128 + piece[3] <= 128
            blocks.append((*piece, base + place // 128, place % 128))
            place += piece[3]
        assert base or place <= 128
    return blocks, 1 + max(b[4] for b in blocks)


BLOCKS, TILES = staircase()
NEED = (LOW, LOW + 1, LOW + 2, LOW + 3, LOW + 3)


def shifted(value, lanes):
    return pltpu.roll(value, lanes % 128, 1) if lanes % 128 else value


def parity():
    return lax.rem(lax.axis_index("space"), 2)


def split3(x):
    hi = x.astype(jnp.bfloat16)
    rest = x - hi.astype(jnp.float32)
    mid = rest.astype(jnp.bfloat16)
    lo = (rest - mid.astype(jnp.float32)).astype(jnp.bfloat16)
    return hi, mid, lo


def rows_dot(weights3, plane):
    stacked = jnp.concatenate(split3(plane), axis=0)
    return jnp.dot(weights3, stacked, preferred_element_type=jnp.float32)


def lanes_dot(planes, weights):
    total = None
    for piece in split3(planes):
        part = jnp.dot(piece, weights, preferred_element_type=jnp.float32)
        total = part if total is None else total + part
    return total


def next_z(row):
    return pltpu.roll(row, NZ - 1, 2)


def prev_z(row):
    return pltpu.roll(row, 1, 2)


def fetch(ref, index):
    row = ref.at[index]
    return jnp.stack([row[pl.ds(v, 8, 8), :] for v in range(8)], axis=0)


def row_coefs(k):
    ahead = jnp.concatenate([k[1:], pltpu.roll(k[0:1], 7, 1)], axis=0)
    behind = pltpu.roll(k[7:8], 1, 1)
    cz, czm = 0.5 * (k + next_z(k)), 0.5 * (k + prev_z(k))
    return 0.5 * (k + ahead), cz, czm, (1.0 - cz) - czm, 0.5 * (k[0] + behind[0])


def step_rows(rows, take, put, coef, first_y, keep=None):
    before, here = take(rows[0] - 1), take(rows[0])
    flux = coef(0, rows[0] - 1) * (here - before)
    for i in rows:
        after = take(i + 1)
        ahead, behind = pltpu.roll(here[0:1], 7, 1), pltpu.roll(here[7:8], 1, 1)
        flux_y = coef(1, i) * (jnp.concatenate([here[1:], ahead], axis=0) - here)
        flux_b = first_y(i) * (here[0] - behind[0])
        along_z = (coef(2, i) * next_z(here) + coef(3, i) * prev_z(here)) + coef(4, i) * here
        flux_x = coef(0, i) * (after - here)
        if keep is not None:
            keep(i, here)
        along_y = flux_y - jnp.concatenate([flux_b[None], flux_y[:7]], axis=0)
        put(i, along_z + ((flux_x - flux) + along_y))
        here, flux = after, flux_x


def inner_rows(step):
    reach = ITERS - step
    if 2 * reach + 1 >= GAP:
        return [range(step, ROWS - step)]
    spans = [range(n - reach, min(n + reach + 1, ROWS - step)) for n in range(GAP, ROWS, GAP)]
    return [r for r in spans if len(r)]


def write_marks(lev, marks):
    level_x, level_y, level_z = lev[0, 0], lev[0, 1], lev[0, 2]
    lane = lax.broadcasted_iota(jnp.int32, (8, 128), 1)
    groups_y = lax.shift_left(1, level_y - LOW)
    width_z = lax.shift_left(1, level_z)
    for b, (plane, group, source, width, _, _) in enumerate(BLOCKS):
        keep = (lane >= source) & (lane < jnp.minimum(width_z, source + width)) & (group < groups_y) & (level_x >= NEED[plane])
        marks[b] = jnp.where(keep, 1.0, 0.0)
    marks[len(BLOCKS)] = jnp.full((8, 128), parity() * 1.0, jnp.float32)


def inner_kernel(lev_h, den, kap, hy3, hz, f_ref, c_ref, cl_ref, old_l, old_r, ends, marks, hy3_v, hz_v, den_v, kap_v, lev, sem, sem_w):
    parts = ROWS // CHUNK

    def copies(part):
        at = pl.ds(part * CHUNK, CHUNK)
        return (
            pltpu.make_async_copy(kap.at[at], kap_v.at[at], sem.at[0, part]),
            pltpu.make_async_copy(den.at[at], den_v.at[at], sem.at[1, part]),
        )

    for part in range(parts):
        for copy in copies(part):
            copy.start()
    weights = [pltpu.make_async_copy(hy3, hy3_v, sem_w.at[0]), pltpu.make_async_copy(hz, hz_v, sem_w.at[1])]
    scalars = [pltpu.make_async_copy(lev_h, lev, sem_w.at[2])]
    for copy in scalars + weights:
        copy.start()
    for copy in scalars:
        copy.wait()
    write_marks(lev, marks)
    for part in range(parts):
        for copy in copies(part):
            copy.wait()

        @pl.when(parity() < 2)
        def _(part=part):
            before = fetch(kap_v, part * CHUNK - 1) if part else None
            for i in range(part * CHUNK, part * CHUNK + CHUNK):
                k = fetch(kap_v, i)
                f_ref[i] = fetch(den_v, i)
                if before is not None:
                    c_ref[0, i - 1] = 0.5 * (before + k)
                c_ref[1, i], c_ref[2, i], c_ref[3, i], c_ref[4, i], cl_ref[i] = row_coefs(k)
                before = k

    ends[0] = fetch(kap_v, 0)
    ends[1] = fetch(kap_v, ROWS - 1)

    for step in range(1, ITERS + 1):
        for rows in inner_rows(step):
            def keep(i, value, step=step):
                if i == step and step <= 4:
                    old_l[step - 1] = value
                if i == ROWS - 1 - step:
                    old_r[step - 1] = value

            def put(i, value):
                f_ref[i] = value

            step_rows(rows, lambda i: f_ref[i], put, lambda a, i: c_ref[a, i], lambda i: cl_ref[i], keep)
    old_r[ITERS - 1] = f_ref[ROWS - 1 - ITERS]
    for copy in weights:
        copy.wait()


def hierarchize(rows, hy3, hz, out):
    planes = [rows_dot(hy3[...], row.reshape(NY, NZ)) for row in rows]
    out[...] = lanes_dot(jnp.concatenate(planes, axis=0), hz[...]).reshape(out.shape)


def read_end(is_left, state, halo, f_new, c_new, cl_new):
    ends = state[5]
    first = -LEFT if is_left else ROWS
    before = None if is_left else ends[1]
    for t in range(ITERS):
        at = first + t + LEFT
        k = fetch(halo, ITERS + t)
        f_new[at] = fetch(halo, t)
        c_new[1, at], c_new[2, at], c_new[3, at], c_new[4, at], cl_new[at] = row_coefs(k)
        if before is not None:
            c_new[0, at - 1] = 0.5 * (before + k)
        before = k
    if is_left:
        c_new[0, LEFT - 1] = 0.5 * (before + ends[0])
    else:
        f_new[TALL - 1] = f_new[TALL - 2]
        c_new[0, TALL - 2] = jnp.zeros_like(before)


def one_end(is_left, state, halo, f_new, c_new, cl_new):
    read_end(is_left, state, halo, f_new, c_new, cl_new)
    f_in, c_in, cl_in, old_l, old_r, _ = state
    fresh = set()

    def take(i):
        return f_new[i + LEFT] if i in fresh or not 0 <= i < ROWS else f_in[i]

    def put(i, value):
        fresh.add(i)
        f_new[i + LEFT] = value

    def coef_at(a, i):
        return c_in[a, i] if 0 <= i < ROWS - 1 or (a and i == ROWS - 1) else c_new[a, i + LEFT]

    def first_y(i):
        return cl_in[i] if 0 <= i < ROWS else cl_new[i + LEFT]

    for step in range(1, ITERS + 1):
        reach = ITERS - step
        if is_left:
            spans = [range(-reach, step if step <= 4 else reach + 1)]
        elif step <= 4:
            spans = [range(ROWS - step, ROWS + reach + 1)]
        else:
            spans = [range(ROWS - step, ROWS - step + 1), range(ROWS - reach, ROWS + reach + 1)]

        def take_old(i, step=step):
            if is_left:
                return old_l[step - 1] if i == step and step <= 4 else take(i)
            return old_r[step - 1] if i == ROWS - 1 - step else take(i)

        for n, rows in enumerate(spans):
            step_rows(rows, take if n else take_old, put, coef_at, first_y)
    return take


def chip_kernel(*refs):
    state, halo, out, work = refs[:6], refs[6], refs[7], refs[8:]

    @pl.when(parity() == 0)
    def _():
        take = one_end(False, state, halo, *work)
        out[0] = take(3 * GAP)
        out[1] = take(4 * GAP) + fetch(halo, SENT - 1)

    @pl.when(parity() == 1)
    def _():
        out[0] = one_end(True, state, halo, *work)(0)


def cross_kernel(*refs):
    state, (marks, hy3, hz, near, halo, coef, out, stay) = refs[:6], refs[6:14]
    work, nodes, nodal = refs[14:17], refs[17], refs[18]
    for n in (1, 2):
        nodes[n] = state[0][n * GAP]

    @pl.when(parity() == 0)
    def _():
        nodes[0] = one_end(True, state, halo, *work)(0)
        nodes[3] = near[0]
        nodes[4] = near[1]

    @pl.when(parity() == 1)
    def _():
        take = one_end(False, state, halo, *work)
        nodes[0] = near[0]
        nodes[3] = take(3 * GAP)
        nodes[4] = take(4 * GAP) + fetch(halo, SENT - 1)

    hierarchize([nodes[n] for n in range(NODES)], hy3, hz, nodal)
    finish(coef, marks, nodal, out, stay)


def finish(coef, marks, nodal, out, stay):
    swapped = marks[len(BLOCKS)] > 0.5

    def planes_of(group):
        u = [nodal[n, group] for n in range(NODES)]
        outer = jnp.where(swapped, u[4], u[0])
        inner = jnp.where(swapped, u[0], u[4])
        return (
            outer,
            0.5 * (inner - outer),
            u[2] - 0.5 * (u[0] + u[4]),
            u[1] - 0.5 * (u[0] + u[2]),
            u[3] - 0.5 * (u[2] + u[4]),
        )

    cache = {}
    tiles = [jnp.zeros((8, 128), jnp.float32)] * TILES
    for b, (plane, group, source, width, tile, first) in enumerate(BLOCKS):
        if group not in cache:
            cache[group] = planes_of(group)
        value = marks[b] * cache[group][plane]
        tiles[tile] = tiles[tile] + shifted(value, first - source)
    weight = jnp.broadcast_to(coef[...].astype(jnp.float32), (8, 128))
    tiles = [weight * tile for tile in tiles]
    for member in range(out.shape[0]):
        out[member] = tiles[0]
    for tile in range(1, TILES):
        stay[tile - 1] = tiles[tile]


def unpacked(marks, tiles, wanted):
    zero = jnp.zeros((8, 128), jnp.float32)
    planes = {plane: [zero] * 8 for plane in wanted}
    for b, (plane, group, source, width, tile, first) in enumerate(BLOCKS):
        if plane in planes:
            planes[plane][group] += marks[b] * shifted(tiles[tile], source - first)
    return [jnp.concatenate(planes[plane], axis=0) for plane in wanted]


def own_kernel(marks, mine, dy3, dz, out):
    swapped = marks[len(BLOCKS), 0:1] > 0.5
    outer, half, five, six, seven = unpacked(marks, mine, range(5))
    middle = 0.5 * outer + half
    n0 = jnp.where(swapped, middle, outer)
    n4 = jnp.where(swapped, outer, middle)
    n2 = 0.5 * (n0 + n4) + five
    n1 = 0.5 * (n0 + n2) + six
    n3 = 0.5 * (n2 + n4) + seven
    wide = [rows_dot(dy3[...], n) for n in (n0, n1, n2, n3, n4)]
    out[...] = lanes_dot(jnp.concatenate(wide, axis=0), dz[...]).reshape(NODES, NY, NZ)


def spread_kernel(marks, other, dy3, dz, full_ref, out, held, sem):
    outer, half = unpacked(marks, other, (0, 1))
    middle = lanes_dot(rows_dot(dy3[...], 0.5 * outer + half), dz[...])
    odd = parity() == 1
    full = []
    for n in range(NODES):
        share = n / (NODES - 1)
        full.append(full_ref[n] + jnp.where(odd, 1.0 - share, share) * middle)
    copies = []
    for q in range(NODES - 1):
        slope = (full[q + 1] - full[q]) * (1.0 / GAP)
        for k in range(GAP):
            held[q * GAP + k] = full[q] + float(k) * slope
        at = pl.ds(q * GAP, GAP)
        copies.append(pltpu.make_async_copy(held.at[at], out.at[at], sem.at[q]))
        copies[-1].start()
    for copy in copies:
        copy.wait()


VMEM = pl.BlockSpec(memory_space=pltpu.VMEM)
SMEM = pl.BlockSpec(memory_space=pltpu.SMEM)
FAR = pl.BlockSpec(memory_space=pltpu.HBM)


def straight(halo, far):
    part = halo[ITERS - 1]
    part = far[0] - part
    for j in range(ITERS):
        after = halo[ITERS + j + 1] if j < ITERS - 1 else far[1]
        part = part * (0.5 * (halo[ITERS + j] + after))
    return part


def send_kernel(den, kap, cross, chip, far, sem):
    low = (ROWS - ITERS) * parity()
    copies = []
    for m, source in enumerate((den, kap)):
        at = pl.ds(m * ITERS, ITERS)
        for n, (out, start) in enumerate(((cross, low), (chip, ROWS - ITERS - low))):
            copies.append(pltpu.make_async_copy(source.at[pl.ds(start, ITERS)], out.at[at], sem.at[n, m]))
        copies.append(pltpu.make_async_copy(source.at[ITERS], far.at[m], sem.at[2, m]))
    for copy in copies:
        copy.start()
    for copy in copies:
        copy.wait()

    @pl.when(parity() == 0)
    def _():
        cross[SENT - 1] = straight(cross, far)
        chip[SENT - 1] = jnp.zeros((NY, NZ), jnp.float32)

    @pl.when(parity() == 1)
    def _():
        cross[SENT - 1] = jnp.zeros((NY, NZ), jnp.float32)
        chip[SENT - 1] = straight(chip, far)


def params(room=ROOM):
    return pltpu.CompilerParams(vmem_limit_bytes=room)


def rows_shape(*lead):
    return jax.ShapeDtypeStruct((*lead, 8, 8, 128), jnp.float32)


def far(x):
    return pltpu.with_memory_space_constraint(x, pltpu.HBM)


def send(den, kap, interpret=False):
    rows = jax.ShapeDtypeStruct((SENT, NY, NZ), jnp.float32)
    return pl.pallas_call(
        send_kernel,
        out_shape=(rows, rows),
        in_specs=[FAR] * 2,
        out_specs=(VMEM, VMEM),
        scratch_shapes=[pltpu.VMEM((2, NY, NZ), jnp.float32), pltpu.SemaphoreType.DMA((3, 2))],
        compiler_params=params(8 * 1024 * 1024),
        interpret=interpret,
        name="send",
    )(far(den), far(kap))


def inner(levels, den, kap, interpret=False):
    rows = rows_shape(ROWS)
    hy3, hz, _, _ = constants()
    return pl.pallas_call(
        inner_kernel,
        out_shape=(
            rows,
            rows_shape(5, ROWS),
            jax.ShapeDtypeStruct((ROWS, 8, 128), jnp.float32),
            rows_shape(4),
            rows_shape(ITERS),
            rows_shape(2),
            jax.ShapeDtypeStruct((len(BLOCKS) + 1, 8, 128), jnp.float32),
            jax.ShapeDtypeStruct(hy3.shape, jnp.bfloat16),
            jax.ShapeDtypeStruct(hz.shape, jnp.bfloat16),
        ),
        in_specs=[FAR] * 5,
        out_specs=(VMEM,) * 9,
        scratch_shapes=[pltpu.VMEM((ROWS, NY, NZ), jnp.float32)] * 2
        + [
            pltpu.SMEM((1, 3), jnp.int32),
            pltpu.SemaphoreType.DMA((2, ROWS // CHUNK)),
            pltpu.SemaphoreType.DMA((3,)),
        ],
        compiler_params=params(),
        cost_estimate=pl.CostEstimate(flops=20_000_000, bytes_accessed=8_000_000, transcendentals=0),
        interpret=interpret,
        name="inner",
    )(far(levels), far(den), far(kap), far(jnp.asarray(hy3, jnp.bfloat16)), far(jnp.asarray(hz, jnp.bfloat16)))


def work():
    return [
        pltpu.VMEM((TALL, 8, 8, 128), jnp.float32),
        pltpu.VMEM((5, TALL, 8, 8, 128), jnp.float32),
        pltpu.VMEM((TALL, 8, 128), jnp.float32),
    ]


def chip_end(state, halo, interpret=False):
    return pl.pallas_call(
        chip_kernel,
        out_shape=rows_shape(2),
        in_specs=[VMEM] * 7,
        out_specs=VMEM,
        scratch_shapes=work(),
        compiler_params=params(),
        cost_estimate=pl.CostEstimate(flops=10_000_000, bytes_accessed=4_000_000, transcendentals=0),
        interpret=interpret,
        name="chip_end",
    )(*state[:6], halo)


def cross_end(members, coefs, state, near, halo, interpret=False):
    return pl.pallas_call(
        cross_kernel,
        out_shape=(
            jax.ShapeDtypeStruct((members, 8, 128), jnp.float32),
            jax.ShapeDtypeStruct((TILES - 1, 8, 128), jnp.float32),
        ),
        in_specs=[VMEM] * 12,
        out_specs=(VMEM, VMEM),
        scratch_shapes=work() + [pltpu.VMEM((NODES, 8, 8, 128), jnp.float32)] * 2,
        compiler_params=params(),
        interpret=interpret,
        name="cross_end",
    )(*state, near, halo, coefs.reshape(1, 1))


def spread_tables():
    _, _, dy3, dz = constants()
    return jnp.asarray(dy3, jnp.bfloat16), jnp.asarray(dz, jnp.bfloat16)


def own_nodes(marks, mine, interpret=False):
    return pl.pallas_call(
        own_kernel,
        out_shape=jax.ShapeDtypeStruct((NODES, NY, NZ), jnp.float32),
        in_specs=[VMEM] * 4,
        out_specs=VMEM,
        compiler_params=params(),
        cost_estimate=pl.CostEstimate(flops=40_000_000, bytes_accessed=400_000, transcendentals=0),
        interpret=interpret,
        name="own_nodes",
    )(marks, mine, *spread_tables())


def spread(marks, other, full, interpret=False):
    return pl.pallas_call(
        spread_kernel,
        out_shape=jax.ShapeDtypeStruct((ROWS, NY, NZ), jnp.float32),
        in_specs=[VMEM] * 5,
        out_specs=FAR,
        scratch_shapes=[pltpu.VMEM((ROWS, NY, NZ), jnp.float32), pltpu.SemaphoreType.DMA((NODES - 1,))],
        compiler_params=params(),
        interpret=interpret,
        name="spread",
    )(marks, other, *spread_tables(), full)


def local(density, kappa, levels, coefs):
    den, kap = density[0], kappa[0]
    space, grid = lax.axis_size("space"), lax.axis_size("grid")
    assert den.shape == (ROWS, NY, NZ) and space * ROWS == 512
    pair = [(i, i ^ 1) for i in range(space)]
    other_chip = [(i, (i + 1 if i % 2 else i - 1) % space) for i in range(space)]
    to_cross, to_chip = send(den, kap)
    cross = lax.ppermute(to_cross, "space", other_chip)
    chip = lax.ppermute(to_chip, "space", pair)
    state = inner(levels, den, kap)
    near = chip_end(state, chip)
    sent, stay = cross_end(grid, coefs, state, near, cross)
    got = lax.all_to_all(sent, "grid", split_axis=0, concat_axis=0, tiled=True)
    mine = jnp.concatenate([jnp.sum(got, axis=0, keepdims=True), stay], axis=0)
    other = lax.ppermute(mine, "space", pair)
    return spread(state[6], other, own_nodes(state[6], mine))[None]


def solution(mesh):
    in_specs = (
        P("grid", "space", None, None),
        P("grid", "space", None, None),
        P("grid", None),
        P("grid"),
    )
    out_specs = P("grid", "space", None, None)
    return jax.shard_map(local, mesh=mesh, in_specs=in_specs, out_specs=out_specs, check_vma=False)
```

```python
import functools

import jax
import jax.numpy as jnp
import numpy as np
from jax import lax
from jax.experimental import pallas as pl
from jax.experimental.pallas import tpu as pltpu
from jax.sharding import PartitionSpec as P


ITERS = 8
LOW = 3
SPAN = 3
ROWS = 32
GAP = 8
NODES = ROWS // GAP + 1
LEFT = ITERS
RIGHT = ITERS
TALL = LEFT + ROWS + RIGHT + 1
SENT = 2 * ITERS + 1
CHUNK = 4
ROOM = 24 * 1024 * 1024
NY = 64
NZ = 128
TOP = 1 << (LOW + SPAN)


def level_order(count):
    step = count >> (LOW + SPAN)
    order = list(range(0, count, count >> LOW))
    for level in range(LOW + 1, LOW + SPAN + 1):
        gap = count >> level
        order += list(range(gap, count, 2 * gap))
    assert len(order) == TOP and all(i % step == 0 for i in order)
    return order


def tables(count):
    order = level_order(count)
    hier = np.eye(count)
    hats = np.eye(count)
    for index in range(1, count):
        gap = index & -index
        hier[index, (index - gap) % count] -= 0.5
        hier[index, (index + gap) % count] -= 0.5
    gap = count // 2
    while gap:
        for index in range(gap, count, 2 * gap):
            hats[index] += 0.5 * (hats[(index - gap) % count] + hats[(index + gap) % count])
        gap //= 2
    return hier[order], hats[:, order]


@functools.lru_cache(None)
def constants():
    hy, dy = tables(NY)
    hz, dz = tables(NZ)
    spread = [v + 8 * s for v in range(8) for s in range(8)]
    hy = hy[:, spread]
    hz_t = np.zeros((NZ, 128))
    hz_t[:, :TOP] = hz.T
    dz_t = np.zeros((128, NZ))
    dz_t[:TOP] = dz.T
    hy3 = np.concatenate([hy] * 3, axis=1)
    dy3 = np.concatenate([dy] * 3, axis=1)
    return tuple(np.asarray(m, np.float32) for m in (hy3, hz_t, dy3, dz_t))


def staircase():
    spare = {0: SPAN, 1: SPAN - 1, 2: SPAN - 2, 3: SPAN - 3, 4: SPAN - 3}
    summed, kept = [], []
    for plane, left in spare.items():
        for extra in range(left + 1):
            whole = 1 << (LOW + left - extra)
            half = whole // 2 if extra < left else 0
            groups = range(1 << (extra - 1), 1 << extra) if extra else range(1)
            for group in groups:
                if half:
                    summed.append((plane, group, 0, half))
                kept.append((plane, group, half, whole - half))
    blocks = []
    for base, pieces in ((0, summed), (1, kept)):
        place = 0
        for piece in pieces:
            assert place % 128 + piece[3] <= 128
            blocks.append((*piece, base + place // 128, place % 128))
            place += piece[3]
        assert base or place <= 128
    return blocks, 1 + max(b[4] for b in blocks)


BLOCKS, TILES = staircase()
NEED = (LOW, LOW + 1, LOW + 2, LOW + 3, LOW + 3)


def shifted(value, lanes):
    return pltpu.roll(value, lanes % 128, 1) if lanes % 128 else value


def parity():
    return lax.rem(lax.axis_index("space"), 2)


def split3(x):
    hi = x.astype(jnp.bfloat16)
    rest = x - hi.astype(jnp.float32)
    mid = rest.astype(jnp.bfloat16)
    lo = (rest - mid.astype(jnp.float32)).astype(jnp.bfloat16)
    return hi, mid, lo


def rows_dot(weights3, plane):
    stacked = jnp.concatenate(split3(plane), axis=0)
    return jnp.dot(weights3, stacked, preferred_element_type=jnp.float32)


def lanes_dot(planes, weights):
    total = None
    for piece in split3(planes):
        part = jnp.dot(piece, weights, preferred_element_type=jnp.float32)
        total = part if total is None else total + part
    return total


def next_z(row):
    return pltpu.roll(row, NZ - 1, 2)


def prev_z(row):
    return pltpu.roll(row, 1, 2)


def fetch(ref, index):
    row = ref.at[index]
    return jnp.stack([row[pl.ds(v, 8, 8), :] for v in range(8)], axis=0)


def row_coefs(k):
    ahead = jnp.concatenate([k[1:], pltpu.roll(k[0:1], 7, 1)], axis=0)
    behind = pltpu.roll(k[7:8], 1, 1)
    cz, czm = 0.5 * (k + next_z(k)), 0.5 * (k + prev_z(k))
    return 0.5 * (k + ahead), cz, czm, (1.0 - cz) - czm, 0.5 * (k[0] + behind[0])


def step_rows(rows, take, put, coef, first_y, keep=None):
    before, here = take(rows[0] - 1), take(rows[0])
    flux = coef(0, rows[0] - 1) * (here - before)
    for i in rows:
        after = take(i + 1)
        ahead, behind = pltpu.roll(here[0:1], 7, 1), pltpu.roll(here[7:8], 1, 1)
        flux_y = coef(1, i) * (jnp.concatenate([here[1:], ahead], axis=0) - here)
        flux_b = first_y(i) * (here[0] - behind[0])
        along_z = (coef(2, i) * next_z(here) + coef(3, i) * prev_z(here)) + coef(4, i) * here
        flux_x = coef(0, i) * (after - here)
        if keep is not None:
            keep(i, here)
        along_y = flux_y - jnp.concatenate([flux_b[None], flux_y[:7]], axis=0)
        put(i, along_z + ((flux_x - flux) + along_y))
        here, flux = after, flux_x


def inner_rows(step):
    reach = ITERS - step
    if 2 * reach + 1 >= GAP:
        return [range(step, ROWS - step)]
    spans = [range(n - reach, min(n + reach + 1, ROWS - step)) for n in range(GAP, ROWS, GAP)]
    return [r for r in spans if len(r)]


def write_marks(lev, marks):
    level_x, level_y, level_z = lev[0, 0], lev[0, 1], lev[0, 2]
    lane = lax.broadcasted_iota(jnp.int32, (8, 128), 1)
    groups_y = lax.shift_left(1, level_y - LOW)
    width_z = lax.shift_left(1, level_z)
    for b, (plane, group, source, width, _, _) in enumerate(BLOCKS):
        keep = (lane >= source) & (lane < jnp.minimum(width_z, source + width)) & (group < groups_y) & (level_x >= NEED[plane])
        marks[b] = jnp.where(keep, 1.0, 0.0)
    marks[len(BLOCKS)] = jnp.full((8, 128), parity() * 1.0, jnp.float32)


def inner_kernel(lev_h, den, kap, hy3, hz, f_ref, c_ref, cl_ref, old_l, old_r, ends, marks, hy3_v, hz_v, den_v, kap_v, lev, sem, sem_w):
    parts = ROWS // CHUNK

    def copies(part):
        at = pl.ds(part * CHUNK, CHUNK)
        return (
            pltpu.make_async_copy(kap.at[at], kap_v.at[at], sem.at[0, part]),
            pltpu.make_async_copy(den.at[at], den_v.at[at], sem.at[1, part]),
        )

    for part in range(parts):
        for copy in copies(part):
            copy.start()
    weights = [pltpu.make_async_copy(hy3, hy3_v, sem_w.at[0]), pltpu.make_async_copy(hz, hz_v, sem_w.at[1])]
    scalars = [pltpu.make_async_copy(lev_h, lev, sem_w.at[2])]
    for copy in scalars + weights:
        copy.start()
    for copy in scalars:
        copy.wait()
    write_marks(lev, marks)
    for part in range(parts):
        for copy in copies(part):
            copy.wait()

        @pl.when(parity() < 2)
        def _(part=part):
            before = fetch(kap_v, part * CHUNK - 1) if part else None
            for i in range(part * CHUNK, part * CHUNK + CHUNK):
                k = fetch(kap_v, i)
                f_ref[i] = fetch(den_v, i)
                if before is not None:
                    c_ref[0, i - 1] = 0.5 * (before + k)
                c_ref[1, i], c_ref[2, i], c_ref[3, i], c_ref[4, i], cl_ref[i] = row_coefs(k)
                before = k

    ends[0] = fetch(kap_v, 0)
    ends[1] = fetch(kap_v, ROWS - 1)

    for step in range(1, ITERS + 1):
        for rows in inner_rows(step):
            def keep(i, value, step=step):
                if i == step and step <= 4:
                    old_l[step - 1] = value
                if i == ROWS - 1 - step:
                    old_r[step - 1] = value

            def put(i, value):
                f_ref[i] = value

            step_rows(rows, lambda i: f_ref[i], put, lambda a, i: c_ref[a, i], lambda i: cl_ref[i], keep)
    old_r[ITERS - 1] = f_ref[ROWS - 1 - ITERS]
    for copy in weights:
        copy.wait()


def hierarchize(rows, hy3, hz, out):
    planes = [rows_dot(hy3[...], row.reshape(NY, NZ)) for row in rows]
    out[...] = lanes_dot(jnp.concatenate(planes, axis=0), hz[...]).reshape(out.shape)


def read_end(is_left, state, halo, f_new, c_new, cl_new):
    ends = state[5]
    first = -LEFT if is_left else ROWS
    before = None if is_left else ends[1]
    for t in range(ITERS):
        at = first + t + LEFT
        k = fetch(halo, ITERS + t)
        f_new[at] = fetch(halo, t)
        c_new[1, at], c_new[2, at], c_new[3, at], c_new[4, at], cl_new[at] = row_coefs(k)
        if before is not None:
            c_new[0, at - 1] = 0.5 * (before + k)
        before = k
    if is_left:
        c_new[0, LEFT - 1] = 0.5 * (before + ends[0])
    else:
        f_new[TALL - 1] = f_new[TALL - 2]
        c_new[0, TALL - 2] = jnp.zeros_like(before)


def one_end(is_left, state, halo, f_new, c_new, cl_new):
    read_end(is_left, state, halo, f_new, c_new, cl_new)
    f_in, c_in, cl_in, old_l, old_r, _ = state
    fresh = set()

    def take(i):
        return f_new[i + LEFT] if i in fresh or not 0 <= i < ROWS else f_in[i]

    def put(i, value):
        fresh.add(i)
        f_new[i + LEFT] = value

    def coef_at(a, i):
        return c_in[a, i] if 0 <= i < ROWS - 1 or (a and i == ROWS - 1) else c_new[a, i + LEFT]

    def first_y(i):
        return cl_in[i] if 0 <= i < ROWS else cl_new[i + LEFT]

    for step in range(1, ITERS + 1):
        reach = ITERS - step
        if is_left:
            spans = [range(-reach, step if step <= 4 else reach + 1)]
        elif step <= 4:
            spans = [range(ROWS - step, ROWS + reach + 1)]
        else:
            spans = [range(ROWS - step, ROWS - step + 1), range(ROWS - reach, ROWS + reach + 1)]

        def take_old(i, step=step):
            if is_left:
                return old_l[step - 1] if i == step and step <= 4 else take(i)
            return old_r[step - 1] if i == ROWS - 1 - step else take(i)

        for n, rows in enumerate(spans):
            step_rows(rows, take if n else take_old, put, coef_at, first_y)
    return take


def chip_kernel(*refs):
    state, halo, out, work = refs[:6], refs[6], refs[7], refs[8:]

    @pl.when(parity() == 0)
    def _():
        take = one_end(False, state, halo, *work)
        out[0] = take(3 * GAP)
        out[1] = take(4 * GAP) + fetch(halo, SENT - 1)

    @pl.when(parity() == 1)
    def _():
        out[0] = one_end(True, state, halo, *work)(0)


def cross_kernel(*refs):
    state, (marks, hy3, hz, near, halo, coef, out, stay) = refs[:6], refs[6:14]
    work, nodes, nodal = refs[14:17], refs[17], refs[18]
    for n in (1, 2):
        nodes[n] = state[0][n * GAP]

    @pl.when(parity() == 0)
    def _():
        nodes[0] = one_end(True, state, halo, *work)(0)
        nodes[3] = near[0]
        nodes[4] = near[1]

    @pl.when(parity() == 1)
    def _():
        take = one_end(False, state, halo, *work)
        nodes[0] = near[0]
        nodes[3] = take(3 * GAP)
        nodes[4] = take(4 * GAP) + fetch(halo, SENT - 1)

    hierarchize([nodes[n] for n in range(NODES)], hy3, hz, nodal)
    finish(coef, marks, nodal, out, stay)


def finish(coef, marks, nodal, out, stay):
    swapped = marks[len(BLOCKS)] > 0.5

    def planes_of(group):
        u = [nodal[n, group] for n in range(NODES)]
        outer = jnp.where(swapped, u[4], u[0])
        inner = jnp.where(swapped, u[0], u[4])
        return (
            outer,
            0.5 * (inner - outer),
            u[2] - 0.5 * (u[0] + u[4]),
            u[1] - 0.5 * (u[0] + u[2]),
            u[3] - 0.5 * (u[2] + u[4]),
        )

    cache = {}
    tiles = [jnp.zeros((8, 128), jnp.float32)] * TILES
    for b, (plane, group, source, width, tile, first) in enumerate(BLOCKS):
        if group not in cache:
            cache[group] = planes_of(group)
        value = marks[b] * cache[group][plane]
        tiles[tile] = tiles[tile] + shifted(value, first - source)
    weight = jnp.broadcast_to(coef[...].astype(jnp.float32), (8, 128))
    tiles = [weight * tile for tile in tiles]
    for member in range(out.shape[0]):
        out[member] = tiles[0]
    for tile in range(1, TILES):
        stay[tile - 1] = tiles[tile]


def spread_kernel(marks, mine, other, dy3, dz, out, held, sem):
    swapped = marks[len(BLOCKS), 0:1] > 0.5
    zero = jnp.zeros((8, 128), jnp.float32)
    planes = [[zero] * 8 for _ in range(5)]
    outer_other = [zero] * 8
    for b, (plane, group, source, width, tile, first) in enumerate(BLOCKS):

        def pick(value):
            return marks[b] * shifted(value, source - first)

        if plane == 1:
            planes[1][group] += pick(mine[tile] + other[tile])
        else:
            planes[plane][group] += pick(mine[tile])
        if plane == 0:
            outer_other[group] += pick(other[tile])
    wide = []
    outer = jnp.concatenate(planes[0], axis=0)
    middle = 0.5 * (outer + jnp.concatenate(outer_other, axis=0)) + jnp.concatenate(planes[1], axis=0)
    n0 = jnp.where(swapped, middle, outer)
    n4 = jnp.where(swapped, outer, middle)
    n2 = 0.5 * (n0 + n4) + jnp.concatenate(planes[2], axis=0)
    n1 = 0.5 * (n0 + n2) + jnp.concatenate(planes[3], axis=0)
    n3 = 0.5 * (n2 + n4) + jnp.concatenate(planes[4], axis=0)
    for n in (n0, n1, n2, n3, n4):
        wide.append(rows_dot(dy3[...], n))
    full = lanes_dot(jnp.concatenate(wide, axis=0), dz[...]).reshape(NODES, NY, NZ)
    copies = []
    for q in range(NODES - 1):
        slope = (full[q + 1] - full[q]) * (1.0 / GAP)
        for k in range(GAP):
            held[q * GAP + k] = full[q] + float(k) * slope
        at = pl.ds(q * GAP, GAP)
        copies.append(pltpu.make_async_copy(held.at[at], out.at[at], sem.at[q]))
        copies[-1].start()
    for copy in copies:
        copy.wait()


VMEM = pl.BlockSpec(memory_space=pltpu.VMEM)
SMEM = pl.BlockSpec(memory_space=pltpu.SMEM)
FAR = pl.BlockSpec(memory_space=pltpu.HBM)


def straight(halo, far):
    part = halo[ITERS - 1]
    part = far[0] - part
    for j in range(ITERS):
        after = halo[ITERS + j + 1] if j < ITERS - 1 else far[1]
        part = part * (0.5 * (halo[ITERS + j] + after))
    return part


def send_kernel(den, kap, cross, chip, far, sem):
    low = (ROWS - ITERS) * parity()
    copies = []
    for m, source in enumerate((den, kap)):
        at = pl.ds(m * ITERS, ITERS)
        for n, (out, start) in enumerate(((cross, low), (chip, ROWS - ITERS - low))):
            copies.append(pltpu.make_async_copy(source.at[pl.ds(start, ITERS)], out.at[at], sem.at[n, m]))
        copies.append(pltpu.make_async_copy(source.at[ITERS], far.at[m], sem.at[2, m]))
    for copy in copies:
        copy.start()
    for copy in copies:
        copy.wait()

    @pl.when(parity() == 0)
    def _():
        cross[SENT - 1] = straight(cross, far)
        chip[SENT - 1] = jnp.zeros((NY, NZ), jnp.float32)

    @pl.when(parity() == 1)
    def _():
        cross[SENT - 1] = jnp.zeros((NY, NZ), jnp.float32)
        chip[SENT - 1] = straight(chip, far)


def params(room=ROOM):
    return pltpu.CompilerParams(vmem_limit_bytes=room)


def rows_shape(*lead):
    return jax.ShapeDtypeStruct((*lead, 8, 8, 128), jnp.float32)


def far(x):
    return pltpu.with_memory_space_constraint(x, pltpu.HBM)


def send(den, kap, interpret=False):
    rows = jax.ShapeDtypeStruct((SENT, NY, NZ), jnp.float32)
    return pl.pallas_call(
        send_kernel,
        out_shape=(rows, rows),
        in_specs=[FAR] * 2,
        out_specs=(VMEM, VMEM),
        scratch_shapes=[pltpu.VMEM((2, NY, NZ), jnp.float32), pltpu.SemaphoreType.DMA((3, 2))],
        compiler_params=params(8 * 1024 * 1024),
        interpret=interpret,
        name="send",
    )(far(den), far(kap))


def inner(levels, den, kap, interpret=False):
    rows = rows_shape(ROWS)
    hy3, hz, _, _ = constants()
    return pl.pallas_call(
        inner_kernel,
        out_shape=(
            rows,
            rows_shape(5, ROWS),
            jax.ShapeDtypeStruct((ROWS, 8, 128), jnp.float32),
            rows_shape(4),
            rows_shape(ITERS),
            rows_shape(2),
            jax.ShapeDtypeStruct((len(BLOCKS) + 1, 8, 128), jnp.float32),
            jax.ShapeDtypeStruct(hy3.shape, jnp.bfloat16),
            jax.ShapeDtypeStruct(hz.shape, jnp.bfloat16),
        ),
        in_specs=[FAR] * 5,
        out_specs=(VMEM,) * 9,
        scratch_shapes=[pltpu.VMEM((ROWS, NY, NZ), jnp.float32)] * 2
        + [
            pltpu.SMEM((1, 3), jnp.int32),
            pltpu.SemaphoreType.DMA((2, ROWS // CHUNK)),
            pltpu.SemaphoreType.DMA((3,)),
        ],
        compiler_params=params(),
        cost_estimate=pl.CostEstimate(flops=20_000_000, bytes_accessed=8_000_000, transcendentals=0),
        interpret=interpret,
        name="inner",
    )(far(levels), far(den), far(kap), far(jnp.asarray(hy3, jnp.bfloat16)), far(jnp.asarray(hz, jnp.bfloat16)))


def work():
    return [
        pltpu.VMEM((TALL, 8, 8, 128), jnp.float32),
        pltpu.VMEM((5, TALL, 8, 8, 128), jnp.float32),
        pltpu.VMEM((TALL, 8, 128), jnp.float32),
    ]


def chip_end(state, halo, interpret=False):
    return pl.pallas_call(
        chip_kernel,
        out_shape=rows_shape(2),
        in_specs=[VMEM] * 7,
        out_specs=VMEM,
        scratch_shapes=work(),
        compiler_params=params(),
        cost_estimate=pl.CostEstimate(flops=10_000_000, bytes_accessed=4_000_000, transcendentals=0),
        interpret=interpret,
        name="chip_end",
    )(*state[:6], halo)


def cross_end(members, coefs, state, near, halo, interpret=False):
    return pl.pallas_call(
        cross_kernel,
        out_shape=(
            jax.ShapeDtypeStruct((members, 8, 128), jnp.float32),
            jax.ShapeDtypeStruct((TILES - 1, 8, 128), jnp.float32),
        ),
        in_specs=[VMEM] * 12,
        out_specs=(VMEM, VMEM),
        scratch_shapes=work() + [pltpu.VMEM((NODES, 8, 8, 128), jnp.float32)] * 2,
        compiler_params=params(),
        interpret=interpret,
        name="cross_end",
    )(*state, near, halo, coefs.reshape(1, 1))


def spread(marks, mine, other, interpret=False):
    _, _, dy3, dz = constants()
    return pl.pallas_call(
        spread_kernel,
        out_shape=jax.ShapeDtypeStruct((ROWS, NY, NZ), jnp.float32),
        in_specs=[VMEM] * 5,
        out_specs=FAR,
        scratch_shapes=[pltpu.VMEM((ROWS, NY, NZ), jnp.float32), pltpu.SemaphoreType.DMA((NODES - 1,))],
        compiler_params=params(),
        interpret=interpret,
        name="spread",
    )(marks, mine, other, jnp.asarray(dy3, jnp.bfloat16), jnp.asarray(dz, jnp.bfloat16))


def local(density, kappa, levels, coefs):
    den, kap = density[0], kappa[0]
    space, grid = lax.axis_size("space"), lax.axis_size("grid")
    assert den.shape == (ROWS, NY, NZ) and space * ROWS == 512
    pair = [(i, i ^ 1) for i in range(space)]
    other_chip = [(i, (i + 1 if i % 2 else i - 1) % space) for i in range(space)]
    to_cross, to_chip = send(den, kap)
    cross = lax.ppermute(to_cross, "space", other_chip)
    chip = lax.ppermute(to_chip, "space", pair)
    state = inner(levels, den, kap)
    near = chip_end(state, chip)
    sent, stay = cross_end(grid, coefs, state, near, cross)
    got = lax.all_to_all(sent, "grid", split_axis=0, concat_axis=0, tiled=True)
    mine = jnp.concatenate([jnp.sum(got, axis=0, keepdims=True), stay], axis=0)
    other = lax.ppermute(mine, "space", pair)
    return spread(state[6], mine, other)[None]


def solution(mesh):
    in_specs = (
        P("grid", "space", None, None),
        P("grid", "space", None, None),
        P("grid", None),
        P("grid"),
    )
    out_specs = P("grid", "space", None, None)
    return jax.shard_map(local, mesh=mesh, in_specs=in_specs, out_specs=out_specs, check_vma=False)
```
